32 devices in a mesh: frow: 16 (over z, y, core), fcol: 2 (over x).
Axes of the slice: x: 2, y: 2, z: 4, core: 2. Of those that a mesh axis runs over, the one named last changes fastest.
Arguments:
- face_input: bfloat16 [12, 64, 64, 256], P(None, 'frow', 'fcol'), may hold values from -6 to 6
- kernel: bfloat16 [3, 3, 256, 256], replicated, may hold values from -0.125 to 0.125
- convolution_bias: float32 [256], replicated, may hold values from -3 to 3
- upstream: bfloat16 [12, 64, 64, 256], P(None, 'frow', 'fcol'), may hold values from -6 to 6
- adjacency: int32 [12, 4, 3], replicated, may hold values from 0 to 11, as said below
Outputs:
- activation: bfloat16 [12, 64, 64, 256], P(None, 'frow', 'fcol')
- input_gradient: bfloat16 [12, 64, 64, 256], P(None, 'frow', 'fcol')
- kernel_grad: float32 [3, 3, 256, 256], replicated
- bias_grad: float32 [256], replicated
The draws below stay inside these ranges and needn't reach their ends.
Inputs may be any that keep to these rules, and one draw needn't show every extreme that they name: adjacency[f, s] = (g, t, r): side s of face f (0 top, 1 bottom, 2 left, 3 right) borders side t of face g; t is 0 or 1 exactly when s is; r = 1 when positions along the seam run in opposite directions, else 0; the relation is symmetric, adjacency[g, t] = (f, s, r), and no side borders itself.
All inputs are finite; a program needn't handle non-finite values.
Results may differ from the reference program's by a relative error of at most 0.018.
Values may be sent and summed in bfloat16 or wider, within the bound.
No kernel may reach another device: no remote copies, remote signals or barrier semaphores. Data moves between devices by JAX's collectives and lax.ppermute only.
A program may use at most 128 MiB of HBM per device.

```python
import math
import jax
import jax.numpy as jnp
from jax import lax

FACE_TOTAL = 12
CHANNEL_COUNT = 256
DILATION_STEP = 2
EDGE_PIXELS = 64


def draw_adjacency(key, part):
    adjacency_table = jnp.zeros((FACE_TOTAL, 4, 3), jnp.int32)
    for side_group in range(2):
        order_key = jax.random.fold_in(key, 2 * side_group + 1)
        flip_key = jax.random.fold_in(key, 2 * side_group + 2)
        side_order = jax.random.permutation(order_key, 2 * FACE_TOTAL).astype(jnp.int32)
        first_items = side_order[0::2]
        second_items = side_order[1::2]
        flip_bits = jax.random.randint(flip_key, (FACE_TOTAL,), 0, 2).astype(jnp.int32)
        first_face = first_items // 2
        first_side = 2 * side_group + first_items % 2
        second_face = second_items // 2
        second_side = 2 * side_group + second_items % 2
        adjacency_table = adjacency_table.at[first_face, first_side].set(jnp.stack([second_face, second_side, flip_bits], 1))
        adjacency_table = adjacency_table.at[second_face, second_side].set(jnp.stack([first_face, first_side, flip_bits], 1))
    return adjacency_table


def block_levels(key, shape, shards, smallest, largest):
    def one(dim, shards_of):
        heights = jax.random.uniform(jax.random.fold_in(jax.random.fold_in(key, 6), dim), (shards_of,), jnp.float32, smallest / len(shards), largest / len(shards))
        return jnp.repeat(jnp.exp(heights), shape[dim] // shards_of).reshape((-1,) + (1,) * (len(shape) - dim - 1))

    loudness = one(*shards[0])
    for cut in shards[1:]:
        loudness = loudness * one(*cut)
    return loudness


def gaussian(own_key, dims, width, most, cuts=(), dtype=jnp.bfloat16):
    array = jax.random.normal(own_key, dims, jnp.float32) * width
    if len(cuts) > 0:
        array = block_levels(own_key, dims, cuts, -0.22, 0.18) * array
    return jnp.clip(array, min=-most, max=most).astype(dtype)


def setup_inputs(seed: int = 0) -> dict:
    splits = jax.random.split(jax.random.key(seed), 6)
    return {
        "face_input": gaussian(splits[0], (FACE_TOTAL, EDGE_PIXELS, EDGE_PIXELS, CHANNEL_COUNT), 1.0, 6.0, ((1, 16), (2, 2))),
        "kernel": gaussian(splits[1], (3, 3, CHANNEL_COUNT, CHANNEL_COUNT), (9 * CHANNEL_COUNT) ** -0.5, 0.125),
        "convolution_bias": gaussian(splits[2], (CHANNEL_COUNT,), 0.5, 3.0, (), jnp.float32),
        "upstream": gaussian(splits[3], (FACE_TOTAL, EDGE_PIXELS, EDGE_PIXELS, CHANNEL_COUNT), 1.0, 6.0, ((1, 16), (2, 2))),
        "adjacency": draw_adjacency(jax.random.fold_in(splits[5], 71), 0),
    }


half_root = 0.7071067811865476
density_scale = 0.3989422804014327

def gelu_value(value):
    return 0.5 * value * (1.0 + jax.scipy.special.erf(value * half_root))

def gelu_slope(value):
    return 0.5 * (1.0 + jax.scipy.special.erf(value * half_root)) + value * jnp.exp(-0.5 * value * value) * density_scale

def side_strips(face_input):
    upper_rows = face_input[:, :DILATION_STEP]
    lower_rows = jnp.flip(face_input[:, EDGE_PIXELS - DILATION_STEP:], 1)
    left_columns = jnp.transpose(face_input[:, :, :DILATION_STEP], (0, 2, 1, 3))
    right_columns = jnp.transpose(jnp.flip(face_input[:, :, EDGE_PIXELS - DILATION_STEP:], 2), (0, 2, 1, 3))
    return jnp.stack([upper_rows, lower_rows, left_columns, right_columns], 1)

def reference(face_input, kernel, convolution_bias, upstream, adjacency):
    adjacent_face = adjacency[:, :, 0]
    adjacent_edge = adjacency[:, :, 1]
    reversed_seam = adjacency[:, :, 2] == 1
    strips = side_strips(face_input)
    halo_border = strips[adjacent_face, adjacent_edge]
    halo_border = jnp.where(reversed_seam[:, :, None, None, None], jnp.flip(halo_border, 3), halo_border)
    edge_length = EDGE_PIXELS + 2 * DILATION_STEP
    padded_input = jnp.zeros((FACE_TOTAL, edge_length, edge_length, CHANNEL_COUNT), jnp.bfloat16)
    padded_input = padded_input.at[:, DILATION_STEP:EDGE_PIXELS + DILATION_STEP, DILATION_STEP:EDGE_PIXELS + DILATION_STEP].set(face_input)
    padded_input = padded_input.at[:, :DILATION_STEP, DILATION_STEP:EDGE_PIXELS + DILATION_STEP].set(jnp.flip(halo_border[:, 0], 1))
    padded_input = padded_input.at[:, EDGE_PIXELS + DILATION_STEP:, DILATION_STEP:EDGE_PIXELS + DILATION_STEP].set(halo_border[:, 1])
    padded_input = padded_input.at[:, DILATION_STEP:EDGE_PIXELS + DILATION_STEP, :DILATION_STEP].set(jnp.transpose(jnp.flip(halo_border[:, 2], 1), (0, 2, 1, 3)))
    padded_input = padded_input.at[:, DILATION_STEP:EDGE_PIXELS + DILATION_STEP, EDGE_PIXELS + DILATION_STEP:].set(jnp.transpose(halo_border[:, 3], (0, 2, 1, 3)))
    random_values = ('NHWC', 'HWIO', 'NHWC')
    rotated_strip = jnp.transpose(jnp.flip(kernel, (0, 1)), (0, 1, 3, 2))

    def per_face(carry, inputs):
        face_with_halo, face_upstream = inputs
        preactivation = lax.conv_general_dilated(face_with_halo[None], kernel, (1, 1), 'VALID', rhs_dilation=(DILATION_STEP, DILATION_STEP), dimension_numbers=random_values, preferred_element_type=jnp.float32) + convolution_bias
        face_out = gelu_value(preactivation).astype(jnp.bfloat16)
        preactivation_gradient = (face_upstream[None].astype(jnp.float32) * gelu_slope(preactivation)).astype(jnp.bfloat16)
        tap_list = []
        for kernel_row_offset in range(3):
            for kernel_column_offset in range(3):
                input_window = face_with_halo[None, kernel_row_offset * DILATION_STEP:kernel_row_offset * DILATION_STEP + EDGE_PIXELS, kernel_column_offset * DILATION_STEP:kernel_column_offset * DILATION_STEP + EDGE_PIXELS]
                tap_list.append(lax.dot_general(input_window, preactivation_gradient, (((0, 1, 2), (0, 1, 2)), ((), ())), preferred_element_type=jnp.float32))
        kernel_part = jnp.stack(tap_list, 0).reshape(3, 3, CHANNEL_COUNT, CHANNEL_COUNT)
        bias_part = lax.optimization_barrier(jnp.sum(preactivation_gradient.astype(jnp.float32), axis=(0, 1, 2)))
        face_gradient = lax.conv_general_dilated(preactivation_gradient, rotated_strip, (1, 1), ((2 * DILATION_STEP, 2 * DILATION_STEP), (2 * DILATION_STEP, 2 * DILATION_STEP)), rhs_dilation=(DILATION_STEP, DILATION_STEP), dimension_numbers=random_values, preferred_element_type=jnp.float32).astype(jnp.bfloat16)
        return ((carry[0] + kernel_part, carry[1] + bias_part), (face_out[0], face_gradient[0]))
    start = (jnp.zeros((3, 3, CHANNEL_COUNT, CHANNEL_COUNT), jnp.float32), jnp.zeros((CHANNEL_COUNT,), jnp.float32))
    totals, stacked = lax.scan(per_face, start, (padded_input, upstream))
    activation, padded_gradient = stacked
    scale = 1.0 / math.sqrt(FACE_TOTAL * EDGE_PIXELS * EDGE_PIXELS)
    kernel_grad = totals[0] * scale
    bias_grad = totals[1] * scale
    upper_edge_gradient = jnp.flip(padded_gradient[:, :DILATION_STEP, DILATION_STEP:EDGE_PIXELS + DILATION_STEP], 1)
    lower_edge_gradient = padded_gradient[:, EDGE_PIXELS + DILATION_STEP:, DILATION_STEP:EDGE_PIXELS + DILATION_STEP]
    left_edge_gradient = jnp.flip(jnp.transpose(padded_gradient[:, DILATION_STEP:EDGE_PIXELS + DILATION_STEP, :DILATION_STEP], (0, 2, 1, 3)), 1)
    right_edge_gradient = jnp.transpose(padded_gradient[:, DILATION_STEP:EDGE_PIXELS + DILATION_STEP, EDGE_PIXELS + DILATION_STEP:], (0, 2, 1, 3))
    halo_gradient = jnp.stack([upper_edge_gradient, lower_edge_gradient, left_edge_gradient, right_edge_gradient], 1).astype(jnp.float32)
    halo_gradient = jnp.where(reversed_seam[:, :, None, None, None], jnp.flip(halo_gradient, 3), halo_gradient)
    edge_gradient = jnp.zeros((FACE_TOTAL, 4, DILATION_STEP, EDGE_PIXELS, CHANNEL_COUNT), jnp.float32).at[adjacent_face, adjacent_edge].add(halo_gradient)
    input_gradient = padded_gradient[:, DILATION_STEP:EDGE_PIXELS + DILATION_STEP, DILATION_STEP:EDGE_PIXELS + DILATION_STEP].astype(jnp.float32)
    input_gradient = input_gradient.at[:, :DILATION_STEP].add(edge_gradient[:, 0])
    input_gradient = input_gradient.at[:, EDGE_PIXELS - DILATION_STEP:].add(jnp.flip(edge_gradient[:, 1], 1))
    input_gradient = input_gradient.at[:, :, :DILATION_STEP].add(jnp.transpose(edge_gradient[:, 2], (0, 2, 1, 3)))
    input_gradient = input_gradient.at[:, :, EDGE_PIXELS - DILATION_STEP:].add(jnp.flip(jnp.transpose(edge_gradient[:, 3], (0, 2, 1, 3)), 2))
    return (activation, input_gradient.astype(jnp.bfloat16), kernel_grad, bias_grad)
```

```python
import math

import jax
import jax.numpy as jnp
from jax import lax
from jax.sharding import PartitionSpec as P

DILATION_STEP = 2


half_root = 0.7071067811865476
density_scale = 0.3989422804014327


def with_halo(block, sides, width):
    for axis, dim in sides:
        count = lax.axis_size(axis)
        forward = [(i, i + 1) for i in range(count - 1)]
        forward.append((count - 1, 0))
        backward = [(target, source) for source, target in forward]
        low = lax.ppermute(
            lax.slice_in_dim(block, block.shape[dim] - width, None, axis=dim), axis, forward
        )
        high = lax.ppermute(lax.slice_in_dim(block, 0, width, axis=dim), axis, backward)
        block = jnp.concatenate([low, block, high], axis=dim)
    return block


def gelu_value(value):
    return 0.5 * value * (1.0 + jax.scipy.special.erf(value * half_root))


def gelu_slope(value):
    return (
        0.5 * (1.0 + jax.scipy.special.erf(value * half_root))
        + value * jnp.exp(-0.5 * value * value) * density_scale
    )


def pick_table(entries, side_near, face_count):
    same_side = (entries[:, 1] == side_near).astype(jnp.int32)
    slot_index = (2 * entries[:, 2] + same_side) * face_count + entries[:, 0]
    return (slot_index[:, None] == jnp.arange(4 * face_count, dtype=jnp.int32)[None, :]).astype(
        jnp.bfloat16
    )


def mirror_pairs(rows, cols, edge_rows, flip_rows, flip_cols):
    pairs = []
    for r in range(rows):
        for c in range(cols):
            on_edge = r in (0, rows - 1) if edge_rows else c in (0, cols - 1)
            if on_edge:
                target_row = rows - 1 - r if flip_rows else r
                target_col = cols - 1 - c if flip_cols else c
                pairs.append((r * cols + c, target_row * cols + target_col))
    return pairs


def reflect(row_band, col_band):
    rows, cols = lax.axis_size("frow"), lax.axis_size("fcol")
    axes = ("frow", "fcol")
    row_band = lax.ppermute(row_band, axes, mirror_pairs(rows, cols, True, False, True))
    col_band = lax.ppermute(col_band, axes, mirror_pairs(rows, cols, False, True, False))
    return (row_band, col_band)


def reduce_stages():
    col_bits = lax.axis_size("fcol").bit_length() - 1
    all_bits = (lax.axis_size("frow") * lax.axis_size("fcol")).bit_length() - 1
    rest = [1 << bit for bit in range(all_bits) if bit != col_bits]
    stages = [(1 << col_bits,)]
    while rest:
        stages.append(tuple(rest[:2]))
        rest = rest[2:]
    return stages


def stage_offsets(stage):
    return (0, stage[0]) if len(stage) == 1 else (0, stage[0], stage[1], stage[0] ^ stage[1])


def stage_place(index, stage):
    place = (index // stage[0]) % 2
    if len(stage) == 2:
        place = place + 2 * ((index // stage[1]) % 2)
    return place


def fold_sum(terms):
    while len(terms) > 1:
        terms = [terms[i] + terms[i + 1] for i in range(0, len(terms), 2)]
    return terms[0]


def reduce_everywhere(matrix, vector):
    axes = ("frow", "fcol")
    count = lax.axis_size("frow") * lax.axis_size("fcol")
    index = lax.axis_index("frow") * lax.axis_size("fcol") + lax.axis_index("fcol")
    width = matrix.shape[-1]
    pad = jnp.zeros((7, width), jnp.float32)
    vector = jnp.concatenate([vector[None], pad], 0)
    part = matrix.reshape(-1, width)
    stages = reduce_stages()
    for stage in stages:
        offsets = stage_offsets(stage)
        place = stage_place(index, stage)
        part = part.reshape(len(offsets), -1, width).astype(jnp.bfloat16)
        vector = lax.optimization_barrier(vector.astype(jnp.bfloat16))
        rows = part.shape[1]
        sums, vectors = [], []
        for order, offset in enumerate(offsets):
            piece = lax.dynamic_index_in_dim(part, place ^ order, 0, False)
            if offset:
                packed = jnp.concatenate([piece, vector], 0)
                packed = lax.ppermute(packed, axes, [(i, i ^ offset) for i in range(count)])
                sums.append(packed[:rows].astype(jnp.float32))
                vectors.append(packed[rows:].astype(jnp.float32))
            else:
                sums.append(piece.astype(jnp.float32))
                vectors.append(vector.astype(jnp.float32))
        part = fold_sum(sums)
        vector = fold_sum(vectors)
    part = lax.optimization_barrier(part.astype(jnp.bfloat16))[None]
    for stage in stages[::-1]:
        offsets = stage_offsets(stage)
        place = stage_place(index, stage)
        pieces = [part] + [
            lax.ppermute(part, axes, [(i, i ^ offset) for i in range(count)])
            for offset in offsets[1:]
        ]
        stacked = jnp.stack(pieces, 0)
        part = jnp.concatenate(
            [
                lax.dynamic_index_in_dim(stacked, place ^ order, 0, False)
                for order in range(len(offsets))
            ],
            0,
        )
    return (part.reshape(matrix.shape).astype(jnp.float32), vector[0])


def fold_border(extended, along, cells, inner_size):
    middle = lax.slice_in_dim(extended, 2 * cells, 2 * cells + inner_size, axis=along)
    before = lax.slice_in_dim(extended, 0, cells, axis=along)
    after_rim = lax.slice_in_dim(
        extended, inner_size + 3 * cells, inner_size + 4 * cells, axis=along
    )
    lead_pads = [(0, 0)] * extended.ndim
    tail_pads = [(0, 0)] * extended.ndim
    lead_pads[along] = (0, inner_size - cells)
    tail_pads[along] = (inner_size - cells, 0)
    return middle + jnp.pad(before, lead_pads) + jnp.pad(after_rim, tail_pads)


def local(face_input, kernel, convolution_bias, upstream, adjacency):
    face_count = face_input.shape[0]
    tile_rows = face_input.shape[1]
    tile_cols = face_input.shape[2]
    dilation_step = DILATION_STEP
    height = tile_rows + 2 * dilation_step
    breadth = tile_cols + 2 * dilation_step
    at_top = lax.axis_index("frow") == 0
    at_bottom = lax.axis_index("frow") == lax.axis_size("frow") - 1
    at_left = lax.axis_index("fcol") == 0
    at_right = lax.axis_index("fcol") == lax.axis_size("fcol") - 1
    column_index = jnp.arange(breadth)
    keep_cols = jnp.logical_not(
        at_left & (column_index < dilation_step)
        | at_right & (column_index >= tile_cols + dilation_step)
    )
    row_index = jnp.arange(height)
    keep_rows = jnp.logical_not(
        at_top & (row_index < dilation_step) | at_bottom & (row_index >= tile_rows + dilation_step)
    )
    padded_input = with_halo(face_input, (("frow", 1), ("fcol", 2)), dilation_step)
    row_wrap = jnp.where(
        at_top, padded_input[:, :dilation_step], padded_input[:, tile_rows + dilation_step :]
    )
    row_own = jnp.where(
        at_top,
        padded_input[:, dilation_step : 2 * dilation_step],
        padded_input[:, tile_rows : tile_rows + dilation_step],
    )
    col_wrap = jnp.where(
        at_left, padded_input[:, :, :dilation_step], padded_input[:, :, tile_cols + dilation_step :]
    )
    col_own = jnp.where(
        at_left,
        padded_input[:, :, dilation_step : 2 * dilation_step],
        padded_input[:, :, tile_cols : tile_cols + dilation_step],
    )
    row_send = jnp.concatenate([row_wrap, row_own], 1)
    col_send = jnp.concatenate([col_wrap, col_own], 2)
    far_rows, far_cols = reflect(row_send, col_send)
    row_pick = pick_table(
        jnp.where(at_top, adjacency[:, 0], adjacency[:, 1]), jnp.where(at_top, 0, 1), face_count
    )
    col_pick = pick_table(
        jnp.where(at_left, adjacency[:, 2], adjacency[:, 3]), jnp.where(at_left, 2, 3), face_count
    )
    row_cands = jnp.concatenate(
        [
            row_wrap,
            jnp.flip(row_own, 1),
            jnp.flip(far_rows[:, :dilation_step], 2),
            jnp.flip(far_rows[:, dilation_step:], (1, 2)),
        ],
        0,
    )
    row_halo = jnp.einsum("fk,kdwc->fdwc", row_pick, row_cands, preferred_element_type=jnp.float32)
    row_halo = jnp.where(keep_cols[None, None, :, None], row_halo, 0.0).astype(jnp.bfloat16)
    top_rim = jnp.where(at_top, row_halo, padded_input[:, :dilation_step])
    bottom_rim = jnp.where(at_bottom, row_halo, padded_input[:, tile_rows + dilation_step :])
    padded_input = jnp.concatenate(
        [top_rim, padded_input[:, dilation_step : tile_rows + dilation_step], bottom_rim], 1
    )
    col_cands = jnp.concatenate(
        [
            col_wrap,
            jnp.flip(col_own, 2),
            jnp.flip(far_cols[:, :, :dilation_step], 1),
            jnp.flip(far_cols[:, :, dilation_step:], (1, 2)),
        ],
        0,
    )
    col_halo = jnp.einsum("fk,kadc->fadc", col_pick, col_cands, preferred_element_type=jnp.float32)
    col_halo = jnp.where(keep_rows[None, :, None, None], col_halo, 0.0).astype(jnp.bfloat16)
    left_rim = jnp.where(at_left, col_halo, padded_input[:, :, :dilation_step])
    right_rim = jnp.where(at_right, col_halo, padded_input[:, :, tile_cols + dilation_step :])
    padded_input = jnp.concatenate(
        [left_rim, padded_input[:, :, dilation_step : tile_cols + dilation_step], right_rim], 2
    )
    random_values = ("NHWC", "HWIO", "NHWC")
    preactivation = (
        lax.conv_general_dilated(
            padded_input,
            kernel,
            (1, 1),
            "VALID",
            rhs_dilation=(dilation_step, dilation_step),
            dimension_numbers=random_values,
            preferred_element_type=jnp.float32,
        )
        + convolution_bias
    )
    activation = gelu_value(preactivation).astype(jnp.bfloat16)
    preactivation_gradient = (upstream.astype(jnp.float32) * gelu_slope(preactivation)).astype(
        jnp.bfloat16
    )
    tap_list = []
    for kernel_row_offset in range(3):
        for kernel_column_offset in range(3):
            input_window = padded_input[
                :,
                kernel_row_offset * dilation_step : kernel_row_offset * dilation_step + tile_rows,
                kernel_column_offset * dilation_step : kernel_column_offset * dilation_step
                + tile_cols,
            ]
            tap_list.append(
                lax.dot_general(
                    input_window,
                    preactivation_gradient,
                    (((0, 1, 2), (0, 1, 2)), ((), ())),
                    preferred_element_type=jnp.float32,
                )
            )
    kernel_local = jnp.stack(tap_list, 0).reshape(kernel.shape)
    bias_local = jnp.sum(preactivation_gradient.astype(jnp.float32), axis=(0, 1, 2))
    kernel_total, bias_total = reduce_everywhere(kernel_local, bias_local)
    scale = 1.0 / math.sqrt(
        face_count * tile_rows * lax.axis_size("frow") * tile_cols * lax.axis_size("fcol")
    )
    kernel_grad = kernel_total * scale
    bias_grad = bias_total * scale
    rotated_strip = jnp.transpose(jnp.flip(kernel, (0, 1)), (0, 1, 3, 2))
    twice = 2 * dilation_step
    padded_gradient = lax.conv_general_dilated(
        preactivation_gradient,
        rotated_strip,
        (1, 1),
        ((twice, twice), (twice, twice)),
        rhs_dilation=(dilation_step, dilation_step),
        dimension_numbers=random_values,
        preferred_element_type=jnp.float32,
    ).astype(jnp.bfloat16)
    row_seam = jnp.where(
        at_top, padded_gradient[:, :dilation_step], padded_gradient[:, tile_rows + dilation_step :]
    )
    row_seam = jnp.where(keep_cols[None, None, :, None], row_seam, jnp.zeros_like(row_seam))
    row_split = jnp.einsum("fk,fdwc->kdwc", row_pick, row_seam, preferred_element_type=jnp.float32)
    row_split = row_split.reshape((4, face_count) + row_split.shape[1:])
    col_seam = jnp.where(
        at_left,
        padded_gradient[:, :, :dilation_step],
        padded_gradient[:, :, tile_cols + dilation_step :],
    )
    col_seam = jnp.where(keep_rows[None, :, None, None], col_seam, jnp.zeros_like(col_seam))
    col_split = jnp.einsum("fk,fadc->kadc", col_pick, col_seam, preferred_element_type=jnp.float32)
    col_split = col_split.reshape((4, face_count) + col_split.shape[1:])
    row_far_grad = jnp.concatenate(
        [jnp.flip(row_split[2], 2), jnp.flip(row_split[3], (1, 2))], 1
    ).astype(jnp.bfloat16)
    col_far_grad = jnp.concatenate(
        [jnp.flip(col_split[2], 1), jnp.flip(col_split[3], (1, 2))], 2
    ).astype(jnp.bfloat16)
    row_back, col_back = reflect(row_far_grad, col_far_grad)
    wrap_rows = row_split[0] + row_back[:, :dilation_step].astype(jnp.float32)
    own_rows = jnp.flip(row_split[1], 1) + row_back[:, dilation_step:].astype(jnp.float32)
    wrap_cols = col_split[0] + col_back[:, :, :dilation_step].astype(jnp.float32)
    own_cols = jnp.flip(col_split[1], 2) + col_back[:, :, dilation_step:].astype(jnp.float32)
    gathered = padded_gradient.astype(jnp.float32)
    middle_rows = gathered[:, dilation_step : tile_rows + dilation_step]
    middle_rows = middle_rows + jnp.pad(
        jnp.where(at_top, own_rows, 0.0), ((0, 0), (0, tile_rows - dilation_step), (0, 0), (0, 0))
    )
    middle_rows = middle_rows + jnp.pad(
        jnp.where(at_bottom, own_rows, 0.0),
        ((0, 0), (tile_rows - dilation_step, 0), (0, 0), (0, 0)),
    )
    top_grad = jnp.where(at_top, wrap_rows, gathered[:, :dilation_step])
    bottom_grad = jnp.where(at_bottom, wrap_rows, gathered[:, tile_rows + dilation_step :])
    gathered = jnp.concatenate([top_grad, middle_rows, bottom_grad], 1)
    middle_cols = gathered[:, :, dilation_step : tile_cols + dilation_step]
    middle_cols = middle_cols + jnp.pad(
        jnp.where(at_left, own_cols, 0.0), ((0, 0), (0, 0), (0, tile_cols - dilation_step), (0, 0))
    )
    middle_cols = middle_cols + jnp.pad(
        jnp.where(at_right, own_cols, 0.0), ((0, 0), (0, 0), (tile_cols - dilation_step, 0), (0, 0))
    )
    left_grad = jnp.where(at_left, wrap_cols, gathered[:, :, :dilation_step])
    right_grad = jnp.where(at_right, wrap_cols, gathered[:, :, tile_cols + dilation_step :])
    gathered = jnp.concatenate([left_grad, middle_cols, right_grad], 2)
    returned = with_halo(
        gathered.astype(jnp.bfloat16), (("frow", 1), ("fcol", 2)), dilation_step
    ).astype(gathered.dtype)
    folded = fold_border(returned, 1, dilation_step, tile_rows)
    folded = fold_border(folded, 2, dilation_step, tile_cols)
    input_gradient = folded.astype(jnp.bfloat16)
    return (activation, input_gradient, kernel_grad, bias_grad)


def solution(mesh):
    return jax.shard_map(
        local,
        mesh=mesh,
        in_specs=(P(None, "frow", "fcol", None), P(), P(), P(None, "frow", "fcol", None), P()),
        out_specs=(P(None, "frow", "fcol", None), P(None, "frow", "fcol", None), P(), P()),
        check_vma=False,
    )
```

```python
import functools
import math

import jax
import jax.numpy as jnp
import numpy as np
from jax import lax
from jax.experimental import pallas as pl
from jax.experimental.pallas import tpu as pltpu
from jax.sharding import PartitionSpec as P

DILATION_STEP = 2


half_root = 0.7071067811865476
density_scale = 0.3989422804014327
axes = ("frow", "fcol")
vmem_bytes = 48 * 1024 * 1024


def shifted_pairs(row_step, col_step):
    rows, cols = lax.axis_size("frow"), lax.axis_size("fcol")
    return [
        (r * cols + c, (r + row_step) % rows * cols + (c + col_step) % cols)
        for r in range(rows)
        for c in range(cols)
    ]


def mirror_pairs(edge_rows, flip_rows, flip_cols):
    rows, cols = lax.axis_size("frow"), lax.axis_size("fcol")
    pairs = []
    for r in range(rows):
        for c in range(cols):
            on_edge = r in (0, rows - 1) if edge_rows else c in (0, cols - 1)
            if on_edge:
                target_row = rows - 1 - r if flip_rows else r
                target_col = cols - 1 - c if flip_cols else c
                pairs.append((r * cols + c, target_row * cols + target_col))
    return pairs


def round_up(value, step):
    return -(-value // step) * step


def col_flips(tile_rows):
    size = 2 * tile_rows
    table = np.zeros((4, size, size), np.float32)
    for kind in range(4):
        for y in range(tile_rows):
            for k in range(2):
                source_y = tile_rows - 1 - y if kind >= 2 else y
                source_k = 1 - k if kind % 2 else k
                table[kind, 2 * y + k, 2 * source_y + source_k] = 1
    return jnp.asarray(table, jnp.bfloat16)


def row_flips(width):
    size = 2 * width + 8
    table = np.zeros((4, size, size), np.float32)
    for kind in range(4):
        for d in range(2):
            source_d = 1 - d if kind % 2 else d
            for p in range(width):
                source_p = width - 1 - p if kind >= 2 else p
                table[kind, d * width + p, source_d * width + source_p] = 1
            for e in range(4):
                source_e = 3 - e if kind >= 2 else e
                table[kind, 2 * width + 4 * d + e, 2 * width + 4 * source_d + source_e] = 1
    return jnp.asarray(table, jnp.bfloat16)


def tail_picks(tile_rows):
    table = np.zeros((2, 8, 4 * tile_rows), np.float32)
    for place, first in enumerate((0, tile_rows - 2)):
        for d in range(2):
            for e in range(4):
                source = 2 * tile_rows * (e // 2) + 2 * (first + d) + e % 2
                table[place, 4 * d + e, source] = 1
    return jnp.asarray(table, jnp.bfloat16)


def stack_places(tile_rows, width):
    strip = round_up(2 * width + 8, 16)
    beside = tile_rows * width
    above = beside + 4 * tile_rows
    below = above + strip
    return (beside, above, below, round_up(below + strip, 128))


def stack_row(tile_rows, width, q, w):
    beside, above, below, _ = stack_places(tile_rows, width)
    side_cell = w if w < 2 else w - width
    inner = 2 <= w < width + 2
    if 2 <= q < tile_rows + 2:
        y = q - 2
        if inner:
            return y * width + w - 2
        return beside + 2 * tile_rows * (side_cell // 2) + 2 * y + side_cell % 2
    base, d = (above, q) if q < 2 else (below, q - tile_rows - 2)
    return base + (d * width + w - 2 if inner else 2 * width + 4 * d + side_cell)


def pad_picks(tile_rows, width):
    breadth = round_up(width + 4, 8)
    size = stack_places(tile_rows, width)[3]
    table = np.zeros(((tile_rows + 4) * breadth, size), np.float32)
    for q in range(tile_rows + 4):
        for w in range(width + 4):
            table[q * breadth + w, stack_row(tile_rows, width, q, w)] = 1
    return jnp.asarray(table, jnp.bfloat16)


def pick(table, value):
    return jnp.dot(table, value, preferred_element_type=jnp.float32).astype(jnp.bfloat16)


def seam_of(adjacency, face, side):
    base = (face * 4 + side) * 3
    near = (adjacency[base + 1] == side).astype(jnp.int32)
    return adjacency[base], 2 * adjacency[base + 2] + near


def col_kernel(
    adjacency, field, edges, beside, far_same, far_cross, flips, tails,
    side_out, top_out, bottom_out, edge_out, seam,
):
    face_count, tile_rows, width, channels = field.shape
    half = 2 * tile_rows
    row_place, col_place = lax.axis_index("frow"), lax.axis_index("fcol")
    at_top = row_place == 0
    at_bottom = row_place == lax.axis_size("frow") - 1
    at_left = col_place == 0
    at_right = col_place == lax.axis_size("fcol") - 1

    @pl.loop(0, face_count)
    def _(face):
        @pl.when(jnp.logical_or(at_left, at_right))
        def _():
            source, kind = seam_of(adjacency, face, jnp.where(at_left, 2, 3))

            @pl.when(kind == 0)
            def _():
                both = beside[source]
                seam[...] = jnp.where(at_left, both[half:], both[:half])

            @pl.when(kind == 1)
            def _():
                both = edges[source]
                seam[...] = pick(flips[1], jnp.where(at_left, both[:half], both[half:]))

            @pl.when(kind == 2)
            def _():
                seam[...] = pick(flips[2], far_cross[source])

            @pl.when(kind == 3)
            def _():
                seam[...] = pick(flips[3], far_same[source])

        both = beside[face]
        left = jnp.where(at_left, seam[...], both[half:])
        right = jnp.where(at_right, seam[...], both[:half])
        sides = jnp.concatenate([left, right], 0)
        side_out[face] = sides
        blank = jnp.zeros_like(left)
        inner = jnp.concatenate(
            [jnp.where(at_left, blank, left), jnp.where(at_right, blank, right)], 0
        )
        upper = pick(tails[0], jnp.where(at_top, inner, sides))
        lower = pick(tails[1], jnp.where(at_bottom, inner, sides))
        for d in range(2):
            rows = pl.ds(d * width, width)
            top_out[face, rows] = field[face, d]
            bottom_out[face, rows] = field[face, tile_rows - 2 + d]
            edge_out[face, rows] = jnp.where(
                at_top, field[face, d], field[face, tile_rows - 2 + d]
            )
        rows = pl.ds(2 * width, 8)
        top_out[face, rows] = upper
        bottom_out[face, rows] = lower
        edge_out[face, rows] = jnp.where(at_top, upper, lower)


def load_stack(adjacency, face, field, sides, up, down, edge, far_same, far_cross, flips, stack):
    tile_rows, width, channels = field.shape[1:]
    strip = 2 * width + 8
    beside, above, below, _ = stack_places(tile_rows, width)
    row_place = lax.axis_index("frow")
    stack[pl.ds(0, beside)] = field[face].reshape(beside, channels)
    stack[pl.ds(beside, 4 * tile_rows)] = sides[face]
    for side, place, near in ((0, above, up), (1, below, down)):
        at_edge = row_place == side * (lax.axis_size("frow") - 1)
        rows = pl.ds(place, strip)

        @pl.when(jnp.logical_not(at_edge))
        def _():
            stack[rows] = near[face]

        source, kind = seam_of(adjacency, face, side)
        for choice, strips in enumerate((near, edge, far_cross, far_same)):

            @pl.when(jnp.logical_and(at_edge, kind == choice))
            def _():
                stack[rows] = pick(flips[choice], strips[source])


def pad_kernel(
    adjacency, field, sides, up, down, edge, far_same, far_cross, flips, picks, padded, stack
):
    face_count, tile_rows, width, channels = field.shape
    breadth = picks.shape[0] // (tile_rows + 4)
    stack[...] = jnp.zeros_like(stack)

    @pl.loop(0, face_count)
    def _(face):
        load_stack(
            adjacency, face, field, sides, up, down, edge, far_same, far_cross, flips, stack
        )
        out = pick(picks[...], stack[...])
        for q in range(tile_rows + 4):
            padded[face, q] = out[q * breadth : q * breadth + width + 4]


def whole(count):
    return [pl.BlockSpec(memory_space=pltpu.SMEM)] + [
        pl.BlockSpec(memory_space=pltpu.VMEM) for _ in range(count)
    ]


def gather_strips(field, adjacency):
    face_count, tile_rows, width, channels = field.shape
    cols = lax.axis_size("fcol")
    left = field[:, :, :2].reshape(face_count, 2 * tile_rows, channels)
    right = field[:, :, width - 2 :].reshape(face_count, 2 * tile_rows, channels)
    edges = jnp.concatenate([left, right], 1)
    if cols == 2:
        beside = lax.ppermute(edges, axes, shifted_pairs(0, 1))
    else:
        beside = jnp.concatenate(
            [
                lax.ppermute(left, axes, shifted_pairs(0, -1)),
                lax.ppermute(right, axes, shifted_pairs(0, 1)),
            ],
            1,
        )
    edge = jnp.where(lax.axis_index("fcol") == 0, left, right)
    far_same = lax.ppermute(edge, axes, mirror_pairs(False, True, False))
    far_cross = lax.ppermute(edge, axes, mirror_pairs(False, True, True))
    strip = jax.ShapeDtypeStruct((face_count, 2 * width + 8, channels), field.dtype)
    sides, top, bottom, edge_strip = pl.pallas_call(
        col_kernel,
        out_shape=(jax.ShapeDtypeStruct(edges.shape, field.dtype), strip, strip, strip),
        in_specs=whole(7),
        out_specs=[pl.BlockSpec(memory_space=pltpu.VMEM)] * 4,
        scratch_shapes=[pltpu.VMEM((2 * tile_rows, channels), field.dtype)],
        compiler_params=pltpu.CompilerParams(vmem_limit_bytes=vmem_bytes),
        cost_estimate=pl.CostEstimate(flops=1000, bytes_accessed=3000000, transcendentals=0),
    )(
        adjacency, field, edges, beside, far_same, far_cross,
        col_flips(tile_rows), tail_picks(tile_rows),
    )
    up = lax.ppermute(bottom, axes, shifted_pairs(1, 0))
    down = lax.ppermute(top, axes, shifted_pairs(-1, 0))
    row_same = lax.ppermute(edge_strip, axes, mirror_pairs(True, False, True))
    row_cross = lax.ppermute(edge_strip, axes, mirror_pairs(True, True, True))
    return (field, sides, up, down, edge_strip, row_same, row_cross)


def pad_field(field, adjacency):
    face_count, tile_rows, width, channels = field.shape
    strips = gather_strips(field, adjacency)
    padded = (face_count, tile_rows + 4, width + 4, channels)
    size = stack_places(tile_rows, width)[3]
    return pl.pallas_call(
        pad_kernel,
        out_shape=jax.ShapeDtypeStruct(padded, field.dtype),
        in_specs=whole(9),
        out_specs=pl.BlockSpec(memory_space=pltpu.VMEM),
        scratch_shapes=[pltpu.VMEM((size, channels), field.dtype)],
        compiler_params=pltpu.CompilerParams(vmem_limit_bytes=vmem_bytes),
        cost_estimate=pl.CostEstimate(flops=1000, bytes_accessed=5000000, transcendentals=0),
    )(adjacency, *strips, row_flips(width), pad_picks(tile_rows, width))


def with_halo(block, sides, width):
    for axis, dim in sides:
        count = lax.axis_size(axis)
        forward = [(i, i + 1) for i in range(count - 1)]
        forward.append((count - 1, 0))
        backward = [(target, source) for source, target in forward]
        low = lax.ppermute(
            lax.slice_in_dim(block, block.shape[dim] - width, None, axis=dim), axis, forward
        )
        high = lax.ppermute(lax.slice_in_dim(block, 0, width, axis=dim), axis, backward)
        block = jnp.concatenate([low, block, high], axis=dim)
    return block


def gelu_value(value):
    return 0.5 * value * (1.0 + jax.scipy.special.erf(value * half_root))


def gelu_slope(value):
    return (
        0.5 * (1.0 + jax.scipy.special.erf(value * half_root))
        + value * jnp.exp(-0.5 * value * value) * density_scale
    )


def pick_table(entries, side_near, face_count):
    same_side = (entries[:, 1] == side_near).astype(jnp.int32)
    slot_index = (2 * entries[:, 2] + same_side) * face_count + entries[:, 0]
    return (slot_index[:, None] == jnp.arange(4 * face_count, dtype=jnp.int32)[None, :]).astype(
        jnp.bfloat16
    )


def reflect(row_band, col_band):
    row_band = lax.ppermute(row_band, axes, mirror_pairs(True, False, True))
    col_band = lax.ppermute(col_band, axes, mirror_pairs(False, True, False))
    return (row_band, col_band)


def reduce_stages():
    col_bits = lax.axis_size("fcol").bit_length() - 1
    all_bits = (lax.axis_size("frow") * lax.axis_size("fcol")).bit_length() - 1
    rest = [1 << bit for bit in range(all_bits) if bit != col_bits]
    stages = [(1 << col_bits,)]
    while rest:
        stages.append(tuple(rest[:2]))
        rest = rest[2:]
    return stages


def stage_offsets(stage):
    return (0, stage[0]) if len(stage) == 1 else (0, stage[0], stage[1], stage[0] ^ stage[1])


def stage_place(index, stage):
    place = (index // stage[0]) % 2
    if len(stage) == 2:
        place = place + 2 * ((index // stage[1]) % 2)
    return place


def fold_sum(terms):
    while len(terms) > 1:
        terms = [terms[i] + terms[i + 1] for i in range(0, len(terms), 2)]
    return terms[0]


def reduce_everywhere(matrix, vector):
    count = lax.axis_size("frow") * lax.axis_size("fcol")
    index = lax.axis_index("frow") * lax.axis_size("fcol") + lax.axis_index("fcol")
    width = matrix.shape[-1]
    pad = jnp.zeros((7, width), jnp.float32)
    vector = jnp.concatenate([vector[None], pad], 0)
    part = matrix.reshape(-1, width)
    stages = reduce_stages()
    for stage in stages:
        offsets = stage_offsets(stage)
        place = stage_place(index, stage)
        part = part.reshape(len(offsets), -1, width).astype(jnp.bfloat16)
        vector = lax.optimization_barrier(vector.astype(jnp.bfloat16))
        rows = part.shape[1]
        sums, vectors = [], []
        for order, offset in enumerate(offsets):
            piece = lax.dynamic_index_in_dim(part, place ^ order, 0, False)
            if offset:
                packed = jnp.concatenate([piece, vector], 0)
                packed = lax.ppermute(packed, axes, [(i, i ^ offset) for i in range(count)])
                sums.append(packed[:rows].astype(jnp.float32))
                vectors.append(packed[rows:].astype(jnp.float32))
            else:
                sums.append(piece.astype(jnp.float32))
                vectors.append(vector.astype(jnp.float32))
        part = fold_sum(sums)
        vector = fold_sum(vectors)
    part = lax.optimization_barrier(part.astype(jnp.bfloat16))[None]
    for stage in stages[::-1]:
        offsets = stage_offsets(stage)
        place = stage_place(index, stage)
        pieces = [part] + [
            lax.ppermute(part, axes, [(i, i ^ offset) for i in range(count)])
            for offset in offsets[1:]
        ]
        stacked = jnp.stack(pieces, 0)
        part = jnp.concatenate(
            [
                lax.dynamic_index_in_dim(stacked, place ^ order, 0, False)
                for order in range(len(offsets))
            ],
            0,
        )
    return (part.reshape(matrix.shape).astype(jnp.float32), vector[0])


def fold_border(extended, along, cells, inner_size):
    middle = lax.slice_in_dim(extended, 2 * cells, 2 * cells + inner_size, axis=along)
    before = lax.slice_in_dim(extended, 0, cells, axis=along)
    after_rim = lax.slice_in_dim(
        extended, inner_size + 3 * cells, inner_size + 4 * cells, axis=along
    )
    lead_pads = [(0, 0)] * extended.ndim
    tail_pads = [(0, 0)] * extended.ndim
    lead_pads[along] = (0, inner_size - cells)
    tail_pads[along] = (inner_size - cells, 0)
    return middle + jnp.pad(before, lead_pads) + jnp.pad(after_rim, tail_pads)


def local(face_input, kernel, convolution_bias, upstream, adjacency):
    face_count = face_input.shape[0]
    tile_rows = face_input.shape[1]
    tile_cols = face_input.shape[2]
    dilation_step = DILATION_STEP
    height = tile_rows + 2 * dilation_step
    breadth = tile_cols + 2 * dilation_step
    at_top = lax.axis_index("frow") == 0
    at_bottom = lax.axis_index("frow") == lax.axis_size("frow") - 1
    at_left = lax.axis_index("fcol") == 0
    at_right = lax.axis_index("fcol") == lax.axis_size("fcol") - 1
    column_index = jnp.arange(breadth)
    keep_cols = jnp.logical_not(
        at_left & (column_index < dilation_step)
        | at_right & (column_index >= tile_cols + dilation_step)
    )
    row_index = jnp.arange(height)
    keep_rows = jnp.logical_not(
        at_top & (row_index < dilation_step) | at_bottom & (row_index >= tile_rows + dilation_step)
    )
    padded_input = pad_field(face_input, adjacency.reshape(-1))
    row_pick = pick_table(
        jnp.where(at_top, adjacency[:, 0], adjacency[:, 1]), jnp.where(at_top, 0, 1), face_count
    )
    col_pick = pick_table(
        jnp.where(at_left, adjacency[:, 2], adjacency[:, 3]), jnp.where(at_left, 2, 3), face_count
    )
    random_values = ("NHWC", "HWIO", "NHWC")
    preactivation = (
        lax.conv_general_dilated(
            padded_input,
            kernel,
            (1, 1),
            "VALID",
            rhs_dilation=(dilation_step, dilation_step),
            dimension_numbers=random_values,
            preferred_element_type=jnp.float32,
        )
        + convolution_bias
    )
    activation = gelu_value(preactivation).astype(jnp.bfloat16)
    preactivation_gradient = (upstream.astype(jnp.float32) * gelu_slope(preactivation)).astype(
        jnp.bfloat16
    )
    tap_list = []
    for kernel_row_offset in range(3):
        for kernel_column_offset in range(3):
            input_window = padded_input[
                :,
                kernel_row_offset * dilation_step : kernel_row_offset * dilation_step + tile_rows,
                kernel_column_offset * dilation_step : kernel_column_offset * dilation_step
                + tile_cols,
            ]
            tap_list.append(
                lax.dot_general(
                    input_window,
                    preactivation_gradient,
                    (((0, 1, 2), (0, 1, 2)), ((), ())),
                    preferred_element_type=jnp.float32,
                )
            )
    kernel_local = jnp.stack(tap_list, 0).reshape(kernel.shape)
    bias_local = jnp.sum(preactivation_gradient.astype(jnp.float32), axis=(0, 1, 2))
    kernel_total, bias_total = reduce_everywhere(kernel_local, bias_local)
    scale = 1.0 / math.sqrt(
        face_count * tile_rows * lax.axis_size("frow") * tile_cols * lax.axis_size("fcol")
    )
    kernel_grad = kernel_total * scale
    bias_grad = bias_total * scale
    rotated_strip = jnp.transpose(jnp.flip(kernel, (0, 1)), (0, 1, 3, 2))
    twice = 2 * dilation_step
    padded_gradient = lax.conv_general_dilated(
        preactivation_gradient,
        rotated_strip,
        (1, 1),
        ((twice, twice), (twice, twice)),
        rhs_dilation=(dilation_step, dilation_step),
        dimension_numbers=random_values,
        preferred_element_type=jnp.float32,
    ).astype(jnp.bfloat16)
    row_seam = jnp.where(
        at_top, padded_gradient[:, :dilation_step], padded_gradient[:, tile_rows + dilation_step :]
    )
    row_seam = jnp.where(keep_cols[None, None, :, None], row_seam, jnp.zeros_like(row_seam))
    row_split = jnp.einsum("fk,fdwc->kdwc", row_pick, row_seam, preferred_element_type=jnp.float32)
    row_split = row_split.reshape((4, face_count) + row_split.shape[1:])
    col_seam = jnp.where(
        at_left,
        padded_gradient[:, :, :dilation_step],
        padded_gradient[:, :, tile_cols + dilation_step :],
    )
    col_seam = jnp.where(keep_rows[None, :, None, None], col_seam, jnp.zeros_like(col_seam))
    col_split = jnp.einsum("fk,fadc->kadc", col_pick, col_seam, preferred_element_type=jnp.float32)
    col_split = col_split.reshape((4, face_count) + col_split.shape[1:])
    row_far_grad = jnp.concatenate(
        [jnp.flip(row_split[2], 2), jnp.flip(row_split[3], (1, 2))], 1
    ).astype(jnp.bfloat16)
    col_far_grad = jnp.concatenate(
        [jnp.flip(col_split[2], 1), jnp.flip(col_split[3], (1, 2))], 2
    ).astype(jnp.bfloat16)
    row_back, col_back = reflect(row_far_grad, col_far_grad)
    wrap_rows = row_split[0] + row_back[:, :dilation_step].astype(jnp.float32)
    own_rows = jnp.flip(row_split[1], 1) + row_back[:, dilation_step:].astype(jnp.float32)
    wrap_cols = col_split[0] + col_back[:, :, :dilation_step].astype(jnp.float32)
    own_cols = jnp.flip(col_split[1], 2) + col_back[:, :, dilation_step:].astype(jnp.float32)
    gathered = padded_gradient.astype(jnp.float32)
    middle_rows = gathered[:, dilation_step : tile_rows + dilation_step]
    middle_rows = middle_rows + jnp.pad(
        jnp.where(at_top, own_rows, 0.0), ((0, 0), (0, tile_rows - dilation_step), (0, 0), (0, 0))
    )
    middle_rows = middle_rows + jnp.pad(
        jnp.where(at_bottom, own_rows, 0.0),
        ((0, 0), (tile_rows - dilation_step, 0), (0, 0), (0, 0)),
    )
    top_grad = jnp.where(at_top, wrap_rows, gathered[:, :dilation_step])
    bottom_grad = jnp.where(at_bottom, wrap_rows, gathered[:, tile_rows + dilation_step :])
    gathered = jnp.concatenate([top_grad, middle_rows, bottom_grad], 1)
    middle_cols = gathered[:, :, dilation_step : tile_cols + dilation_step]
    middle_cols = middle_cols + jnp.pad(
        jnp.where(at_left, own_cols, 0.0), ((0, 0), (0, 0), (0, tile_cols - dilation_step), (0, 0))
    )
    middle_cols = middle_cols + jnp.pad(
        jnp.where(at_right, own_cols, 0.0), ((0, 0), (0, 0), (tile_cols - dilation_step, 0), (0, 0))
    )
    left_grad = jnp.where(at_left, wrap_cols, gathered[:, :, :dilation_step])
    right_grad = jnp.where(at_right, wrap_cols, gathered[:, :, tile_cols + dilation_step :])
    gathered = jnp.concatenate([left_grad, middle_cols, right_grad], 2)
    returned = with_halo(
        gathered.astype(jnp.bfloat16), (("frow", 1), ("fcol", 2)), dilation_step
    ).astype(gathered.dtype)
    folded = fold_border(returned, 1, dilation_step, tile_rows)
    folded = fold_border(folded, 2, dilation_step, tile_cols)
    input_gradient = folded.astype(jnp.bfloat16)
    return (activation, input_gradient, kernel_grad, bias_grad)


def solution(mesh):
    return jax.shard_map(
        local,
        mesh=mesh,
        in_specs=(P(None, "frow", "fcol", None), P(), P(), P(None, "frow", "fcol", None), P()),
        out_specs=(P(None, "frow", "fcol", None), P(None, "frow", "fcol", None), P(), P()),
        check_vma=False,
    )
```

```python
import functools
import math

import jax
import jax.numpy as jnp
import numpy as np
from jax import lax
from jax.experimental import pallas as pl
from jax.experimental.pallas import tpu as pltpu
from jax.sharding import PartitionSpec as P

DILATION_STEP = 2


half_root = 0.7071067811865476
density_scale = 0.3989422804014327
axes = ("frow", "fcol")
vmem_bytes = 48 * 1024 * 1024


def shifted_pairs(row_step, col_step):
    rows, cols = lax.axis_size("frow"), lax.axis_size("fcol")
    return [
        (r * cols + c, (r + row_step) % rows * cols + (c + col_step) % cols)
        for r in range(rows)
        for c in range(cols)
    ]


def mirror_pairs(edge_rows, flip_rows, flip_cols):
    rows, cols = lax.axis_size("frow"), lax.axis_size("fcol")
    pairs = []
    for r in range(rows):
        for c in range(cols):
            on_edge = r in (0, rows - 1) if edge_rows else c in (0, cols - 1)
            if on_edge:
                target_row = rows - 1 - r if flip_rows else r
                target_col = cols - 1 - c if flip_cols else c
                pairs.append((r * cols + c, target_row * cols + target_col))
    return pairs


def round_up(value, step):
    return -(-value // step) * step


def col_flips(tile_rows):
    size = 2 * tile_rows
    table = np.zeros((4, size, size), np.float32)
    for kind in range(4):
        for y in range(tile_rows):
            for k in range(2):
                source_y = tile_rows - 1 - y if kind >= 2 else y
                source_k = 1 - k if kind % 2 else k
                table[kind, 2 * y + k, 2 * source_y + source_k] = 1
    return jnp.asarray(table, jnp.bfloat16)


def row_flips(width):
    size = 2 * width + 8
    table = np.zeros((4, size, size), np.float32)
    for kind in range(4):
        for d in range(2):
            source_d = 1 - d if kind % 2 else d
            for p in range(width):
                source_p = width - 1 - p if kind >= 2 else p
                table[kind, d * width + p, source_d * width + source_p] = 1
            for e in range(4):
                source_e = 3 - e if kind >= 2 else e
                table[kind, 2 * width + 4 * d + e, 2 * width + 4 * source_d + source_e] = 1
    return jnp.asarray(table, jnp.bfloat16)


def tail_picks(tile_rows):
    table = np.zeros((2, 8, 4 * tile_rows), np.float32)
    for place, first in enumerate((0, tile_rows - 2)):
        for d in range(2):
            for e in range(4):
                source = 2 * tile_rows * (e // 2) + 2 * (first + d) + e % 2
                table[place, 4 * d + e, source] = 1
    return jnp.asarray(table, jnp.bfloat16)


def stack_places(tile_rows, width):
    strip = round_up(2 * width + 8, 16)
    beside = tile_rows * width
    above = beside + 4 * tile_rows
    below = above + strip
    return (beside, above, below, round_up(below + strip, 128))


def stack_row(tile_rows, width, q, w):
    beside, above, below, _ = stack_places(tile_rows, width)
    side_cell = w if w < 2 else w - width
    inner = 2 <= w < width + 2
    if 2 <= q < tile_rows + 2:
        y = q - 2
        if inner:
            return y * width + w - 2
        return beside + 2 * tile_rows * (side_cell // 2) + 2 * y + side_cell % 2
    base, d = (above, q) if q < 2 else (below, q - tile_rows - 2)
    return base + (d * width + w - 2 if inner else 2 * width + 4 * d + side_cell)


def pad_picks(tile_rows, width):
    breadth = round_up(width + 4, 8)
    size = stack_places(tile_rows, width)[3]
    table = np.zeros(((tile_rows + 4) * breadth, size), np.float32)
    for q in range(tile_rows + 4):
        for w in range(width + 4):
            table[q * breadth + w, stack_row(tile_rows, width, q, w)] = 1
    return jnp.asarray(table, jnp.bfloat16)


def pick(table, value):
    return jnp.dot(table, value, preferred_element_type=jnp.float32).astype(jnp.bfloat16)


def seam_of(adjacency, face, side):
    base = (face * 4 + side) * 3
    near = (adjacency[base + 1] == side).astype(jnp.int32)
    return adjacency[base], 2 * adjacency[base + 2] + near


def col_kernel(
    adjacency, field, edges, beside, far_same, far_cross, flips, tails,
    side_out, top_out, bottom_out, edge_out, seam,
):
    face_count, tile_rows, width, channels = field.shape
    half = 2 * tile_rows
    row_place, col_place = lax.axis_index("frow"), lax.axis_index("fcol")
    at_top = row_place == 0
    at_bottom = row_place == lax.axis_size("frow") - 1
    at_left = col_place == 0
    at_right = col_place == lax.axis_size("fcol") - 1

    @pl.loop(0, face_count)
    def _(face):
        @pl.when(jnp.logical_or(at_left, at_right))
        def _():
            source, kind = seam_of(adjacency, face, jnp.where(at_left, 2, 3))

            @pl.when(kind == 0)
            def _():
                both = beside[source]
                seam[...] = jnp.where(at_left, both[half:], both[:half])

            @pl.when(kind == 1)
            def _():
                both = edges[source]
                seam[...] = pick(flips[1], jnp.where(at_left, both[:half], both[half:]))

            @pl.when(kind == 2)
            def _():
                seam[...] = pick(flips[2], far_cross[source])

            @pl.when(kind == 3)
            def _():
                seam[...] = pick(flips[3], far_same[source])

        both = beside[face]
        left = jnp.where(at_left, seam[...], both[half:])
        right = jnp.where(at_right, seam[...], both[:half])
        sides = jnp.concatenate([left, right], 0)
        side_out[face] = sides
        blank = jnp.zeros_like(left)
        inner = jnp.concatenate(
            [jnp.where(at_left, blank, left), jnp.where(at_right, blank, right)], 0
        )
        upper = pick(tails[0], jnp.where(at_top, inner, sides))
        lower = pick(tails[1], jnp.where(at_bottom, inner, sides))
        for d in range(2):
            rows = pl.ds(d * width, width)
            top_out[face, rows] = field[face, d]
            bottom_out[face, rows] = field[face, tile_rows - 2 + d]
            edge_out[face, rows] = jnp.where(
                at_top, field[face, d], field[face, tile_rows - 2 + d]
            )
        rows = pl.ds(2 * width, 8)
        top_out[face, rows] = upper
        bottom_out[face, rows] = lower
        edge_out[face, rows] = jnp.where(at_top, upper, lower)


def load_stack(adjacency, face, field, sides, up, down, edge, far_same, far_cross, flips, stack):
    tile_rows, width, channels = field.shape[1:]
    strip = 2 * width + 8
    beside, above, below, _ = stack_places(tile_rows, width)
    row_place = lax.axis_index("frow")
    stack[pl.ds(0, beside)] = field[face].reshape(beside, channels)
    stack[pl.ds(beside, 4 * tile_rows)] = sides[face]
    for side, place, near in ((0, above, up), (1, below, down)):
        at_edge = row_place == side * (lax.axis_size("frow") - 1)
        rows = pl.ds(place, strip)

        @pl.when(jnp.logical_not(at_edge))
        def _():
            stack[rows] = near[face]

        source, kind = seam_of(adjacency, face, side)
        for choice, strips in enumerate((near, edge, far_cross, far_same)):

            @pl.when(jnp.logical_and(at_edge, kind == choice))
            def _():
                stack[rows] = pick(flips[choice], strips[source])


def pad_kernel(
    adjacency, field, sides, up, down, edge, far_same, far_cross, flips, picks, padded, stack
):
    face_count, tile_rows, width, channels = field.shape
    breadth = picks.shape[0] // (tile_rows + 4)
    stack[...] = jnp.zeros_like(stack)

    @pl.loop(0, face_count)
    def _(face):
        load_stack(
            adjacency, face, field, sides, up, down, edge, far_same, far_cross, flips, stack
        )
        out = pick(picks[...], stack[...])
        for q in range(tile_rows + 4):
            padded[face, q] = out[q * breadth : q * breadth + width + 4]


def whole(count):
    return [pl.BlockSpec(memory_space=pltpu.SMEM)] + [
        pl.BlockSpec(memory_space=pltpu.VMEM) for _ in range(count)
    ]


def gather_strips(field, adjacency):
    face_count, tile_rows, width, channels = field.shape
    cols = lax.axis_size("fcol")
    left = field[:, :, :2].reshape(face_count, 2 * tile_rows, channels)
    right = field[:, :, width - 2 :].reshape(face_count, 2 * tile_rows, channels)
    edges = jnp.concatenate([left, right], 1)
    if cols == 2:
        beside = lax.ppermute(edges, axes, shifted_pairs(0, 1))
    else:
        beside = jnp.concatenate(
            [
                lax.ppermute(left, axes, shifted_pairs(0, -1)),
                lax.ppermute(right, axes, shifted_pairs(0, 1)),
            ],
            1,
        )
    edge = jnp.where(lax.axis_index("fcol") == 0, left, right)
    far_same = lax.ppermute(edge, axes, mirror_pairs(False, True, False))
    far_cross = lax.ppermute(edge, axes, mirror_pairs(False, True, True))
    strip = jax.ShapeDtypeStruct((face_count, 2 * width + 8, channels), field.dtype)
    sides, top, bottom, edge_strip = pl.pallas_call(
        col_kernel,
        out_shape=(jax.ShapeDtypeStruct(edges.shape, field.dtype), strip, strip, strip),
        in_specs=whole(7),
        out_specs=[pl.BlockSpec(memory_space=pltpu.VMEM)] * 4,
        scratch_shapes=[pltpu.VMEM((2 * tile_rows, channels), field.dtype)],
        compiler_params=pltpu.CompilerParams(vmem_limit_bytes=vmem_bytes),
        cost_estimate=pl.CostEstimate(flops=1000, bytes_accessed=3000000, transcendentals=0),
    )(
        adjacency, field, edges, beside, far_same, far_cross,
        col_flips(tile_rows), tail_picks(tile_rows),
    )
    up = lax.ppermute(bottom, axes, shifted_pairs(1, 0))
    down = lax.ppermute(top, axes, shifted_pairs(-1, 0))
    row_same = lax.ppermute(edge_strip, axes, mirror_pairs(True, False, True))
    row_cross = lax.ppermute(edge_strip, axes, mirror_pairs(True, True, True))
    return (field, sides, up, down, edge_strip, row_same, row_cross)


def pad_field(field, adjacency):
    face_count, tile_rows, width, channels = field.shape
    strips = gather_strips(field, adjacency)
    padded = (face_count, tile_rows + 4, width + 4, channels)
    size = stack_places(tile_rows, width)[3]
    return pl.pallas_call(
        pad_kernel,
        out_shape=jax.ShapeDtypeStruct(padded, field.dtype),
        in_specs=whole(9),
        out_specs=pl.BlockSpec(memory_space=pltpu.VMEM),
        scratch_shapes=[pltpu.VMEM((size, channels), field.dtype)],
        compiler_params=pltpu.CompilerParams(vmem_limit_bytes=vmem_bytes),
        cost_estimate=pl.CostEstimate(flops=1000, bytes_accessed=5000000, transcendentals=0),
    )(adjacency, *strips, row_flips(width), pad_picks(tile_rows, width))


def seam_row_picks(width):
    size = round_up(2 * width + 8, 16)
    table = np.zeros((3, 2 * width, size), np.float32)
    for shift in range(3):
        for d in range(2):
            for x in range(width):
                w = x + 2 * shift
                if 2 <= w < width + 2:
                    source = d * width + w - 2
                else:
                    source = 2 * width + 4 * d + (w if w < 2 else w - width)
                table[shift, d * width + x, source] = 1
    return jnp.asarray(table, jnp.bfloat16)


def seam_col_picks(tile_rows, width):
    size = stack_places(tile_rows, width)[3]
    table = np.zeros((2, 3 * 2 * tile_rows, size), np.float32)
    for right in range(2):
        for shift in range(3):
            for y in range(tile_rows):
                for k in range(2):
                    w = width + 2 + k if right else k
                    table[
                        right,
                        (shift * tile_rows + y) * 2 + k,
                        stack_row(tile_rows, width, y + 2 * shift, w),
                    ] = 1
    return jnp.asarray(table, jnp.bfloat16)


def tap_dot(value, tap):
    return lax.dot_general(value, tap, (((1,), (1,)), ((), ())), preferred_element_type=jnp.float32)


def return_kernel(
    adjacency, field, sides, up, down, edge, far_same, far_cross, flips, picks, row_picks,
    col_picks, kernel, padded, extra, stack, kept_picks, col_terms, col_sum,
):
    face_count, tile_rows, width, channels = field.shape
    breadth = picks.shape[0] // (tile_rows + 4)
    half = 2 * tile_rows
    slot = round_up(half, 16)
    _, above, below, _ = stack_places(tile_rows, width)
    strip = row_picks.shape[2]
    row_place, col_place = lax.axis_index("frow"), lax.axis_index("fcol")
    at_top = row_place == 0
    at_bottom = row_place == lax.axis_size("frow") - 1
    at_left = col_place == 0
    at_right = col_place == lax.axis_size("fcol") - 1
    on_col_edge = jnp.logical_or(at_left, at_right)
    stack[...] = jnp.zeros_like(stack)
    extra[...] = jnp.zeros_like(extra)
    col_terms[...] = jnp.zeros_like(col_terms)
    cell = lax.broadcasted_iota(jnp.int32, (breadth, picks.shape[1]), 0)
    for q in range(tile_rows + 4):
        rows = pl.ds(q * breadth, breadth)
        dropped = jnp.logical_or(
            jnp.logical_and(at_left, cell < 2), jnp.logical_and(at_right, cell >= width + 2)
        )
        if q < 2:
            dropped = jnp.logical_or(dropped, at_top)
        if q >= tile_rows + 2:
            dropped = jnp.logical_or(dropped, at_bottom)
        kept = jnp.where(dropped, 0.0, picks[rows].astype(jnp.float32))
        kept_picks[rows] = kept.astype(jnp.bfloat16)

    @pl.loop(0, face_count)
    def _(face):
        load_stack(
            adjacency, face, field, sides, up, down, edge, far_same, far_cross, flips, stack
        )
        out = pick(kept_picks[...], stack[...])
        for q in range(tile_rows + 4):
            padded[face, q] = out[q * breadth : q * breadth + width + 4]
        for side, place, at_edge in ((0, above, at_top), (1, below, at_bottom)):

            @pl.when(at_edge)
            def _():
                base = (face * 4 + side) * 3
                row_tap = 2 * adjacency[base + 1]
                turned = adjacency[base + 2]
                total = jnp.zeros((2 * width, channels), jnp.float32)
                for shift in range(3):
                    value = pick(row_picks[shift], stack[pl.ds(place, strip)])
                    col_tap = jnp.where(turned == 1, shift, 2 - shift)
                    total += tap_dot(value, kernel[row_tap, col_tap])
                for d in range(2):
                    extra[face, side * (tile_rows - 2) + d] = total[d * width : (d + 1) * width]

        @pl.when(on_col_edge)
        def _():
            base = (face * 4 + jnp.where(at_left, 2, 3)) * 3
            variant = 2 * adjacency[base + 2] + adjacency[base + 1] - 2
            value = jnp.dot(
                col_picks[jnp.where(at_left, 0, 1)],
                stack[...],
                preferred_element_type=jnp.float32,
            )
            for shift in range(3):
                rows = pl.ds(pl.multiple_of(face * slot, 16), half)
                part = value[shift * half : (shift + 1) * half]
                col_terms[variant, shift, rows] = part.astype(jnp.bfloat16)

    @pl.when(on_col_edge)
    def _():
        total = jnp.zeros(col_sum.shape, jnp.float32)
        for variant in range(4):
            for shift in range(3):
                row_tap = shift if variant >= 2 else 2 - shift
                total += tap_dot(col_terms[variant, shift], kernel[row_tap, 2 * (variant % 2)])
        col_sum[...] = total

        @pl.loop(0, face_count)
        def _(face):
            value = col_sum[pl.ds(pl.multiple_of(face * slot, 16), half)]
            for first, at_edge in ((0, at_left), (width - 2, at_right)):

                @pl.when(at_edge)
                def _():
                    for y in range(tile_rows):
                        cells = pl.ds(first, 2)
                        extra[face, y, cells] = (
                            extra[face, y, cells] + value[2 * y : 2 * y + 2]
                        )


def return_field(field, adjacency, kernel):
    face_count, tile_rows, width, channels = field.shape
    strips = gather_strips(field, adjacency)
    padded = (face_count, tile_rows + 4, width + 4, channels)
    size = stack_places(tile_rows, width)[3]
    picks = pad_picks(tile_rows, width)
    cells = face_count * round_up(2 * tile_rows, 16)
    return pl.pallas_call(
        return_kernel,
        out_shape=(
            jax.ShapeDtypeStruct(padded, field.dtype),
            jax.ShapeDtypeStruct(field.shape, jnp.float32),
        ),
        in_specs=whole(12),
        out_specs=[pl.BlockSpec(memory_space=pltpu.VMEM)] * 2,
        scratch_shapes=[
            pltpu.VMEM((size, channels), field.dtype),
            pltpu.VMEM(picks.shape, field.dtype),
            pltpu.VMEM((4, 3, cells, channels), field.dtype),
            pltpu.VMEM((cells, channels), jnp.float32),
        ],
        compiler_params=pltpu.CompilerParams(vmem_limit_bytes=vmem_bytes),
        cost_estimate=pl.CostEstimate(flops=1000, bytes_accessed=8000000, transcendentals=0),
    )(
        adjacency, *strips, row_flips(width), picks, seam_row_picks(width),
        seam_col_picks(tile_rows, width), kernel,
    )


def gelu_value(value):
    return 0.5 * value * (1.0 + jax.scipy.special.erf(value * half_root))


def gelu_slope(value):
    return (
        0.5 * (1.0 + jax.scipy.special.erf(value * half_root))
        + value * jnp.exp(-0.5 * value * value) * density_scale
    )


def reduce_stages():
    col_bits = lax.axis_size("fcol").bit_length() - 1
    all_bits = (lax.axis_size("frow") * lax.axis_size("fcol")).bit_length() - 1
    rest = [1 << bit for bit in range(all_bits) if bit != col_bits]
    stages = [(1 << col_bits,)]
    while rest:
        stages.append(tuple(rest[:2]))
        rest = rest[2:]
    return stages


def stage_offsets(stage):
    return (0, stage[0]) if len(stage) == 1 else (0, stage[0], stage[1], stage[0] ^ stage[1])


def stage_place(index, stage):
    place = (index // stage[0]) % 2
    if len(stage) == 2:
        place = place + 2 * ((index // stage[1]) % 2)
    return place


def fold_sum(terms):
    while len(terms) > 1:
        terms = [terms[i] + terms[i + 1] for i in range(0, len(terms), 2)]
    return terms[0]


def reduce_everywhere(matrix, vector):
    count = lax.axis_size("frow") * lax.axis_size("fcol")
    index = lax.axis_index("frow") * lax.axis_size("fcol") + lax.axis_index("fcol")
    width = matrix.shape[-1]
    pad = jnp.zeros((7, width), jnp.float32)
    vector = jnp.concatenate([vector[None], pad], 0)
    part = matrix.reshape(-1, width)
    stages = reduce_stages()
    for stage in stages:
        offsets = stage_offsets(stage)
        place = stage_place(index, stage)
        part = part.reshape(len(offsets), -1, width).astype(jnp.bfloat16)
        vector = lax.optimization_barrier(vector.astype(jnp.bfloat16))
        rows = part.shape[1]
        sums, vectors = [], []
        for order, offset in enumerate(offsets):
            piece = lax.dynamic_index_in_dim(part, place ^ order, 0, False)
            if offset:
                packed = jnp.concatenate([piece, vector], 0)
                packed = lax.ppermute(packed, axes, [(i, i ^ offset) for i in range(count)])
                sums.append(packed[:rows].astype(jnp.float32))
                vectors.append(packed[rows:].astype(jnp.float32))
            else:
                sums.append(piece.astype(jnp.float32))
                vectors.append(vector.astype(jnp.float32))
        part = fold_sum(sums)
        vector = fold_sum(vectors)
    part = lax.optimization_barrier(part.astype(jnp.bfloat16))[None]
    for stage in stages[::-1]:
        offsets = stage_offsets(stage)
        place = stage_place(index, stage)
        pieces = [part] + [
            lax.ppermute(part, axes, [(i, i ^ offset) for i in range(count)])
            for offset in offsets[1:]
        ]
        stacked = jnp.stack(pieces, 0)
        part = jnp.concatenate(
            [
                lax.dynamic_index_in_dim(stacked, place ^ order, 0, False)
                for order in range(len(offsets))
            ],
            0,
        )
    return (part.reshape(matrix.shape).astype(jnp.float32), vector[0])


def local(face_input, kernel, convolution_bias, upstream, adjacency):
    face_count, tile_rows, tile_cols, channels = face_input.shape
    table = adjacency.reshape(-1)
    padded_input = pad_field(face_input, table)
    layout = ("NHWC", "HWIO", "NHWC")
    preactivation = (
        lax.conv_general_dilated(
            padded_input,
            kernel,
            (1, 1),
            "VALID",
            rhs_dilation=(DILATION_STEP, DILATION_STEP),
            dimension_numbers=layout,
            preferred_element_type=jnp.float32,
        )
        + convolution_bias
    )
    activation = gelu_value(preactivation).astype(jnp.bfloat16)
    pre_grad = (upstream.astype(jnp.float32) * gelu_slope(preactivation)).astype(jnp.bfloat16)
    tap_list = []
    for a in range(3):
        for b in range(3):
            row, col = a * DILATION_STEP, b * DILATION_STEP
            window = padded_input[:, row : row + tile_rows, col : col + tile_cols]
            tap_list.append(
                lax.dot_general(
                    window,
                    pre_grad,
                    (((0, 1, 2), (0, 1, 2)), ((), ())),
                    preferred_element_type=jnp.float32,
                )
            )
    kernel_local = jnp.stack(tap_list, 0).reshape(kernel.shape)
    bias_local = jnp.sum(pre_grad.astype(jnp.float32), axis=(0, 1, 2))
    kernel_total, bias_total = reduce_everywhere(kernel_local, bias_local)
    scale = 1.0 / math.sqrt(
        face_count * tile_rows * lax.axis_size("frow") * tile_cols * lax.axis_size("fcol")
    )
    kernel_grad = kernel_total * scale
    bias_grad = bias_total * scale
    padded_grad, extra = return_field(pre_grad, table, kernel)
    rotated = jnp.transpose(jnp.flip(kernel, (0, 1)), (0, 1, 3, 2))
    input_gradient = (
        lax.conv_general_dilated(
            padded_grad,
            rotated,
            (1, 1),
            "VALID",
            rhs_dilation=(DILATION_STEP, DILATION_STEP),
            dimension_numbers=layout,
            preferred_element_type=jnp.float32,
        )
        + extra
    ).astype(jnp.bfloat16)
    return (activation, input_gradient, kernel_grad, bias_grad)


def solution(mesh):
    return jax.shard_map(
        local,
        mesh=mesh,
        in_specs=(P(None, "frow", "fcol", None), P(), P(), P(None, "frow", "fcol", None), P()),
        out_specs=(P(None, "frow", "fcol", None), P(None, "frow", "fcol", None), P(), P()),
        check_vma=False,
    )
```

```python
import functools
import math

import jax
import jax.numpy as jnp
import numpy as np
from jax import lax
from jax.experimental import pallas as pl
from jax.experimental.pallas import tpu as pltpu
from jax.sharding import PartitionSpec as P

DILATION_STEP = 2


half_root = 0.7071067811865476
density_scale = 0.3989422804014327
axes = ("frow", "fcol")
vmem_bytes = 12 * 1024 * 1024


def shifted_pairs(row_step, col_step):
    rows, cols = lax.axis_size("frow"), lax.axis_size("fcol")
    return [
        (r * cols + c, (r + row_step) % rows * cols + (c + col_step) % cols)
        for r in range(rows)
        for c in range(cols)
    ]


def mirror_pairs(edge_rows, flip_rows, flip_cols):
    rows, cols = lax.axis_size("frow"), lax.axis_size("fcol")
    pairs = []
    for r in range(rows):
        for c in range(cols):
            on_edge = r in (0, rows - 1) if edge_rows else c in (0, cols - 1)
            if on_edge:
                target_row = rows - 1 - r if flip_rows else r
                target_col = cols - 1 - c if flip_cols else c
                pairs.append((r * cols + c, target_row * cols + target_col))
    return pairs


def round_up(value, step):
    return -(-value // step) * step


def col_flips(tile_rows):
    size = 2 * tile_rows
    table = np.zeros((4, size, size), np.float32)
    for kind in range(4):
        for y in range(tile_rows):
            for k in range(2):
                source_y = tile_rows - 1 - y if kind >= 2 else y
                source_k = 1 - k if kind % 2 else k
                table[kind, 2 * y + k, 2 * source_y + source_k] = 1
    return jnp.asarray(table, jnp.bfloat16)


def row_flips(width):
    size = 2 * width + 8
    table = np.zeros((4, size, size), np.float32)
    for kind in range(4):
        for d in range(2):
            source_d = 1 - d if kind % 2 else d
            for p in range(width):
                source_p = width - 1 - p if kind >= 2 else p
                table[kind, d * width + p, source_d * width + source_p] = 1
            for e in range(4):
                source_e = 3 - e if kind >= 2 else e
                table[kind, 2 * width + 4 * d + e, 2 * width + 4 * source_d + source_e] = 1
    return jnp.asarray(table, jnp.bfloat16)


def tail_picks(tile_rows):
    table = np.zeros((2, 8, 4 * tile_rows), np.float32)
    for place, first in enumerate((0, tile_rows - 2)):
        for d in range(2):
            for e in range(4):
                source = 2 * tile_rows * (e // 2) + 2 * (first + d) + e % 2
                table[place, 4 * d + e, source] = 1
    return jnp.asarray(table, jnp.bfloat16)


def stack_places(tile_rows, width):
    strip = round_up(2 * width + 8, 16)
    beside = tile_rows * width
    above = beside + 4 * tile_rows
    below = above + strip
    return (beside, above, below, round_up(below + strip, 128))


def stack_row(tile_rows, width, q, w):
    beside, above, below, _ = stack_places(tile_rows, width)
    side_cell = w if w < 2 else w - width
    inner = 2 <= w < width + 2
    if 2 <= q < tile_rows + 2:
        y = q - 2
        if inner:
            return y * width + w - 2
        return beside + 2 * tile_rows * (side_cell // 2) + 2 * y + side_cell % 2
    base, d = (above, q) if q < 2 else (below, q - tile_rows - 2)
    return base + (d * width + w - 2 if inner else 2 * width + 4 * d + side_cell)


def pad_picks(tile_rows, width):
    breadth = round_up(width + 4, 8)
    size = stack_places(tile_rows, width)[3]
    table = np.zeros(((tile_rows + 4) * breadth, size), np.float32)
    for q in range(tile_rows + 4):
        for w in range(width + 4):
            table[q * breadth + w, stack_row(tile_rows, width, q, w)] = 1
    return jnp.asarray(table, jnp.bfloat16)


def pick(table, value):
    return jnp.dot(table, value, preferred_element_type=jnp.float32).astype(jnp.bfloat16)


def seam_of(adjacency, face, side):
    base = (face * 4 + side) * 3
    near = (adjacency[base + 1] == side).astype(jnp.int32)
    return adjacency[base], 2 * adjacency[base + 2] + near


def col_kernel(
    adjacency, field, edges, beside, far_same, far_cross, flips, tails,
    side_out, top_out, bottom_out, edge_out, seam,
):
    face_count, tile_rows, width, channels = field.shape
    half = 2 * tile_rows
    row_place, col_place = lax.axis_index("frow"), lax.axis_index("fcol")
    at_top = row_place == 0
    at_bottom = row_place == lax.axis_size("frow") - 1
    at_left = col_place == 0
    at_right = col_place == lax.axis_size("fcol") - 1

    @pl.when(jnp.logical_or(at_left, at_right))
    def _():
        @pl.loop(0, face_count)
        def _(face):
            source, kind = seam_of(adjacency, face, jnp.where(at_left, 2, 3))

            @pl.when(kind == 0)
            def _():
                both = beside[source]
                seam[face] = jnp.where(at_left, both[half:], both[:half])

            @pl.when(kind == 1)
            def _():
                both = edges[source]
                seam[face] = pick(flips[1], jnp.where(at_left, both[:half], both[half:]))

            @pl.when(kind == 2)
            def _():
                seam[face] = pick(flips[2], far_cross[source])

            @pl.when(kind == 3)
            def _():
                seam[face] = pick(flips[3], far_same[source])

    for face in range(face_count):
        both = beside[face]
        left = jnp.where(at_left, seam[face], both[half:])
        right = jnp.where(at_right, seam[face], both[:half])
        sides = jnp.concatenate([left, right], 0)
        side_out[face] = sides
        blank = jnp.zeros_like(left)
        inner = jnp.concatenate(
            [jnp.where(at_left, blank, left), jnp.where(at_right, blank, right)], 0
        )
        upper = pick(tails[0], jnp.where(at_top, inner, sides))
        lower = pick(tails[1], jnp.where(at_bottom, inner, sides))
        for d in range(2):
            rows = pl.ds(d * width, width)
            first, last = field[face, d], field[face, tile_rows - 2 + d]
            top_out[face, rows] = first
            bottom_out[face, rows] = last
            edge_out[face, rows] = jnp.where(at_top, first, last)
        rows = pl.ds(2 * width, 8)
        top_out[face, rows] = upper
        bottom_out[face, rows] = lower
        edge_out[face, rows] = jnp.where(at_top, upper, lower)


def load_stack(adjacency, face, field, sides, up, down, edge, far_same, far_cross, flips, stack):
    tile_rows, width, channels = field.shape[1:]
    strip = 2 * width + 8
    beside, above, below, _ = stack_places(tile_rows, width)
    row_place = lax.axis_index("frow")
    stack[face, pl.ds(0, beside)] = field[face].reshape(beside, channels)
    stack[face, pl.ds(beside, 4 * tile_rows)] = sides[face]
    for side, place, near in ((0, above, up), (1, below, down)):
        at_edge = row_place == side * (lax.axis_size("frow") - 1)
        rows = pl.ds(place, strip)

        @pl.when(jnp.logical_not(at_edge))
        def _():
            stack[face, rows] = near[face]

        source, kind = seam_of(adjacency, face, side)
        for choice, strips in enumerate((near, edge, far_cross, far_same)):

            @pl.when(jnp.logical_and(at_edge, kind == choice))
            def _():
                stack[face, rows] = pick(flips[choice], strips[source])


def write_padded(picks, stack, padded):
    face_count, rows, breadth, channels = padded.shape
    step = picks.shape[0] // rows
    for face in range(face_count):
        out = pick(picks[...], stack[face])
        for q in range(rows):
            padded[face, q] = out[q * step : q * step + breadth]


def pad_kernel(
    adjacency, field, sides, up, down, edge, far_same, far_cross, flips, picks, padded, stack
):
    face_count, tile_rows, width, channels = field.shape
    stack[...] = jnp.zeros_like(stack)

    @pl.loop(0, face_count)
    def _(face):
        load_stack(
            adjacency, face, field, sides, up, down, edge, far_same, far_cross, flips, stack
        )

    write_padded(picks, stack, padded)


def whole(count):
    return [pl.BlockSpec(memory_space=pltpu.SMEM)] + [
        pl.BlockSpec(memory_space=pltpu.VMEM) for _ in range(count)
    ]


def gather_strips(field, adjacency):
    face_count, tile_rows, width, channels = field.shape
    cols = lax.axis_size("fcol")
    left = field[:, :, :2].reshape(face_count, 2 * tile_rows, channels)
    right = field[:, :, width - 2 :].reshape(face_count, 2 * tile_rows, channels)
    edges = jnp.concatenate([left, right], 1)
    if cols == 2:
        beside = lax.ppermute(edges, axes, shifted_pairs(0, 1))
    else:
        beside = jnp.concatenate(
            [
                lax.ppermute(left, axes, shifted_pairs(0, -1)),
                lax.ppermute(right, axes, shifted_pairs(0, 1)),
            ],
            1,
        )
    edge = jnp.where(lax.axis_index("fcol") == 0, left, right)
    far_same = lax.ppermute(edge, axes, mirror_pairs(False, True, False))
    far_cross = lax.ppermute(edge, axes, mirror_pairs(False, True, True))
    strip = jax.ShapeDtypeStruct((face_count, 2 * width + 8, channels), field.dtype)
    sides, top, bottom, edge_strip = pl.pallas_call(
        col_kernel,
        out_shape=(jax.ShapeDtypeStruct(edges.shape, field.dtype), strip, strip, strip),
        in_specs=whole(7),
        out_specs=[pl.BlockSpec(memory_space=pltpu.VMEM)] * 4,
        scratch_shapes=[pltpu.VMEM((face_count, 2 * tile_rows, channels), field.dtype)],
        compiler_params=pltpu.CompilerParams(vmem_limit_bytes=vmem_bytes),
        cost_estimate=pl.CostEstimate(flops=1000, bytes_accessed=3000000, transcendentals=0),
    )(
        adjacency, field, edges, beside, far_same, far_cross,
        col_flips(tile_rows), tail_picks(tile_rows),
    )
    up = lax.ppermute(bottom, axes, shifted_pairs(1, 0))
    down = lax.ppermute(top, axes, shifted_pairs(-1, 0))
    row_same = lax.ppermute(edge_strip, axes, mirror_pairs(True, False, True))
    row_cross = lax.ppermute(edge_strip, axes, mirror_pairs(True, True, True))
    return (field, sides, up, down, edge_strip, row_same, row_cross)


def pad_field(field, adjacency):
    face_count, tile_rows, width, channels = field.shape
    strips = gather_strips(field, adjacency)
    padded = (face_count, tile_rows + 4, width + 4, channels)
    size = stack_places(tile_rows, width)[3]
    return pl.pallas_call(
        pad_kernel,
        out_shape=jax.ShapeDtypeStruct(padded, field.dtype),
        in_specs=whole(9),
        out_specs=pl.BlockSpec(memory_space=pltpu.VMEM),
        scratch_shapes=[pltpu.VMEM((face_count, size, channels), field.dtype)],
        compiler_params=pltpu.CompilerParams(vmem_limit_bytes=vmem_bytes),
        cost_estimate=pl.CostEstimate(flops=1000, bytes_accessed=5000000, transcendentals=0),
    )(adjacency, *strips, row_flips(width), pad_picks(tile_rows, width))


def seam_row_picks(width):
    size = round_up(2 * width + 8, 16)
    table = np.zeros((3, 2 * width, size), np.float32)
    for shift in range(3):
        for d in range(2):
            for x in range(width):
                w = x + 2 * shift
                if 2 <= w < width + 2:
                    source = d * width + w - 2
                else:
                    source = 2 * width + 4 * d + (w if w < 2 else w - width)
                table[shift, d * width + x, source] = 1
    return jnp.asarray(table, jnp.bfloat16)


def seam_col_picks(tile_rows, width):
    size = stack_places(tile_rows, width)[3]
    table = np.zeros((2, 3 * 2 * tile_rows, size), np.float32)
    for right in range(2):
        for shift in range(3):
            for y in range(tile_rows):
                for k in range(2):
                    w = width + 2 + k if right else k
                    table[
                        right,
                        (shift * tile_rows + y) * 2 + k,
                        stack_row(tile_rows, width, y + 2 * shift, w),
                    ] = 1
    return jnp.asarray(table, jnp.bfloat16)


def return_kernel(
    adjacency, field, sides, up, down, edge, far_same, far_cross, flips, picks, row_picks,
    col_picks, rotated, padded, extra, stack, kept_picks, row_terms, col_terms, col_sum,
):
    face_count, tile_rows, width, channels = field.shape
    breadth = picks.shape[0] // (tile_rows + 4)
    half = 2 * tile_rows
    slot = round_up(half, 16)
    row_slot = 2 * width
    _, above, below, _ = stack_places(tile_rows, width)
    strip = row_picks.shape[1]
    row_place, col_place = lax.axis_index("frow"), lax.axis_index("fcol")
    at_top = row_place == 0
    at_bottom = row_place == lax.axis_size("frow") - 1
    at_left = col_place == 0
    at_right = col_place == lax.axis_size("fcol") - 1
    on_row_edge = jnp.logical_or(at_top, at_bottom)
    on_col_edge = jnp.logical_or(at_left, at_right)
    stack[...] = jnp.zeros_like(stack)
    extra[...] = jnp.zeros_like(extra)
    cell = lax.broadcasted_iota(jnp.int32, (breadth, picks.shape[1]), 0)
    for q in range(tile_rows + 4):
        rows = pl.ds(q * breadth, breadth)
        dropped = jnp.logical_or(
            jnp.logical_and(at_left, cell < 2), jnp.logical_and(at_right, cell >= width + 2)
        )
        if q < 2:
            dropped = jnp.logical_or(dropped, at_top)
        if q >= tile_rows + 2:
            dropped = jnp.logical_or(dropped, at_bottom)
        kept = jnp.where(dropped, 0.0, picks[rows].astype(jnp.float32))
        kept_picks[rows] = kept.astype(jnp.bfloat16)

    @pl.loop(0, face_count)
    def _(face):
        load_stack(
            adjacency, face, field, sides, up, down, edge, far_same, far_cross, flips, stack
        )

    write_padded(kept_picks, stack, padded)

    @pl.when(on_col_edge)
    def _():
        col_terms[...] = jnp.zeros_like(col_terms)
        table = col_picks[jnp.where(at_left, 0, 1)]

        @pl.loop(0, face_count)
        def _(face):
            base = (face * 4 + jnp.where(at_left, 2, 3)) * 3
            turned = adjacency[base + 2]
            value = jnp.dot(table, stack[face], preferred_element_type=jnp.float32)
            rows = pl.ds(pl.multiple_of(face * slot, 16), half)
            for shift in range(3):
                part = value[shift * half : (shift + 1) * half].astype(jnp.bfloat16)
                tap = jnp.where(turned == 1, 2 - shift, shift)
                col_terms[adjacency[base + 1] - 2, tap, rows] = part

        total = jnp.zeros(col_sum.shape, jnp.float32)
        for side in range(2):
            for tap in range(3):
                total += jnp.dot(
                    col_terms[side, tap],
                    rotated[tap, 2 - 2 * side],
                    preferred_element_type=jnp.float32,
                )
        col_sum[...] = total

    @pl.when(on_row_edge)
    def _():
        row_terms[...] = jnp.zeros_like(row_terms)

        @pl.loop(0, face_count)
        def _(face):
            base = (face * 4 + jnp.where(at_top, 0, 1)) * 3
            turned = adjacency[base + 2]
            place = pl.multiple_of(jnp.where(at_top, above, below), 16)
            value = pick(row_picks[...], stack[face, pl.ds(place, strip)])
            rows = pl.ds(pl.multiple_of(face * row_slot, 16), row_slot)
            for shift in range(3):
                part = value[shift * row_slot : (shift + 1) * row_slot]
                tap = jnp.where(turned == 1, 2 - shift, shift)
                row_terms[adjacency[base + 1], tap, rows] = part

        first = jnp.where(at_top, 0, tile_rows - 2)

        group = math.gcd(face_count, 4)

        @pl.loop(0, face_count // group)
        def _(part):
            size = group * row_slot
            rows = pl.ds(pl.multiple_of(part * size, 16), size)
            total = jnp.zeros((size, channels), jnp.float32)
            for side in range(2):
                for tap in range(3):
                    total += jnp.dot(
                        row_terms[side, tap, rows],
                        rotated[2 - 2 * side, tap],
                        preferred_element_type=jnp.float32,
                    )
            for face in range(group):
                for d in range(2):
                    start = face * row_slot + d * width
                    extra[part * group + face, first + d] = total[start : start + width]

    for edge_col, at_edge in ((0, at_left), (width - 2, at_right)):

        @pl.when(at_edge)
        def _():
            cells = pl.ds(edge_col, 2)
            for face in range(face_count):
                value = col_sum[pl.ds(face * slot, half)]
                for y in range(tile_rows):
                    extra[face, y, cells] = extra[face, y, cells] + value[2 * y : 2 * y + 2]


def return_field(field, adjacency, rotated):
    face_count, tile_rows, width, channels = field.shape
    strips = gather_strips(field, adjacency)
    padded = (face_count, tile_rows + 4, width + 4, channels)
    size = stack_places(tile_rows, width)[3]
    picks = pad_picks(tile_rows, width)
    cells = face_count * round_up(2 * tile_rows, 16)
    return pl.pallas_call(
        return_kernel,
        out_shape=(
            jax.ShapeDtypeStruct(padded, field.dtype),
            jax.ShapeDtypeStruct(field.shape, jnp.float32),
        ),
        in_specs=whole(12),
        out_specs=[pl.BlockSpec(memory_space=pltpu.VMEM)] * 2,
        scratch_shapes=[
            pltpu.VMEM((face_count, size, channels), field.dtype),
            pltpu.VMEM(picks.shape, field.dtype),
            pltpu.VMEM((2, 3, face_count * 2 * width, channels), field.dtype),
            pltpu.VMEM((2, 3, cells, channels), field.dtype),
            pltpu.VMEM((cells, channels), jnp.float32),
        ],
        compiler_params=pltpu.CompilerParams(vmem_limit_bytes=vmem_bytes),
        cost_estimate=pl.CostEstimate(flops=1000, bytes_accessed=8000000, transcendentals=0),
    )(
        adjacency, *strips, row_flips(width), picks,
        seam_row_picks(width).reshape(6 * width, -1),
        seam_col_picks(tile_rows, width), rotated,
    )


def gelu_value(value):
    return 0.5 * value * (1.0 + jax.scipy.special.erf(value * half_root))


def gelu_slope(value):
    return (
        0.5 * (1.0 + jax.scipy.special.erf(value * half_root))
        + value * jnp.exp(-0.5 * value * value) * density_scale
    )


def reduce_stages():
    col_bits = lax.axis_size("fcol").bit_length() - 1
    all_bits = (lax.axis_size("frow") * lax.axis_size("fcol")).bit_length() - 1
    rest = [1 << bit for bit in range(all_bits) if bit != col_bits]
    stages = [(1 << col_bits,)]
    while rest:
        stages.append(tuple(rest[:2]))
        rest = rest[2:]
    return stages


def stage_offsets(stage):
    return (0, stage[0]) if len(stage) == 1 else (0, stage[0], stage[1], stage[0] ^ stage[1])


def stage_place(index, stage):
    place = (index >> (stage[0].bit_length() - 1)) & 1
    if len(stage) == 2:
        place = place + 2 * ((index >> (stage[1].bit_length() - 1)) & 1)
    return place


def fold_sum(terms):
    while len(terms) > 1:
        terms = [terms[i] + terms[i + 1] for i in range(0, len(terms), 2)]
    return terms[0]


def reduce_everywhere(matrix, vector):
    count = lax.axis_size("frow") * lax.axis_size("fcol")
    index = lax.axis_index("frow") * lax.axis_size("fcol") + lax.axis_index("fcol")
    width = matrix.shape[-1]
    pad = jnp.zeros((7, width), jnp.float32)
    vector = jnp.concatenate([vector[None], pad], 0)
    part = matrix.reshape(-1, width)
    stages = reduce_stages()
    for stage in stages:
        offsets = stage_offsets(stage)
        place = stage_place(index, stage)
        part = part.reshape(len(offsets), -1, width).astype(jnp.bfloat16)
        vector = lax.optimization_barrier(vector.astype(jnp.bfloat16))
        rows = part.shape[1]
        sums, vectors = [], []
        for order, offset in enumerate(offsets):
            piece = lax.dynamic_slice_in_dim(part, place ^ order, 1, 0)[0]
            if offset:
                packed = jnp.concatenate([piece, vector], 0)
                packed = lax.ppermute(packed, axes, [(i, i ^ offset) for i in range(count)])
                sums.append(packed[:rows].astype(jnp.float32))
                vectors.append(packed[rows:].astype(jnp.float32))
            else:
                sums.append(piece.astype(jnp.float32))
                vectors.append(vector.astype(jnp.float32))
        part = fold_sum(sums)
        vector = fold_sum(vectors)
    part = lax.optimization_barrier(part.astype(jnp.bfloat16))[None]
    for stage in stages[::-1]:
        offsets = stage_offsets(stage)
        place = stage_place(index, stage)
        pieces = [part] + [
            lax.ppermute(part, axes, [(i, i ^ offset) for i in range(count)])
            for offset in offsets[1:]
        ]
        stacked = jnp.stack(pieces, 0)
        part = jnp.concatenate(
            [
                lax.dynamic_index_in_dim(stacked, place ^ order, 0, False)
                for order in range(len(offsets))
            ],
            0,
        )
    return (part.reshape(matrix.shape).astype(jnp.float32), vector[0])


def local(face_input, kernel, convolution_bias, upstream, adjacency):
    face_count, tile_rows, tile_cols, channels = face_input.shape
    table = adjacency.reshape(-1)
    padded_input = pad_field(face_input, table)
    layout = ("NHWC", "HWIO", "NHWC")
    preactivation = (
        lax.conv_general_dilated(
            padded_input,
            kernel,
            (1, 1),
            "VALID",
            rhs_dilation=(DILATION_STEP, DILATION_STEP),
            dimension_numbers=layout,
            preferred_element_type=jnp.float32,
        )
        + convolution_bias
    )
    activation = gelu_value(preactivation).astype(jnp.bfloat16)
    pre_grad = (upstream.astype(jnp.float32) * gelu_slope(preactivation)).astype(jnp.bfloat16)
    tap_list = []
    for a in range(3):
        for b in range(3):
            row, col = a * DILATION_STEP, b * DILATION_STEP
            window = padded_input[:, row : row + tile_rows, col : col + tile_cols]
            tap_list.append(
                lax.dot_general(
                    window,
                    pre_grad,
                    (((0, 1, 2), (0, 1, 2)), ((), ())),
                    preferred_element_type=jnp.float32,
                )
            )
    kernel_local = jnp.stack(tap_list, 0).reshape(kernel.shape)
    bias_local = jnp.sum(pre_grad.astype(jnp.float32), axis=(0, 1, 2))
    kernel_total, bias_total = reduce_everywhere(kernel_local, bias_local)
    scale = 1.0 / math.sqrt(
        face_count * tile_rows * lax.axis_size("frow") * tile_cols * lax.axis_size("fcol")
    )
    kernel_grad = kernel_total * scale
    bias_grad = bias_total * scale
    rotated = jnp.transpose(jnp.flip(kernel, (0, 1)), (0, 1, 3, 2))
    padded_grad, extra = return_field(pre_grad, table, rotated)
    input_gradient = (
        lax.conv_general_dilated(
            padded_grad,
            rotated,
            (1, 1),
            "VALID",
            rhs_dilation=(DILATION_STEP, DILATION_STEP),
            dimension_numbers=layout,
            preferred_element_type=jnp.float32,
        )
        + extra
    ).astype(jnp.bfloat16)
    return (activation, input_gradient, kernel_grad, bias_grad)


def solution(mesh):
    return jax.shard_map(
        local,
        mesh=mesh,
        in_specs=(P(None, "frow", "fcol", None), P(), P(), P(None, "frow", "fcol", None), P()),
        out_specs=(P(None, "frow", "fcol", None), P(None, "frow", "fcol", None), P(), P()),
        check_vma=False,
    )
```

```python
import functools
import math

import jax
import jax.numpy as jnp
import numpy as np
from jax import lax
from jax.experimental import pallas as pl
from jax.experimental.pallas import tpu as pltpu
from jax.sharding import PartitionSpec as P

DILATION_STEP = 2


half_root = 0.7071067811865476
density_scale = 0.3989422804014327
axes = ("frow", "fcol")
vmem_bytes = 12 * 1024 * 1024


def shifted_pairs(row_step, col_step):
    rows, cols = lax.axis_size("frow"), lax.axis_size("fcol")
    return [
        (r * cols + c, (r + row_step) % rows * cols + (c + col_step) % cols)
        for r in range(rows)
        for c in range(cols)
    ]


def mirror_pairs(edge_rows, flip_rows, flip_cols):
    rows, cols = lax.axis_size("frow"), lax.axis_size("fcol")
    pairs = []
    for r in range(rows):
        for c in range(cols):
            on_edge = r in (0, rows - 1) if edge_rows else c in (0, cols - 1)
            if on_edge:
                target_row = rows - 1 - r if flip_rows else r
                target_col = cols - 1 - c if flip_cols else c
                pairs.append((r * cols + c, target_row * cols + target_col))
    return pairs


def round_up(value, step):
    return -(-value // step) * step


def row_flips(width):
    size = 2 * width + 8
    table = np.zeros((4, size, size), np.float32)
    for kind in range(4):
        for d in range(2):
            source_d = 1 - d if kind % 2 else d
            for p in range(width):
                source_p = width - 1 - p if kind >= 2 else p
                table[kind, d * width + p, source_d * width + source_p] = 1
            for e in range(4):
                source_e = 3 - e if kind >= 2 else e
                table[kind, 2 * width + 4 * d + e, 2 * width + 4 * source_d + source_e] = 1
    return jnp.asarray(table, jnp.bfloat16)


def corner_picks(width):
    table = np.zeros((2, 8, 2 * width), np.float32)
    for d in range(2):
        for k in range(2):
            table[0, 4 * d + 2 + k, d * width + k] = 1
            table[1, 4 * d + k, d * width + width - 2 + k] = 1
    return jnp.asarray(table, jnp.bfloat16)


def stack_places(tile_rows, width):
    strip = round_up(2 * width + 8, 16)
    beside = tile_rows * width
    above = beside + 4 * tile_rows
    below = above + strip
    return (beside, above, below, round_up(below + strip, 128))


def stack_row(tile_rows, width, q, w):
    beside, above, below, _ = stack_places(tile_rows, width)
    side_cell = w if w < 2 else w - width
    inner = 2 <= w < width + 2
    if 2 <= q < tile_rows + 2:
        y = q - 2
        if inner:
            return y * width + w - 2
        return beside + 2 * tile_rows * (side_cell // 2) + 2 * y + side_cell % 2
    base, d = (above, q) if q < 2 else (below, q - tile_rows - 2)
    return base + (d * width + w - 2 if inner else 2 * width + 4 * d + side_cell)


def pad_picks(tile_rows, width):
    breadth = round_up(width + 4, 8)
    size = stack_places(tile_rows, width)[3]
    table = np.zeros(((tile_rows + 4) * breadth, size), np.float32)
    for q in range(tile_rows + 4):
        for w in range(width + 4):
            table[q * breadth + w, stack_row(tile_rows, width, q, w)] = 1
    return jnp.asarray(table, jnp.bfloat16)


def pick(table, value):
    return jnp.dot(table, value, preferred_element_type=jnp.float32).astype(jnp.bfloat16)


def seam_of(adjacency, face, side):
    base = (face * 4 + side) * 3
    near = (adjacency[base + 1] == side).astype(jnp.int32)
    return adjacency[base], 2 * adjacency[base + 2] + near


def one_hot(source, size):
    columns = lax.broadcasted_iota(jnp.int32, (source.shape[0], size), 1)
    return jnp.where(source == columns, 1.0, 0.0).astype(jnp.bfloat16)


def col_flip(kind, tile_rows):
    size = 2 * tile_rows
    row = lax.broadcasted_iota(jnp.int32, (size, size), 0)
    if kind >= 2:
        row = 2 * (tile_rows - 1 - (row >> 1)) + (row & 1)
    return one_hot(row ^ 1 if kind % 2 else row, size)


def tail_pick(first, tile_rows):
    row = lax.broadcasted_iota(jnp.int32, (8, 4 * tile_rows), 0)
    place = 2 * tile_rows * ((row >> 1) & 1) + 2 * (first + (row >> 2)) + (row & 1)
    return one_hot(place, 4 * tile_rows)


def side_kernel(
    adjacency, edges, beside, far_same, far_cross, side_out, upper_out, lower_out, seam
):
    face_count, both_sides, channels = edges.shape
    tile_rows = both_sides // 4
    half = 2 * tile_rows
    row_place, col_place = lax.axis_index("frow"), lax.axis_index("fcol")
    at_top = row_place == 0
    at_bottom = row_place == lax.axis_size("frow") - 1
    at_left = col_place == 0
    at_right = col_place == lax.axis_size("fcol") - 1

    @pl.when(jnp.logical_or(at_left, at_right))
    def _():
        @pl.loop(0, face_count)
        def _(face):
            source, kind = seam_of(adjacency, face, jnp.where(at_left, 2, 3))

            @pl.when(kind == 0)
            def _():
                both = beside[source]
                seam[face] = jnp.where(at_left, both[half:], both[:half])

            @pl.when(kind == 1)
            def _():
                both = edges[source]
                own = jnp.where(at_left, both[:half], both[half:])
                seam[face] = pick(col_flip(1, tile_rows), own)

            @pl.when(kind == 2)
            def _():
                seam[face] = pick(col_flip(2, tile_rows), far_cross[source])

            @pl.when(kind == 3)
            def _():
                seam[face] = pick(col_flip(3, tile_rows), far_same[source])

    upper_pick = tail_pick(0, tile_rows)
    lower_pick = tail_pick(tile_rows - 2, tile_rows)
    for face in range(face_count):
        both = beside[face]
        left = jnp.where(at_left, seam[face], both[half:])
        right = jnp.where(at_right, seam[face], both[:half])
        sides = jnp.concatenate([left, right], 0)
        side_out[face] = sides
        blank = jnp.zeros_like(left)
        inner = jnp.concatenate(
            [jnp.where(at_left, blank, left), jnp.where(at_right, blank, right)], 0
        )
        upper_out[face] = pick(upper_pick, jnp.where(at_top, inner, sides))
        lower_out[face] = pick(lower_pick, jnp.where(at_bottom, inner, sides))


def load_stack(adjacency, face, strips, flips, corners, stack):
    field, sides, tails, up, down, up_tail, down_tail, edge, far_same, far_cross = strips[:10]
    tile_rows, width, channels = field.shape[1:]
    strip = 2 * width + 8
    beside, above, below, _ = stack_places(tile_rows, width)
    row_place, col_place = lax.axis_index("frow"), lax.axis_index("fcol")
    stack[face, pl.ds(0, beside)] = field[face].reshape(beside, channels)
    stack[face, pl.ds(beside, 4 * tile_rows)] = sides[face]
    for side, place, near, near_tail in (
        (0, above, up, up_tail), (1, below, down, down_tail),
    ):
        at_edge = row_place == side * (lax.axis_size("frow") - 1)
        rows = pl.ds(place, strip)

        @pl.when(jnp.logical_not(at_edge))
        def _():
            stack[face, pl.ds(place, 2 * width)] = near[face]
            stack[face, pl.ds(place + 2 * width, 8)] = near_tail[face]

        source, kind = seam_of(adjacency, face, side)
        for choice, main in enumerate((near, edge, far_cross, far_same)):

            @pl.when(jnp.logical_and(at_edge, kind == choice))
            def _():
                if choice == 0:
                    tail = near_tail[source]
                elif choice == 1:
                    tail = tails[side][source]
                elif len(strips) > 10:
                    tail = strips[13 - choice][source]
                else:
                    other = near if choice == 2 else edge
                    tail = pick(corners[1 - col_place], other[source])
                stack[face, rows] = pick(
                    flips[choice], jnp.concatenate([main[source], tail], 0)
                )


def unpack_strips(refs, count):
    strips = list(refs[:count])
    return (strips[0], strips[1], (strips[2], strips[3]), *strips[4:])


def write_padded(picks, stack, padded):
    face_count, rows, breadth, channels = padded.shape
    step = picks.shape[0] // rows
    for face in range(face_count):
        out = pick(picks[...], stack[face])
        for q in range(rows):
            padded[face, q] = out[q * step : q * step + breadth]


def pad_kernel(count, adjacency, *refs):
    strips = unpack_strips(refs, count)
    flips, corners, picks, padded, stack = refs[count:]
    face_count = strips[0].shape[0]
    stack[...] = jnp.zeros_like(stack)

    @pl.loop(0, face_count)
    def _(face):
        load_stack(adjacency, face, strips, flips, corners, stack)

    write_padded(picks, stack, padded)


def whole(count):
    return [pl.BlockSpec(memory_space=pltpu.SMEM)] + [
        pl.BlockSpec(memory_space=pltpu.VMEM) for _ in range(count)
    ]


def gather_strips(field, adjacency):
    face_count, tile_rows, width, channels = field.shape
    cols = lax.axis_size("fcol")
    at_top = lax.axis_index("frow") == 0
    top = field[:, :2].reshape(face_count, 2 * width, channels)
    bottom = field[:, tile_rows - 2 :].reshape(face_count, 2 * width, channels)
    edge_strip = jnp.where(at_top, top, bottom)
    row_same = lax.ppermute(edge_strip, axes, mirror_pairs(True, False, True))
    row_cross = lax.ppermute(edge_strip, axes, mirror_pairs(True, True, True))
    up = lax.ppermute(bottom, axes, shifted_pairs(1, 0))
    down = lax.ppermute(top, axes, shifted_pairs(-1, 0))
    left = field[:, :, :2].reshape(face_count, 2 * tile_rows, channels)
    right = field[:, :, width - 2 :].reshape(face_count, 2 * tile_rows, channels)
    edges = jnp.concatenate([left, right], 1)
    if cols == 2:
        beside = lax.ppermute(edges, axes, shifted_pairs(0, 1))
    else:
        beside = jnp.concatenate(
            [
                lax.ppermute(left, axes, shifted_pairs(0, -1)),
                lax.ppermute(right, axes, shifted_pairs(0, 1)),
            ],
            1,
        )
    edge = jnp.where(lax.axis_index("fcol") == 0, left, right)
    far_same = lax.ppermute(edge, axes, mirror_pairs(False, True, False))
    far_cross = lax.ppermute(edge, axes, mirror_pairs(False, True, True))
    tail = jax.ShapeDtypeStruct((face_count, 8, channels), field.dtype)
    sides, upper, lower = pl.pallas_call(
        side_kernel,
        out_shape=(jax.ShapeDtypeStruct(edges.shape, field.dtype), tail, tail),
        in_specs=whole(4),
        out_specs=[pl.BlockSpec(memory_space=pltpu.VMEM)] * 3,
        scratch_shapes=[pltpu.VMEM((face_count, 2 * tile_rows, channels), field.dtype)],
        compiler_params=pltpu.CompilerParams(vmem_limit_bytes=vmem_bytes),
        cost_estimate=pl.CostEstimate(flops=1000, bytes_accessed=3000000, transcendentals=0),
    )(adjacency, edges, beside, far_same, far_cross)
    up_tail = lax.ppermute(lower, axes, shifted_pairs(1, 0))
    down_tail = lax.ppermute(upper, axes, shifted_pairs(-1, 0))
    strips = [
        field, sides, upper, lower, up, down, up_tail, down_tail, edge_strip, row_same, row_cross,
    ]
    if cols > 2:
        own_tail = jnp.where(at_top, upper, lower)
        strips.append(lax.ppermute(own_tail, axes, mirror_pairs(True, False, True)))
        strips.append(lax.ppermute(own_tail, axes, mirror_pairs(True, True, True)))
    return strips


def pad_field(field, adjacency):
    face_count, tile_rows, width, channels = field.shape
    strips = gather_strips(field, adjacency)
    padded = (face_count, tile_rows + 4, width + 4, channels)
    size = stack_places(tile_rows, width)[3]
    return pl.pallas_call(
        functools.partial(pad_kernel, len(strips)),
        out_shape=jax.ShapeDtypeStruct(padded, field.dtype),
        in_specs=whole(len(strips) + 3),
        out_specs=pl.BlockSpec(memory_space=pltpu.VMEM),
        scratch_shapes=[pltpu.VMEM((face_count, size, channels), field.dtype)],
        compiler_params=pltpu.CompilerParams(vmem_limit_bytes=vmem_bytes),
        cost_estimate=pl.CostEstimate(flops=1000, bytes_accessed=5000000, transcendentals=0),
    )(adjacency, *strips, row_flips(width), corner_picks(width), pad_picks(tile_rows, width))


def seam_row_picks(width):
    size = round_up(2 * width + 8, 16)
    table = np.zeros((3, 2 * width, size), np.float32)
    for shift in range(3):
        for d in range(2):
            for x in range(width):
                w = x + 2 * shift
                if 2 <= w < width + 2:
                    source = d * width + w - 2
                else:
                    source = 2 * width + 4 * d + (w if w < 2 else w - width)
                table[shift, d * width + x, source] = 1
    return jnp.asarray(table, jnp.bfloat16)


def seam_col_picks(tile_rows, width):
    size = stack_places(tile_rows, width)[3]
    table = np.zeros((2, 3 * 2 * tile_rows, size), np.float32)
    for right in range(2):
        for shift in range(3):
            for y in range(tile_rows):
                for k in range(2):
                    w = width + 2 + k if right else k
                    table[
                        right,
                        (shift * tile_rows + y) * 2 + k,
                        stack_row(tile_rows, width, y + 2 * shift, w),
                    ] = 1
    return jnp.asarray(table, jnp.bfloat16)


def return_kernel(count, adjacency, *refs):
    strips = unpack_strips(refs, count)
    flips, corners, picks, row_picks, col_picks, rotated, padded, extra = refs[count : count + 8]
    stack, kept_picks, row_terms, col_terms, col_sum = refs[count + 8 :]
    field = strips[0]
    face_count, tile_rows, width, channels = field.shape
    breadth = picks.shape[0] // (tile_rows + 4)
    half = 2 * tile_rows
    slot = round_up(half, 16)
    row_slot = 2 * width
    _, above, below, _ = stack_places(tile_rows, width)
    strip = row_picks.shape[1]
    row_place, col_place = lax.axis_index("frow"), lax.axis_index("fcol")
    at_top = row_place == 0
    at_bottom = row_place == lax.axis_size("frow") - 1
    at_left = col_place == 0
    at_right = col_place == lax.axis_size("fcol") - 1
    on_row_edge = jnp.logical_or(at_top, at_bottom)
    on_col_edge = jnp.logical_or(at_left, at_right)
    stack[...] = jnp.zeros_like(stack)
    extra[...] = jnp.zeros_like(extra)
    cell = lax.broadcasted_iota(jnp.int32, (breadth, picks.shape[1]), 0)
    for q in range(tile_rows + 4):
        rows = pl.ds(q * breadth, breadth)
        dropped = jnp.logical_or(
            jnp.logical_and(at_left, cell < 2), jnp.logical_and(at_right, cell >= width + 2)
        )
        if q < 2:
            dropped = jnp.logical_or(dropped, at_top)
        if q >= tile_rows + 2:
            dropped = jnp.logical_or(dropped, at_bottom)
        kept = jnp.where(dropped, 0.0, picks[rows].astype(jnp.float32))
        kept_picks[rows] = kept.astype(jnp.bfloat16)

    @pl.loop(0, face_count)
    def _(face):
        load_stack(adjacency, face, strips, flips, corners, stack)

    write_padded(kept_picks, stack, padded)

    @pl.when(on_col_edge)
    def _():
        col_terms[...] = jnp.zeros_like(col_terms)
        table = col_picks[jnp.where(at_left, 0, 1)]

        @pl.loop(0, face_count)
        def _(face):
            base = (face * 4 + jnp.where(at_left, 2, 3)) * 3
            turned = adjacency[base + 2]
            value = jnp.dot(table, stack[face], preferred_element_type=jnp.float32)
            rows = pl.ds(pl.multiple_of(face * slot, 16), half)
            for shift in range(3):
                part = value[shift * half : (shift + 1) * half].astype(jnp.bfloat16)
                tap = jnp.where(turned == 1, 2 - shift, shift)
                col_terms[adjacency[base + 1] - 2, tap, rows] = part

        total = jnp.zeros(col_sum.shape, jnp.float32)
        for side in range(2):
            for tap in range(3):
                total += jnp.dot(
                    col_terms[side, tap],
                    rotated[tap, 2 - 2 * side],
                    preferred_element_type=jnp.float32,
                )
        col_sum[...] = total

    @pl.when(on_row_edge)
    def _():
        row_terms[...] = jnp.zeros_like(row_terms)

        @pl.loop(0, face_count)
        def _(face):
            base = (face * 4 + jnp.where(at_top, 0, 1)) * 3
            turned = adjacency[base + 2]
            place = pl.multiple_of(jnp.where(at_top, above, below), 16)
            value = pick(row_picks[...], stack[face, pl.ds(place, strip)])
            rows = pl.ds(pl.multiple_of(face * row_slot, 16), row_slot)
            for shift in range(3):
                part = value[shift * row_slot : (shift + 1) * row_slot]
                tap = jnp.where(turned == 1, 2 - shift, shift)
                row_terms[adjacency[base + 1], tap, rows] = part

        first = jnp.where(at_top, 0, tile_rows - 2)

        group = math.gcd(face_count, 4)

        @pl.loop(0, face_count // group)
        def _(part):
            size = group * row_slot
            rows = pl.ds(pl.multiple_of(part * size, 16), size)
            total = jnp.zeros((size, channels), jnp.float32)
            for side in range(2):
                for tap in range(3):
                    total += jnp.dot(
                        row_terms[side, tap, rows],
                        rotated[2 - 2 * side, tap],
                        preferred_element_type=jnp.float32,
                    )
            for face in range(group):
                for d in range(2):
                    start = face * row_slot + d * width
                    extra[part * group + face, first + d] = total[start : start + width]

    for edge_col, at_edge in ((0, at_left), (width - 2, at_right)):

        @pl.when(at_edge)
        def _():
            cells = pl.ds(edge_col, 2)
            for face in range(face_count):
                value = col_sum[pl.ds(face * slot, half)]
                for y in range(tile_rows):
                    extra[face, y, cells] = extra[face, y, cells] + value[2 * y : 2 * y + 2]


def return_field(field, adjacency, rotated):
    face_count, tile_rows, width, channels = field.shape
    strips = gather_strips(field, adjacency)
    padded = (face_count, tile_rows + 4, width + 4, channels)
    size = stack_places(tile_rows, width)[3]
    picks = pad_picks(tile_rows, width)
    cells = face_count * round_up(2 * tile_rows, 16)
    return pl.pallas_call(
        functools.partial(return_kernel, len(strips)),
        out_shape=(
            jax.ShapeDtypeStruct(padded, field.dtype),
            jax.ShapeDtypeStruct(field.shape, jnp.float32),
        ),
        in_specs=whole(len(strips) + 6),
        out_specs=[pl.BlockSpec(memory_space=pltpu.VMEM)] * 2,
        scratch_shapes=[
            pltpu.VMEM((face_count, size, channels), field.dtype),
            pltpu.VMEM(picks.shape, field.dtype),
            pltpu.VMEM((2, 3, face_count * 2 * width, channels), field.dtype),
            pltpu.VMEM((2, 3, cells, channels), field.dtype),
            pltpu.VMEM((cells, channels), jnp.float32),
        ],
        compiler_params=pltpu.CompilerParams(vmem_limit_bytes=vmem_bytes),
        cost_estimate=pl.CostEstimate(flops=1000, bytes_accessed=8000000, transcendentals=0),
    )(
        adjacency, *strips, row_flips(width), corner_picks(width), picks,
        seam_row_picks(width).reshape(6 * width, -1),
        seam_col_picks(tile_rows, width), rotated,
    )


def gelu_value(value):
    return 0.5 * value * (1.0 + jax.scipy.special.erf(value * half_root))


def gelu_slope(value):
    return (
        0.5 * (1.0 + jax.scipy.special.erf(value * half_root))
        + value * jnp.exp(-0.5 * value * value) * density_scale
    )


def reduce_stages():
    col_bits = lax.axis_size("fcol").bit_length() - 1
    all_bits = (lax.axis_size("frow") * lax.axis_size("fcol")).bit_length() - 1
    rest = [1 << bit for bit in range(all_bits) if bit != col_bits]
    stages = [(1 << col_bits,)]
    while rest:
        stages.append(tuple(rest[:2]))
        rest = rest[2:]
    return stages


def stage_offsets(stage):
    return (0, stage[0]) if len(stage) == 1 else (0, stage[0], stage[1], stage[0] ^ stage[1])


def stage_place(index, stage):
    place = (index >> (stage[0].bit_length() - 1)) & 1
    if len(stage) == 2:
        place = place + 2 * ((index >> (stage[1].bit_length() - 1)) & 1)
    return place


def fold_sum(terms):
    while len(terms) > 1:
        terms = [terms[i] + terms[i + 1] for i in range(0, len(terms), 2)]
    return terms[0]


def reduce_everywhere(matrix, vector):
    count = lax.axis_size("frow") * lax.axis_size("fcol")
    index = lax.axis_index("frow") * lax.axis_size("fcol") + lax.axis_index("fcol")
    width = matrix.shape[-1]
    pad = jnp.zeros((7, width), jnp.float32)
    vector = jnp.concatenate([vector[None], pad], 0)
    part = matrix.reshape(-1, width)
    stages = reduce_stages()
    for stage in stages:
        offsets = stage_offsets(stage)
        place = stage_place(index, stage)
        part = part.reshape(len(offsets), -1, width).astype(jnp.bfloat16)
        vector = lax.optimization_barrier(vector.astype(jnp.bfloat16))
        rows = part.shape[1]
        sums, vectors = [], []
        for order, offset in enumerate(offsets):
            piece = lax.dynamic_slice_in_dim(part, place ^ order, 1, 0)[0]
            if offset:
                packed = jnp.concatenate([piece, vector], 0)
                packed = lax.ppermute(packed, axes, [(i, i ^ offset) for i in range(count)])
                sums.append(packed[:rows].astype(jnp.float32))
                vectors.append(packed[rows:].astype(jnp.float32))
            else:
                sums.append(piece.astype(jnp.float32))
                vectors.append(vector.astype(jnp.float32))
        part = fold_sum(sums)
        vector = fold_sum(vectors)
    part = lax.optimization_barrier(part.astype(jnp.bfloat16))[None]
    for stage in stages[::-1]:
        offsets = stage_offsets(stage)
        place = stage_place(index, stage)
        pieces = [part] + [
            lax.ppermute(part, axes, [(i, i ^ offset) for i in range(count)])
            for offset in offsets[1:]
        ]
        stacked = jnp.stack(pieces, 0)
        part = jnp.concatenate(
            [
                lax.dynamic_index_in_dim(stacked, place ^ order, 0, False)
                for order in range(len(offsets))
            ],
            0,
        )
    return (part.reshape(matrix.shape).astype(jnp.float32), vector[0])


def local(face_input, kernel, convolution_bias, upstream, adjacency):
    face_count, tile_rows, tile_cols, channels = face_input.shape
    table = adjacency.reshape(-1)
    padded_input = pad_field(face_input, table)
    layout = ("NHWC", "HWIO", "NHWC")
    preactivation = (
        lax.conv_general_dilated(
            padded_input,
            kernel,
            (1, 1),
            "VALID",
            rhs_dilation=(DILATION_STEP, DILATION_STEP),
            dimension_numbers=layout,
            preferred_element_type=jnp.float32,
        )
        + convolution_bias
    )
    activation = gelu_value(preactivation).astype(jnp.bfloat16)
    pre_grad = (upstream.astype(jnp.float32) * gelu_slope(preactivation)).astype(jnp.bfloat16)
    tap_list = []
    for a in range(3):
        for b in range(3):
            row, col = a * DILATION_STEP, b * DILATION_STEP
            window = padded_input[:, row : row + tile_rows, col : col + tile_cols]
            tap_list.append(
                lax.dot_general(
                    window,
                    pre_grad,
                    (((0, 1, 2), (0, 1, 2)), ((), ())),
                    preferred_element_type=jnp.float32,
                )
            )
    kernel_local = jnp.stack(tap_list, 0).reshape(kernel.shape)
    bias_local = jnp.sum(pre_grad.astype(jnp.float32), axis=(0, 1, 2))
    kernel_total, bias_total = reduce_everywhere(kernel_local, bias_local)
    scale = 1.0 / math.sqrt(
        face_count * tile_rows * lax.axis_size("frow") * tile_cols * lax.axis_size("fcol")
    )
    kernel_grad = kernel_total * scale
    bias_grad = bias_total * scale
    rotated = jnp.transpose(jnp.flip(kernel, (0, 1)), (0, 1, 3, 2))
    padded_grad, extra = return_field(pre_grad, table, rotated)
    input_gradient = (
        lax.conv_general_dilated(
            padded_grad,
            rotated,
            (1, 1),
            "VALID",
            rhs_dilation=(DILATION_STEP, DILATION_STEP),
            dimension_numbers=layout,
            preferred_element_type=jnp.float32,
        )
        + extra
    ).astype(jnp.bfloat16)
    return (activation, input_gradient, kernel_grad, bias_grad)


def solution(mesh):
    return jax.shard_map(
        local,
        mesh=mesh,
        in_specs=(P(None, "frow", "fcol", None), P(), P(), P(None, "frow", "fcol", None), P()),
        out_specs=(P(None, "frow", "fcol", None), P(None, "frow", "fcol", None), P(), P()),
        check_vma=False,
    )
```

```python
import functools
import math

import jax
import jax.numpy as jnp
import numpy as np
from jax import lax
from jax.experimental import pallas as pl
from jax.experimental.pallas import tpu as pltpu
from jax.sharding import PartitionSpec as P

DILATION_STEP = 2


half_root = 0.7071067811865476
density_scale = 0.3989422804014327
axes = ("frow", "fcol")
vmem_bytes = 12 * 1024 * 1024


def shifted_pairs(row_step, col_step):
    rows, cols = lax.axis_size("frow"), lax.axis_size("fcol")
    return [
        (r * cols + c, (r + row_step) % rows * cols + (c + col_step) % cols)
        for r in range(rows)
        for c in range(cols)
    ]


def mirror_pairs(edge_rows, flip_rows, flip_cols):
    rows, cols = lax.axis_size("frow"), lax.axis_size("fcol")
    pairs = []
    for r in range(rows):
        for c in range(cols):
            on_edge = r in (0, rows - 1) if edge_rows else c in (0, cols - 1)
            if on_edge:
                target_row = rows - 1 - r if flip_rows else r
                target_col = cols - 1 - c if flip_cols else c
                pairs.append((r * cols + c, target_row * cols + target_col))
    return pairs


def round_up(value, step):
    return -(-value // step) * step


def row_flips(width):
    size = 2 * width + 8
    table = np.zeros((4, size, size), np.float32)
    for kind in range(4):
        for d in range(2):
            source_d = 1 - d if kind % 2 else d
            for p in range(width):
                source_p = width - 1 - p if kind >= 2 else p
                table[kind, d * width + p, source_d * width + source_p] = 1
            for e in range(4):
                source_e = 3 - e if kind >= 2 else e
                table[kind, 2 * width + 4 * d + e, 2 * width + 4 * source_d + source_e] = 1
    return jnp.asarray(table, jnp.bfloat16)


def corner_picks(width):
    table = np.zeros((2, 8, 2 * width), np.float32)
    for d in range(2):
        for k in range(2):
            table[0, 4 * d + 2 + k, d * width + k] = 1
            table[1, 4 * d + k, d * width + width - 2 + k] = 1
    return jnp.asarray(table, jnp.bfloat16)


def stack_places(tile_rows, width):
    strip = round_up(2 * width + 8, 16)
    beside = tile_rows * width
    above = beside + 4 * tile_rows
    below = above + strip
    return (beside, above, below, round_up(below + strip, 128))


def stack_row(tile_rows, width, q, w):
    beside, above, below, _ = stack_places(tile_rows, width)
    side_cell = w if w < 2 else w - width
    inner = 2 <= w < width + 2
    if 2 <= q < tile_rows + 2:
        y = q - 2
        if inner:
            return y * width + w - 2
        return beside + 2 * tile_rows * (side_cell // 2) + 2 * y + side_cell % 2
    base, d = (above, q) if q < 2 else (below, q - tile_rows - 2)
    return base + (d * width + w - 2 if inner else 2 * width + 4 * d + side_cell)


def pad_picks(tile_rows, width):
    breadth = round_up(width + 4, 8)
    size = stack_places(tile_rows, width)[3]
    table = np.zeros(((tile_rows + 4) * breadth, size), np.float32)
    for q in range(tile_rows + 4):
        for w in range(width + 4):
            table[q * breadth + w, stack_row(tile_rows, width, q, w)] = 1
    return jnp.asarray(table, jnp.bfloat16)


def pick(table, value):
    return jnp.dot(table, value, preferred_element_type=jnp.float32).astype(jnp.bfloat16)


def seam_of(adjacency, face, side):
    base = (face * 4 + side) * 3
    near = (adjacency[base + 1] == side).astype(jnp.int32)
    return adjacency[base], 2 * adjacency[base + 2] + near


def one_hot(source, size):
    columns = lax.broadcasted_iota(jnp.int32, (source.shape[0], size), 1)
    return jnp.where(source == columns, 1.0, 0.0).astype(jnp.bfloat16)


def col_flip(kind, tile_rows):
    size = 2 * tile_rows
    row = lax.broadcasted_iota(jnp.int32, (size, size), 0)
    if kind >= 2:
        row = 2 * (tile_rows - 1 - (row >> 1)) + (row & 1)
    return one_hot(row ^ 1 if kind % 2 else row, size)


def tail_pick(first, tile_rows):
    row = lax.broadcasted_iota(jnp.int32, (8, 4 * tile_rows), 0)
    place = 2 * tile_rows * ((row >> 1) & 1) + 2 * (first + (row >> 2)) + (row & 1)
    return one_hot(place, 4 * tile_rows)


def side_kernel(
    adjacency, edges, beside, far_same, far_cross, side_out, upper_out, lower_out, seam
):
    face_count, both_sides, channels = edges.shape
    tile_rows = both_sides // 4
    half = 2 * tile_rows
    row_place, col_place = lax.axis_index("frow"), lax.axis_index("fcol")
    at_top = row_place == 0
    at_bottom = row_place == lax.axis_size("frow") - 1
    at_left = col_place == 0
    at_right = col_place == lax.axis_size("fcol") - 1

    @pl.when(jnp.logical_or(at_left, at_right))
    def _():
        @pl.loop(0, face_count)
        def _(face):
            source, kind = seam_of(adjacency, face, jnp.where(at_left, 2, 3))

            @pl.when(kind == 0)
            def _():
                both = beside[source]
                seam[face] = jnp.where(at_left, both[half:], both[:half])

            @pl.when(kind == 1)
            def _():
                both = edges[source]
                own = jnp.where(at_left, both[:half], both[half:])
                seam[face] = pick(col_flip(1, tile_rows), own)

            @pl.when(kind == 2)
            def _():
                seam[face] = pick(col_flip(2, tile_rows), far_cross[source])

            @pl.when(kind == 3)
            def _():
                seam[face] = pick(col_flip(3, tile_rows), far_same[source])

    upper_pick = tail_pick(0, tile_rows)
    lower_pick = tail_pick(tile_rows - 2, tile_rows)
    for face in range(face_count):
        both = beside[face]
        left = jnp.where(at_left, seam[face], both[half:])
        right = jnp.where(at_right, seam[face], both[:half])
        sides = jnp.concatenate([left, right], 0)
        side_out[face] = sides
        blank = jnp.zeros_like(left)
        inner = jnp.concatenate(
            [jnp.where(at_left, blank, left), jnp.where(at_right, blank, right)], 0
        )
        upper_out[face] = pick(upper_pick, jnp.where(at_top, inner, sides))
        lower_out[face] = pick(lower_pick, jnp.where(at_bottom, inner, sides))


def col_kernel(
    adjacency, field, edges, beside, far_same, far_cross, side_out, top_out, bottom_out, edge_out,
    upper, lower, seam,
):
    face_count, tile_rows, width, channels = field.shape
    at_top = lax.axis_index("frow") == 0
    side_kernel(adjacency, edges, beside, far_same, far_cross, side_out, upper, lower, seam)
    for face in range(face_count):
        for d in range(2):
            rows = pl.ds(d * width, width)
            first, last = field[face, d], field[face, tile_rows - 2 + d]
            top_out[face, rows] = first
            bottom_out[face, rows] = last
            edge_out[face, rows] = jnp.where(at_top, first, last)
        rows = pl.ds(2 * width, 8)
        top_out[face, rows] = upper[face]
        bottom_out[face, rows] = lower[face]
        edge_out[face, rows] = jnp.where(at_top, upper[face], lower[face])


def joint_readers(up, down, edge, far_same, far_cross):
    def reader(ref):
        return lambda source: ref[source]

    return [[reader(ref) for ref in (near, edge, far_cross, far_same)] for near in (up, down)]


def split_readers(
    upper, lower, up, down, up_tail, down_tail, edge, far_same, far_cross, corners,
    same_tail=None, cross_tail=None,
):
    def reader(main, tail):
        return lambda source: jnp.concatenate([main[source], tail[source]], 0)

    def corner_reader(main, other):
        def read(source):
            tail = pick(corners[1 - lax.axis_index("fcol")], other[source])
            return jnp.concatenate([main[source], tail], 0)

        return read

    readers = []
    for near, near_tail, own_tail in ((up, up_tail, upper), (down, down_tail, lower)):
        readers.append([reader(near, near_tail), reader(edge, own_tail)])
        if same_tail is None:
            readers[-1] += [corner_reader(far_cross, near), corner_reader(far_same, edge)]
        else:
            readers[-1] += [reader(far_cross, cross_tail), reader(far_same, same_tail)]
    return readers


def load_stack(adjacency, face, field, sides, readers, flips, stack):
    tile_rows, width, channels = field.shape[1:]
    strip = 2 * width + 8
    beside, above, below, _ = stack_places(tile_rows, width)
    row_place = lax.axis_index("frow")
    stack[face, pl.ds(0, beside)] = field[face].reshape(beside, channels)
    stack[face, pl.ds(beside, 4 * tile_rows)] = sides[face]
    for side, place in ((0, above), (1, below)):
        at_edge = row_place == side * (lax.axis_size("frow") - 1)
        rows = pl.ds(place, strip)

        @pl.when(jnp.logical_not(at_edge))
        def _():
            stack[face, rows] = readers[side][0](face)

        source, kind = seam_of(adjacency, face, side)
        for choice, read in enumerate(readers[side]):

            @pl.when(jnp.logical_and(at_edge, kind == choice))
            def _():
                stack[face, rows] = pick(flips[choice], read(source))


def write_padded(picks, stack, padded):
    face_count, rows, breadth, channels = padded.shape
    step = picks.shape[0] // rows
    for face in range(face_count):
        out = pick(picks[...], stack[face])
        for q in range(rows):
            padded[face, q] = out[q * step : q * step + breadth]


def pad_kernel(adjacency, flips, picks, field, sides, *refs):
    padded, stack = refs[-2:]
    readers = split_readers(*refs[:-2])
    stack[...] = jnp.zeros_like(stack)

    @pl.loop(0, field.shape[0])
    def _(face):
        load_stack(adjacency, face, field, sides, readers, flips, stack)

    write_padded(picks, stack, padded)


def whole(count):
    return [pl.BlockSpec(memory_space=pltpu.SMEM)] + [
        pl.BlockSpec(memory_space=pltpu.VMEM) for _ in range(count)
    ]


def exchange_cols(field):
    face_count, tile_rows, width, channels = field.shape
    left = field[:, :, :2].reshape(face_count, 2 * tile_rows, channels)
    right = field[:, :, width - 2 :].reshape(face_count, 2 * tile_rows, channels)
    edges = jnp.concatenate([left, right], 1)
    if lax.axis_size("fcol") == 2:
        beside = lax.ppermute(edges, axes, shifted_pairs(0, 1))
    else:
        beside = jnp.concatenate(
            [
                lax.ppermute(left, axes, shifted_pairs(0, -1)),
                lax.ppermute(right, axes, shifted_pairs(0, 1)),
            ],
            1,
        )
    edge = jnp.where(lax.axis_index("fcol") == 0, left, right)
    far_same = lax.ppermute(edge, axes, mirror_pairs(False, True, False))
    far_cross = lax.ppermute(edge, axes, mirror_pairs(False, True, True))
    return (edges, beside, far_same, far_cross)


def exchange_rows(top, bottom, edge):
    up = lax.ppermute(bottom, axes, shifted_pairs(1, 0))
    down = lax.ppermute(top, axes, shifted_pairs(-1, 0))
    if edge is None:
        return (up, down)
    row_same = lax.ppermute(edge, axes, mirror_pairs(True, False, True))
    row_cross = lax.ppermute(edge, axes, mirror_pairs(True, True, True))
    return (up, down, row_same, row_cross)


def side_call(body, field, inputs, outputs, scratch):
    face_count, tile_rows, _, channels = field.shape
    scratch = [*scratch, (face_count, 2 * tile_rows, channels)]
    return pl.pallas_call(
        body,
        out_shape=[jax.ShapeDtypeStruct(shape, field.dtype) for shape in outputs],
        in_specs=whole(len(inputs) - 1),
        out_specs=[pl.BlockSpec(memory_space=pltpu.VMEM) for _ in outputs],
        scratch_shapes=[pltpu.VMEM(shape, field.dtype) for shape in scratch],
        compiler_params=pltpu.CompilerParams(vmem_limit_bytes=vmem_bytes),
        cost_estimate=pl.CostEstimate(flops=1000, bytes_accessed=3000000, transcendentals=0),
    )(*inputs)


def joint_strips(field, adjacency):
    face_count, tile_rows, width, channels = field.shape
    cols = exchange_cols(field)
    strip = (face_count, 2 * width + 8, channels)
    tail = (face_count, 8, channels)
    sides, top, bottom, edge = side_call(
        col_kernel,
        field,
        (adjacency, field, *cols),
        (cols[0].shape, strip, strip, strip),
        (tail, tail),
    )
    up, down, row_same, row_cross = exchange_rows(top, bottom, edge)
    return (field, sides, up, down, edge, row_same, row_cross)


def split_strips(field, adjacency):
    face_count, tile_rows, width, channels = field.shape
    edges, beside, far_same, far_cross = exchange_cols(field)
    at_top = lax.axis_index("frow") == 0
    later, beside, far_same, far_cross = lax.optimization_barrier(
        (field, beside, far_same, far_cross)
    )
    top = later[:, :2].reshape(face_count, 2 * width, channels)
    bottom = later[:, tile_rows - 2 :].reshape(face_count, 2 * width, channels)
    edge = jnp.where(at_top, top, bottom)
    up, down, row_same, row_cross = exchange_rows(top, bottom, edge)
    tail = (face_count, 8, channels)
    sides, upper, lower = side_call(
        side_kernel,
        field,
        (adjacency, edges, beside, far_same, far_cross),
        (edges.shape, tail, tail),
        (),
    )
    up_tail, down_tail = exchange_rows(upper, lower, None)
    strips = [
        field, sides, upper, lower, up, down, up_tail, down_tail, edge, row_same, row_cross,
        corner_picks(width),
    ]
    if lax.axis_size("fcol") > 2:
        own_tail = jnp.where(at_top, upper, lower)
        strips += exchange_rows(upper, lower, own_tail)[2:]
    return strips


def pad_field(field, adjacency):
    face_count, tile_rows, width, channels = field.shape
    strips = split_strips(field, adjacency)
    padded = (face_count, tile_rows + 4, width + 4, channels)
    size = stack_places(tile_rows, width)[3]
    return pl.pallas_call(
        pad_kernel,
        out_shape=jax.ShapeDtypeStruct(padded, field.dtype),
        in_specs=whole(len(strips) + 2),
        out_specs=pl.BlockSpec(memory_space=pltpu.VMEM),
        scratch_shapes=[pltpu.VMEM((face_count, size, channels), field.dtype)],
        compiler_params=pltpu.CompilerParams(vmem_limit_bytes=vmem_bytes),
        cost_estimate=pl.CostEstimate(flops=1000, bytes_accessed=5000000, transcendentals=0),
    )(adjacency, row_flips(width), pad_picks(tile_rows, width), *strips)


def seam_row_picks(width):
    size = round_up(2 * width + 8, 16)
    table = np.zeros((3, 2 * width, size), np.float32)
    for shift in range(3):
        for d in range(2):
            for x in range(width):
                w = x + 2 * shift
                if 2 <= w < width + 2:
                    source = d * width + w - 2
                else:
                    source = 2 * width + 4 * d + (w if w < 2 else w - width)
                table[shift, d * width + x, source] = 1
    return jnp.asarray(table, jnp.bfloat16)


def seam_col_picks(tile_rows, width):
    size = stack_places(tile_rows, width)[3]
    table = np.zeros((2, 3 * 2 * tile_rows, size), np.float32)
    for right in range(2):
        for shift in range(3):
            for y in range(tile_rows):
                for k in range(2):
                    w = width + 2 + k if right else k
                    table[
                        right,
                        (shift * tile_rows + y) * 2 + k,
                        stack_row(tile_rows, width, y + 2 * shift, w),
                    ] = 1
    return jnp.asarray(table, jnp.bfloat16)


def return_kernel(
    adjacency, flips, picks, row_picks, col_picks, rotated, field, sides, up, down, edge,
    far_same, far_cross, padded, extra, stack, kept_picks, row_terms, col_terms, col_sum,
):
    readers = joint_readers(up, down, edge, far_same, far_cross)
    face_count, tile_rows, width, channels = field.shape
    breadth = picks.shape[0] // (tile_rows + 4)
    half = 2 * tile_rows
    slot = round_up(half, 16)
    row_slot = 2 * width
    _, above, below, _ = stack_places(tile_rows, width)
    strip = row_picks.shape[1]
    row_place, col_place = lax.axis_index("frow"), lax.axis_index("fcol")
    at_top = row_place == 0
    at_bottom = row_place == lax.axis_size("frow") - 1
    at_left = col_place == 0
    at_right = col_place == lax.axis_size("fcol") - 1
    on_row_edge = jnp.logical_or(at_top, at_bottom)
    on_col_edge = jnp.logical_or(at_left, at_right)
    stack[...] = jnp.zeros_like(stack)
    extra[...] = jnp.zeros_like(extra)
    cell = lax.broadcasted_iota(jnp.int32, (breadth, picks.shape[1]), 0)
    for q in range(tile_rows + 4):
        rows = pl.ds(q * breadth, breadth)
        dropped = jnp.logical_or(
            jnp.logical_and(at_left, cell < 2), jnp.logical_and(at_right, cell >= width + 2)
        )
        if q < 2:
            dropped = jnp.logical_or(dropped, at_top)
        if q >= tile_rows + 2:
            dropped = jnp.logical_or(dropped, at_bottom)
        kept = jnp.where(dropped, 0.0, picks[rows].astype(jnp.float32))
        kept_picks[rows] = kept.astype(jnp.bfloat16)

    @pl.loop(0, face_count)
    def _(face):
        load_stack(adjacency, face, field, sides, readers, flips, stack)

    write_padded(kept_picks, stack, padded)

    @pl.when(on_col_edge)
    def _():
        col_terms[...] = jnp.zeros_like(col_terms)
        table = col_picks[jnp.where(at_left, 0, 1)]

        @pl.loop(0, face_count)
        def _(face):
            base = (face * 4 + jnp.where(at_left, 2, 3)) * 3
            turned = adjacency[base + 2]
            value = jnp.dot(table, stack[face], preferred_element_type=jnp.float32)
            rows = pl.ds(pl.multiple_of(face * slot, 16), half)
            for shift in range(3):
                part = value[shift * half : (shift + 1) * half].astype(jnp.bfloat16)
                tap = jnp.where(turned == 1, 2 - shift, shift)
                col_terms[adjacency[base + 1] - 2, tap, rows] = part

        total = jnp.zeros(col_sum.shape, jnp.float32)
        for side in range(2):
            for tap in range(3):
                total += jnp.dot(
                    col_terms[side, tap],
                    rotated[tap, 2 - 2 * side],
                    preferred_element_type=jnp.float32,
                )
        col_sum[...] = total

    @pl.when(on_row_edge)
    def _():
        row_terms[...] = jnp.zeros_like(row_terms)

        @pl.loop(0, face_count)
        def _(face):
            base = (face * 4 + jnp.where(at_top, 0, 1)) * 3
            turned = adjacency[base + 2]
            place = pl.multiple_of(jnp.where(at_top, above, below), 16)
            value = pick(row_picks[...], stack[face, pl.ds(place, strip)])
            rows = pl.ds(pl.multiple_of(face * row_slot, 16), row_slot)
            for shift in range(3):
                part = value[shift * row_slot : (shift + 1) * row_slot]
                tap = jnp.where(turned == 1, 2 - shift, shift)
                row_terms[adjacency[base + 1], tap, rows] = part

        first = jnp.where(at_top, 0, tile_rows - 2)

        group = math.gcd(face_count, 4)

        @pl.loop(0, face_count // group)
        def _(part):
            size = group * row_slot
            rows = pl.ds(pl.multiple_of(part * size, 16), size)
            total = jnp.zeros((size, channels), jnp.float32)
            for side in range(2):
                for tap in range(3):
                    total += jnp.dot(
                        row_terms[side, tap, rows],
                        rotated[2 - 2 * side, tap],
                        preferred_element_type=jnp.float32,
                    )
            for face in range(group):
                for d in range(2):
                    start = face * row_slot + d * width
                    extra[part * group + face, first + d] = total[start : start + width]

    for edge_col, at_edge in ((0, at_left), (width - 2, at_right)):

        @pl.when(at_edge)
        def _():
            cells = pl.ds(edge_col, 2)
            for face in range(face_count):
                value = col_sum[pl.ds(face * slot, half)]
                for y in range(tile_rows):
                    extra[face, y, cells] = extra[face, y, cells] + value[2 * y : 2 * y + 2]


def return_field(field, adjacency, rotated):
    face_count, tile_rows, width, channels = field.shape
    strips = joint_strips(field, adjacency)
    padded = (face_count, tile_rows + 4, width + 4, channels)
    size = stack_places(tile_rows, width)[3]
    picks = pad_picks(tile_rows, width)
    cells = face_count * round_up(2 * tile_rows, 16)
    return pl.pallas_call(
        return_kernel,
        out_shape=(
            jax.ShapeDtypeStruct(padded, field.dtype),
            jax.ShapeDtypeStruct(field.shape, jnp.float32),
        ),
        in_specs=whole(len(strips) + 5),
        out_specs=[pl.BlockSpec(memory_space=pltpu.VMEM)] * 2,
        scratch_shapes=[
            pltpu.VMEM((face_count, size, channels), field.dtype),
            pltpu.VMEM(picks.shape, field.dtype),
            pltpu.VMEM((2, 3, face_count * 2 * width, channels), field.dtype),
            pltpu.VMEM((2, 3, cells, channels), field.dtype),
            pltpu.VMEM((cells, channels), jnp.float32),
        ],
        compiler_params=pltpu.CompilerParams(vmem_limit_bytes=vmem_bytes),
        cost_estimate=pl.CostEstimate(flops=1000, bytes_accessed=8000000, transcendentals=0),
    )(
        adjacency, row_flips(width), picks,
        seam_row_picks(width).reshape(6 * width, -1),
        seam_col_picks(tile_rows, width), rotated, *strips,
    )


def gelu_value(value):
    return 0.5 * value * (1.0 + jax.scipy.special.erf(value * half_root))


def gelu_slope(value):
    return (
        0.5 * (1.0 + jax.scipy.special.erf(value * half_root))
        + value * jnp.exp(-0.5 * value * value) * density_scale
    )


def reduce_stages():
    col_bits = lax.axis_size("fcol").bit_length() - 1
    all_bits = (lax.axis_size("frow") * lax.axis_size("fcol")).bit_length() - 1
    rest = [1 << bit for bit in range(all_bits) if bit != col_bits]
    stages = [(1 << col_bits,)]
    while rest:
        stages.append(tuple(rest[:2]))
        rest = rest[2:]
    return stages


def stage_offsets(stage):
    return (0, stage[0]) if len(stage) == 1 else (0, stage[0], stage[1], stage[0] ^ stage[1])


def stage_place(index, stage):
    place = (index >> (stage[0].bit_length() - 1)) & 1
    if len(stage) == 2:
        place = place + 2 * ((index >> (stage[1].bit_length() - 1)) & 1)
    return place


def fold_sum(terms):
    while len(terms) > 1:
        terms = [terms[i] + terms[i + 1] for i in range(0, len(terms), 2)]
    return terms[0]


def reduce_everywhere(matrix, vector):
    count = lax.axis_size("frow") * lax.axis_size("fcol")
    index = lax.axis_index("frow") * lax.axis_size("fcol") + lax.axis_index("fcol")
    width = matrix.shape[-1]
    pad = jnp.zeros((7, width), jnp.float32)
    vector = jnp.concatenate([vector[None], pad], 0)
    part = matrix.reshape(-1, width)
    stages = reduce_stages()
    for stage in stages:
        offsets = stage_offsets(stage)
        place = stage_place(index, stage)
        part = part.reshape(len(offsets), -1, width).astype(jnp.bfloat16)
        vector = lax.optimization_barrier(vector.astype(jnp.bfloat16))
        rows = part.shape[1]
        sums, vectors = [], []
        for order, offset in enumerate(offsets):
            piece = lax.dynamic_slice_in_dim(part, place ^ order, 1, 0)[0]
            if offset:
                packed = jnp.concatenate([piece, vector], 0)
                packed = lax.ppermute(packed, axes, [(i, i ^ offset) for i in range(count)])
                sums.append(packed[:rows].astype(jnp.float32))
                vectors.append(packed[rows:].astype(jnp.float32))
            else:
                sums.append(piece.astype(jnp.float32))
                vectors.append(vector.astype(jnp.float32))
        part = fold_sum(sums)
        vector = fold_sum(vectors)
    part = lax.optimization_barrier(part.astype(jnp.bfloat16))[None]
    for stage in stages[::-1]:
        offsets = stage_offsets(stage)
        place = stage_place(index, stage)
        pieces = [part] + [
            lax.ppermute(part, axes, [(i, i ^ offset) for i in range(count)])
            for offset in offsets[1:]
        ]
        stacked = jnp.stack(pieces, 0)
        part = jnp.concatenate(
            [
                lax.dynamic_index_in_dim(stacked, place ^ order, 0, False)
                for order in range(len(offsets))
            ],
            0,
        )
    return (part.reshape(matrix.shape).astype(jnp.float32), vector[0])


def local(face_input, kernel, convolution_bias, upstream, adjacency):
    face_count, tile_rows, tile_cols, channels = face_input.shape
    table = adjacency.reshape(-1)
    padded_input = pad_field(face_input, table)
    layout = ("NHWC", "HWIO", "NHWC")
    preactivation = (
        lax.conv_general_dilated(
            padded_input,
            kernel,
            (1, 1),
            "VALID",
            rhs_dilation=(DILATION_STEP, DILATION_STEP),
            dimension_numbers=layout,
            preferred_element_type=jnp.float32,
        )
        + convolution_bias
    )
    activation = gelu_value(preactivation).astype(jnp.bfloat16)
    pre_grad = (upstream.astype(jnp.float32) * gelu_slope(preactivation)).astype(jnp.bfloat16)
    tap_list = []
    for a in range(3):
        for b in range(3):
            row, col = a * DILATION_STEP, b * DILATION_STEP
            window = padded_input[:, row : row + tile_rows, col : col + tile_cols]
            tap_list.append(
                lax.dot_general(
                    window,
                    pre_grad,
                    (((0, 1, 2), (0, 1, 2)), ((), ())),
                    preferred_element_type=jnp.float32,
                )
            )
    kernel_local = jnp.stack(tap_list, 0).reshape(kernel.shape)
    bias_local = jnp.sum(pre_grad.astype(jnp.float32), axis=(0, 1, 2))
    kernel_total, bias_total = reduce_everywhere(kernel_local, bias_local)
    scale = 1.0 / math.sqrt(
        face_count * tile_rows * lax.axis_size("frow") * tile_cols * lax.axis_size("fcol")
    )
    kernel_grad = kernel_total * scale
    bias_grad = bias_total * scale
    rotated = jnp.transpose(jnp.flip(kernel, (0, 1)), (0, 1, 3, 2))
    padded_grad, extra = return_field(pre_grad, table, rotated)
    input_gradient = (
        lax.conv_general_dilated(
            padded_grad,
            rotated,
            (1, 1),
            "VALID",
            rhs_dilation=(DILATION_STEP, DILATION_STEP),
            dimension_numbers=layout,
            preferred_element_type=jnp.float32,
        )
        + extra
    ).astype(jnp.bfloat16)
    return (activation, input_gradient, kernel_grad, bias_grad)


def solution(mesh):
    return jax.shard_map(
        local,
        mesh=mesh,
        in_specs=(P(None, "frow", "fcol", None), P(), P(), P(None, "frow", "fcol", None), P()),
        out_specs=(P(None, "frow", "fcol", None), P(None, "frow", "fcol", None), P(), P()),
        check_vma=False,
    )
```

```python
import functools
import math

import jax
import jax.numpy as jnp
import numpy as np
from jax import lax
from jax.experimental import pallas as pl
from jax.experimental.pallas import tpu as pltpu
from jax.sharding import PartitionSpec as P

DILATION_STEP = 2


half_root = 0.7071067811865476
density_scale = 0.3989422804014327
axes = ("frow", "fcol")
vmem_bytes = 12 * 1024 * 1024


def shifted_pairs(row_step, col_step):
    rows, cols = lax.axis_size("frow"), lax.axis_size("fcol")
    return [
        (r * cols + c, (r + row_step) % rows * cols + (c + col_step) % cols)
        for r in range(rows)
        for c in range(cols)
    ]


def mirror_pairs(edge_rows, flip_rows, flip_cols):
    rows, cols = lax.axis_size("frow"), lax.axis_size("fcol")
    pairs = []
    for r in range(rows):
        for c in range(cols):
            on_edge = r in (0, rows - 1) if edge_rows else c in (0, cols - 1)
            if on_edge:
                target_row = rows - 1 - r if flip_rows else r
                target_col = cols - 1 - c if flip_cols else c
                pairs.append((r * cols + c, target_row * cols + target_col))
    return pairs


def round_up(value, step):
    return -(-value // step) * step


def flip_table(width):
    size = 2 * width + 8
    table = np.zeros((4, size, size), np.float32)
    for kind in range(4):
        for d in range(2):
            source_d = 1 - d if kind % 2 else d
            for p in range(width):
                source_p = width - 1 - p if kind >= 2 else p
                table[kind, d * width + p, source_d * width + source_p] = 1
            for e in range(4):
                source_e = 3 - e if kind >= 2 else e
                table[kind, 2 * width + 4 * d + e, 2 * width + 4 * source_d + source_e] = 1
    return table


def row_flips(width):
    return jnp.asarray(flip_table(width), jnp.bfloat16)


def stack_places(tile_rows, width):
    strip = round_up(2 * width + 8, 16)
    beside = tile_rows * width
    above = beside + 4 * tile_rows
    below = above + strip
    return (beside, above, below, round_up(below + strip, 128))


def stack_row(tile_rows, width, q, w):
    beside, above, below, _ = stack_places(tile_rows, width)
    side_cell = w if w < 2 else w - width
    inner = 2 <= w < width + 2
    if 2 <= q < tile_rows + 2:
        y = q - 2
        if inner:
            return y * width + w - 2
        return beside + 2 * tile_rows * (side_cell // 2) + 2 * y + side_cell % 2
    base, d = (above, q) if q < 2 else (below, q - tile_rows - 2)
    return base + (d * width + w - 2 if inner else 2 * width + 4 * d + side_cell)


def pad_picks(tile_rows, width):
    breadth = round_up(width + 4, 8)
    size = stack_places(tile_rows, width)[3]
    table = np.zeros(((tile_rows + 4) * breadth, size), np.float32)
    for q in range(tile_rows + 4):
        for w in range(width + 4):
            table[q * breadth + w, stack_row(tile_rows, width, q, w)] = 1
    return jnp.asarray(table, jnp.bfloat16)


def pick(table, value):
    return jnp.dot(table, value, preferred_element_type=jnp.float32).astype(jnp.bfloat16)


def seam_of(adjacency, face, side):
    base = (face * 4 + side) * 3
    near = (adjacency[base + 1] == side).astype(jnp.int32)
    return adjacency[base], 2 * adjacency[base + 2] + near


def one_hot(source, size):
    columns = lax.broadcasted_iota(jnp.int32, (source.shape[0], size), 1)
    return jnp.where(source == columns, 1.0, 0.0).astype(jnp.bfloat16)


def col_flip(kind, tile_rows):
    size = 2 * tile_rows
    row = lax.broadcasted_iota(jnp.int32, (size, size), 0)
    if kind >= 2:
        row = 2 * (tile_rows - 1 - (row >> 1)) + (row & 1)
    return one_hot(row ^ 1 if kind % 2 else row, size)


def tail_pick(first, tile_rows):
    row = lax.broadcasted_iota(jnp.int32, (8, 4 * tile_rows), 0)
    place = 2 * tile_rows * ((row >> 1) & 1) + 2 * (first + (row >> 2)) + (row & 1)
    return one_hot(place, 4 * tile_rows)


def side_kernel(
    adjacency, edges, beside, far_same, far_cross, side_out, upper_out, lower_out, seam
):
    face_count, both_sides, channels = edges.shape
    tile_rows = both_sides // 4
    half = 2 * tile_rows
    row_place, col_place = lax.axis_index("frow"), lax.axis_index("fcol")
    at_top = row_place == 0
    at_bottom = row_place == lax.axis_size("frow") - 1
    at_left = col_place == 0
    at_right = col_place == lax.axis_size("fcol") - 1

    @pl.when(jnp.logical_or(at_left, at_right))
    def _():
        @pl.loop(0, face_count)
        def _(face):
            source, kind = seam_of(adjacency, face, jnp.where(at_left, 2, 3))

            @pl.when(kind == 0)
            def _():
                both = beside[source]
                seam[face] = jnp.where(at_left, both[half:], both[:half])

            @pl.when(kind == 1)
            def _():
                both = edges[source]
                own = jnp.where(at_left, both[:half], both[half:])
                seam[face] = pick(col_flip(1, tile_rows), own)

            @pl.when(kind == 2)
            def _():
                seam[face] = pick(col_flip(2, tile_rows), far_cross[source])

            @pl.when(kind == 3)
            def _():
                seam[face] = pick(col_flip(3, tile_rows), far_same[source])

    upper_pick = tail_pick(0, tile_rows)
    lower_pick = tail_pick(tile_rows - 2, tile_rows)
    for face in range(face_count):
        both = beside[face]
        left = jnp.where(at_left, seam[face], both[half:])
        right = jnp.where(at_right, seam[face], both[:half])
        sides = jnp.concatenate([left, right], 0)
        side_out[face] = sides
        blank = jnp.zeros_like(left)
        inner = jnp.concatenate(
            [jnp.where(at_left, blank, left), jnp.where(at_right, blank, right)], 0
        )
        upper_out[face] = pick(upper_pick, jnp.where(at_top, inner, sides))
        lower_out[face] = pick(lower_pick, jnp.where(at_bottom, inner, sides))


def col_kernel(
    adjacency, field, edges, beside, far_same, far_cross, side_out, top_out, bottom_out, edge_out,
    upper, lower, seam,
):
    face_count, tile_rows, width, channels = field.shape
    at_top = lax.axis_index("frow") == 0
    side_kernel(adjacency, edges, beside, far_same, far_cross, side_out, upper, lower, seam)
    for face in range(face_count):
        for d in range(2):
            rows = pl.ds(d * width, width)
            first, last = field[face, d], field[face, tile_rows - 2 + d]
            top_out[face, rows] = first
            bottom_out[face, rows] = last
            edge_out[face, rows] = jnp.where(at_top, first, last)
        rows = pl.ds(2 * width, 8)
        top_out[face, rows] = upper[face]
        bottom_out[face, rows] = lower[face]
        edge_out[face, rows] = jnp.where(at_top, upper[face], lower[face])


def joint_readers(up, down, edge, far_same, far_cross):
    def reader(ref):
        return lambda source: ref[source]

    return [[reader(ref) for ref in (near, edge, far_cross, far_same)] for near in (up, down)]


def load_stack(adjacency, face, field, sides, readers, flips, stack):
    tile_rows, width, channels = field.shape[1:]
    strip = 2 * width + 8
    beside, above, below, _ = stack_places(tile_rows, width)
    row_place = lax.axis_index("frow")
    stack[face, pl.ds(0, beside)] = field[face].reshape(beside, channels)
    stack[face, pl.ds(beside, 4 * tile_rows)] = sides[face]
    for side, place in ((0, above), (1, below)):
        at_edge = row_place == side * (lax.axis_size("frow") - 1)
        rows = pl.ds(place, strip)

        @pl.when(jnp.logical_not(at_edge))
        def _():
            stack[face, rows] = readers[side][0](face)

        source, kind = seam_of(adjacency, face, side)
        for choice, read in enumerate(readers[side]):

            @pl.when(jnp.logical_and(at_edge, kind == choice))
            def _():
                stack[face, rows] = pick(flips[choice], read(source))


def write_padded(picks, stack, padded):
    face_count, rows, breadth, channels = padded.shape
    step = picks.shape[0] // rows
    for face in range(face_count):
        out = pick(picks[...], stack[face])
        for q in range(rows):
            padded[face, q] = out[q * step : q * step + breadth]


def pad_kernel(adjacency, flips, picks, field, sides, *refs):
    padded, stack = refs[-2:]
    readers = joint_readers(*refs[:-2])
    stack[...] = jnp.zeros_like(stack)

    @pl.loop(0, field.shape[0])
    def _(face):
        load_stack(adjacency, face, field, sides, readers, flips, stack)

    write_padded(picks, stack, padded)


def whole(count):
    return [pl.BlockSpec(memory_space=pltpu.SMEM)] + [
        pl.BlockSpec(memory_space=pltpu.VMEM) for _ in range(count)
    ]


def exchange_cols(field):
    face_count, tile_rows, width, channels = field.shape
    left = field[:, :, :2].reshape(face_count, 2 * tile_rows, channels)
    right = field[:, :, width - 2 :].reshape(face_count, 2 * tile_rows, channels)
    edges = jnp.concatenate([left, right], 1)
    if lax.axis_size("fcol") == 2:
        beside = lax.ppermute(edges, axes, shifted_pairs(0, 1))
    else:
        beside = jnp.concatenate(
            [
                lax.ppermute(left, axes, shifted_pairs(0, -1)),
                lax.ppermute(right, axes, shifted_pairs(0, 1)),
            ],
            1,
        )
    edge = jnp.where(lax.axis_index("fcol") == 0, left, right)
    far_same = lax.ppermute(edge, axes, mirror_pairs(False, True, False))
    far_cross = lax.ppermute(edge, axes, mirror_pairs(False, True, True))
    return (edges, beside, far_same, far_cross)


def exchange_rows(top, bottom, edge):
    up = lax.ppermute(bottom, axes, shifted_pairs(1, 0))
    down = lax.ppermute(top, axes, shifted_pairs(-1, 0))
    row_same = lax.ppermute(edge, axes, mirror_pairs(True, False, True))
    row_cross = lax.ppermute(edge, axes, mirror_pairs(True, True, True))
    return (up, down, row_same, row_cross)


def side_call(body, field, inputs, outputs, scratch):
    face_count, tile_rows, _, channels = field.shape
    scratch = [*scratch, (face_count, 2 * tile_rows, channels)]
    return pl.pallas_call(
        body,
        out_shape=[jax.ShapeDtypeStruct(shape, field.dtype) for shape in outputs],
        in_specs=whole(len(inputs) - 1),
        out_specs=[pl.BlockSpec(memory_space=pltpu.VMEM) for _ in outputs],
        scratch_shapes=[pltpu.VMEM(shape, field.dtype) for shape in scratch],
        compiler_params=pltpu.CompilerParams(vmem_limit_bytes=vmem_bytes),
        cost_estimate=pl.CostEstimate(flops=1000, bytes_accessed=3000000, transcendentals=0),
    )(*inputs)


def joint_strips(field, adjacency):
    face_count, tile_rows, width, channels = field.shape
    cols = exchange_cols(field)
    strip = (face_count, 2 * width + 8, channels)
    tail = (face_count, 8, channels)
    sides, top, bottom, edge = side_call(
        col_kernel,
        field,
        (adjacency, field, *cols),
        (cols[0].shape, strip, strip, strip),
        (tail, tail),
    )
    up, down, row_same, row_cross = exchange_rows(top, bottom, edge)
    return (field, sides, up, down, edge, row_same, row_cross)


def pad_field(field, adjacency):
    face_count, tile_rows, width, channels = field.shape
    strips = joint_strips(field, adjacency)
    padded = (face_count, tile_rows + 4, width + 4, channels)
    size = stack_places(tile_rows, width)[3]
    return pl.pallas_call(
        pad_kernel,
        out_shape=jax.ShapeDtypeStruct(padded, field.dtype),
        in_specs=whole(len(strips) + 2),
        out_specs=pl.BlockSpec(memory_space=pltpu.VMEM),
        scratch_shapes=[pltpu.VMEM((face_count, size, channels), field.dtype)],
        compiler_params=pltpu.CompilerParams(vmem_limit_bytes=vmem_bytes),
        cost_estimate=pl.CostEstimate(flops=1000, bytes_accessed=5000000, transcendentals=0),
    )(adjacency, row_flips(width), pad_picks(tile_rows, width), *strips)


def seam_row_picks(width):
    flips = flip_table(width)
    table = np.zeros((3 * 2 * width, 2 * width + 8), np.float32)
    for shift in range(3):
        for d in range(2):
            for x in range(width):
                w = x + 2 * shift
                if 2 <= w < width + 2:
                    source = d * width + w - 2
                else:
                    source = 2 * width + 4 * d + (w if w < 2 else w - width)
                table[(shift * 2 + d) * width + x, source] = 1
    turned = table.reshape(3, 2 * width, -1)[::-1].reshape(table.shape)
    parts = [(turned if kind >= 2 else table) @ flips[kind] for kind in range(4)]
    return jnp.asarray(np.stack(parts), jnp.bfloat16)


def seam_col_picks(tile_rows, width):
    size = stack_places(tile_rows, width)[3]
    table = np.zeros((2, 3 * 2 * tile_rows, size), np.float32)
    for right in range(2):
        for shift in range(3):
            for y in range(tile_rows):
                for k in range(2):
                    w = width + 2 + k if right else k
                    table[
                        right,
                        (shift * tile_rows + y) * 2 + k,
                        stack_row(tile_rows, width, y + 2 * shift, w),
                    ] = 1
    return jnp.asarray(table, jnp.bfloat16)


def return_kernel(
    adjacency, picks, col_picks, rotated, field, sides, up, down, padded, extra, stack,
    kept_picks, col_terms, col_sum,
):
    face_count, tile_rows, width, channels = field.shape
    breadth = picks.shape[0] // (tile_rows + 4)
    half = 2 * tile_rows
    slot = round_up(half, 16)
    beside, above, below, _ = stack_places(tile_rows, width)
    row_place, col_place = lax.axis_index("frow"), lax.axis_index("fcol")
    at_top = row_place == 0
    at_bottom = row_place == lax.axis_size("frow") - 1
    at_left = col_place == 0
    at_right = col_place == lax.axis_size("fcol") - 1
    stack[...] = jnp.zeros_like(stack)
    extra[...] = jnp.zeros_like(extra)
    cell = lax.broadcasted_iota(jnp.int32, (breadth, picks.shape[1]), 0)
    dropped = jnp.logical_or(
        jnp.logical_and(at_left, cell < 2), jnp.logical_and(at_right, cell >= width + 2)
    )
    for q in range(tile_rows + 4):
        rows = pl.ds(q * breadth, breadth)
        kept = jnp.where(dropped, 0.0, picks[rows].astype(jnp.float32))
        kept_picks[rows] = kept.astype(jnp.bfloat16)
    for face in range(face_count):
        stack[face, pl.ds(0, beside)] = field[face].reshape(beside, channels)
        stack[face, pl.ds(beside, 4 * tile_rows)] = sides[face]
    for near, place, at_edge in ((up, above, at_top), (down, below, at_bottom)):

        @pl.when(jnp.logical_not(at_edge))
        def _():
            for face in range(face_count):
                stack[face, pl.ds(place, near.shape[1])] = near[face]

    write_padded(kept_picks, stack, padded)

    @pl.when(jnp.logical_or(at_left, at_right))
    def _():
        col_terms[...] = jnp.zeros_like(col_terms)
        table = col_picks[jnp.where(at_left, 0, 1)]
        for face in range(face_count):
            base = (face * 4 + jnp.where(at_left, 2, 3)) * 3
            turned = adjacency[base + 2]
            value = jnp.dot(table, stack[face], preferred_element_type=jnp.float32)
            rows = pl.ds(face * slot, half)
            for shift in range(3):
                part = value[shift * half : (shift + 1) * half].astype(jnp.bfloat16)
                tap = jnp.where(turned == 1, 2 - shift, shift)
                col_terms[adjacency[base + 1] - 2, tap, rows] = part

        total = jnp.zeros(col_sum.shape, jnp.float32)
        for side in range(2):
            for tap in range(3):
                total += jnp.dot(
                    col_terms[side, tap],
                    rotated[tap, 2 - 2 * side],
                    preferred_element_type=jnp.float32,
                )
        col_sum[...] = total

    for edge_col, at_edge in ((0, at_left), (width - 2, at_right)):

        @pl.when(at_edge)
        def _():
            cells = pl.ds(edge_col, 2)
            for face in range(face_count):
                value = col_sum[pl.ds(face * slot, half)]
                for y in range(tile_rows):
                    extra[face, y, cells] = value[2 * y : 2 * y + 2]


def seam_kernel(
    adjacency, row_picks, rotated, partial, up, down, edge, far_same, far_cross, out, values
):
    face_count, tile_rows, width, channels = partial.shape
    row_place = lax.axis_index("frow")
    out[...] = partial[...].astype(jnp.bfloat16)
    readers = joint_readers(up, down, edge, far_same, far_cross)
    for side in range(2):

        @pl.when(row_place == side * (lax.axis_size("frow") - 1))
        def _():
            @pl.loop(0, face_count)
            def _(face):
                source, kind = seam_of(adjacency, face, side)
                for choice, read in enumerate(readers[side]):

                    @pl.when(kind == choice)
                    def _():
                        values[face] = pick(row_picks[choice], read(source))

            for face in range(face_count):
                row_tap = 2 - 2 * adjacency[(face * 4 + side) * 3 + 1]
                total = jnp.zeros((2 * width, channels), jnp.float32)
                for tap in range(3):
                    total += jnp.dot(
                        values[face, pl.ds(tap * 2 * width, 2 * width)],
                        rotated[row_tap, tap],
                        preferred_element_type=jnp.float32,
                    )
                for d in range(2):
                    y = side * (tile_rows - 2) + d
                    term = total[d * width : (d + 1) * width]
                    out[face, y] = (partial[face, y] + term).astype(jnp.bfloat16)


def return_field(field, adjacency, rotated):
    face_count, tile_rows, width, channels = field.shape
    _, sides, up, down, edge, row_same, row_cross = joint_strips(field, adjacency)
    padded = (face_count, tile_rows + 4, width + 4, channels)
    size = stack_places(tile_rows, width)[3]
    picks = pad_picks(tile_rows, width)
    cells = face_count * round_up(2 * tile_rows, 16)
    padded_grad, extra = pl.pallas_call(
        return_kernel,
        out_shape=(
            jax.ShapeDtypeStruct(padded, field.dtype),
            jax.ShapeDtypeStruct(field.shape, jnp.float32),
        ),
        in_specs=whole(7),
        out_specs=[pl.BlockSpec(memory_space=pltpu.VMEM)] * 2,
        scratch_shapes=[
            pltpu.VMEM((face_count, size, channels), field.dtype),
            pltpu.VMEM(picks.shape, field.dtype),
            pltpu.VMEM((2, 3, cells, channels), field.dtype),
            pltpu.VMEM((cells, channels), jnp.float32),
        ],
        compiler_params=pltpu.CompilerParams(vmem_limit_bytes=vmem_bytes),
        cost_estimate=pl.CostEstimate(flops=1000, bytes_accessed=8000000, transcendentals=0),
    )(adjacency, picks, seam_col_picks(tile_rows, width), rotated, field, sides, up, down)
    partial = conv(padded_grad, rotated) + extra
    return pl.pallas_call(
        seam_kernel,
        out_shape=jax.ShapeDtypeStruct(field.shape, field.dtype),
        in_specs=whole(8),
        out_specs=pl.BlockSpec(memory_space=pltpu.VMEM),
        scratch_shapes=[pltpu.VMEM((face_count, 6 * width, channels), field.dtype)],
        compiler_params=pltpu.CompilerParams(vmem_limit_bytes=vmem_bytes),
        cost_estimate=pl.CostEstimate(flops=1000, bytes_accessed=5000000, transcendentals=0),
    )(
        adjacency, seam_row_picks(width), rotated, partial, up, down, edge, row_same,
        row_cross,
    )


def conv(value, taps):
    return lax.conv_general_dilated(
        value,
        taps,
        (1, 1),
        "VALID",
        rhs_dilation=(DILATION_STEP, DILATION_STEP),
        dimension_numbers=("NHWC", "HWIO", "NHWC"),
        preferred_element_type=jnp.float32,
    )


def gelu_value(value):
    return 0.5 * value * (1.0 + jax.scipy.special.erf(value * half_root))


def gelu_slope(value):
    return (
        0.5 * (1.0 + jax.scipy.special.erf(value * half_root))
        + value * jnp.exp(-0.5 * value * value) * density_scale
    )


def reduce_stages():
    col_bits = lax.axis_size("fcol").bit_length() - 1
    all_bits = (lax.axis_size("frow") * lax.axis_size("fcol")).bit_length() - 1
    rest = [1 << bit for bit in range(all_bits) if bit != col_bits]
    stages = [(1 << col_bits,)]
    while rest:
        stages.append(tuple(rest[:2]))
        rest = rest[2:]
    return stages


def stage_offsets(stage):
    return (0, stage[0]) if len(stage) == 1 else (0, stage[0], stage[1], stage[0] ^ stage[1])


def stage_place(index, stage):
    place = (index >> (stage[0].bit_length() - 1)) & 1
    if len(stage) == 2:
        place = place + 2 * ((index >> (stage[1].bit_length() - 1)) & 1)
    return place


def fold_sum(terms):
    while len(terms) > 1:
        terms = [terms[i] + terms[i + 1] for i in range(0, len(terms), 2)]
    return terms[0]


def reduce_everywhere(matrix, vector):
    count = lax.axis_size("frow") * lax.axis_size("fcol")
    index = lax.axis_index("frow") * lax.axis_size("fcol") + lax.axis_index("fcol")
    width = matrix.shape[-1]
    pad = jnp.zeros((7, width), jnp.float32)
    vector = jnp.concatenate([vector[None], pad], 0)
    part = matrix.reshape(-1, width)
    stages = reduce_stages()
    for stage in stages:
        offsets = stage_offsets(stage)
        place = stage_place(index, stage)
        part = part.reshape(len(offsets), -1, width).astype(jnp.bfloat16)
        vector = lax.optimization_barrier(vector.astype(jnp.bfloat16))
        rows = part.shape[1]
        sums, vectors = [], []
        for order, offset in enumerate(offsets):
            piece = lax.dynamic_slice_in_dim(part, place ^ order, 1, 0)[0]
            if offset:
                packed = jnp.concatenate([piece, vector], 0)
                packed = lax.ppermute(packed, axes, [(i, i ^ offset) for i in range(count)])
                sums.append(packed[:rows].astype(jnp.float32))
                vectors.append(packed[rows:].astype(jnp.float32))
            else:
                sums.append(piece.astype(jnp.float32))
                vectors.append(vector.astype(jnp.float32))
        part = fold_sum(sums)
        vector = fold_sum(vectors)
    part = lax.optimization_barrier(part.astype(jnp.bfloat16))[None]
    for stage in stages[::-1]:
        offsets = stage_offsets(stage)
        place = stage_place(index, stage)
        pieces = [part] + [
            lax.ppermute(part, axes, [(i, i ^ offset) for i in range(count)])
            for offset in offsets[1:]
        ]
        stacked = jnp.stack(pieces, 0)
        part = jnp.concatenate(
            [
                lax.dynamic_index_in_dim(stacked, place ^ order, 0, False)
                for order in range(len(offsets))
            ],
            0,
        )
    return (part.reshape(matrix.shape).astype(jnp.float32), vector[0])


def local(face_input, kernel, convolution_bias, upstream, adjacency):
    face_count, tile_rows, tile_cols, channels = face_input.shape
    table = adjacency.reshape(-1)
    padded_input = pad_field(face_input, table)
    preactivation = conv(padded_input, kernel) + convolution_bias
    activation = gelu_value(preactivation).astype(jnp.bfloat16)
    pre_grad = (upstream.astype(jnp.float32) * gelu_slope(preactivation)).astype(jnp.bfloat16)
    tap_list = []
    for a in range(3):
        for b in range(3):
            row, col = a * DILATION_STEP, b * DILATION_STEP
            window = padded_input[:, row : row + tile_rows, col : col + tile_cols]
            tap_list.append(
                lax.dot_general(
                    window,
                    pre_grad,
                    (((0, 1, 2), (0, 1, 2)), ((), ())),
                    preferred_element_type=jnp.float32,
                )
            )
    kernel_local = jnp.stack(tap_list, 0).reshape(kernel.shape)
    bias_local = jnp.sum(pre_grad.astype(jnp.float32), axis=(0, 1, 2))
    kernel_total, bias_total = reduce_everywhere(kernel_local, bias_local)
    scale = 1.0 / math.sqrt(
        face_count * tile_rows * lax.axis_size("frow") * tile_cols * lax.axis_size("fcol")
    )
    kernel_grad = kernel_total * scale
    bias_grad = bias_total * scale
    rotated = jnp.transpose(jnp.flip(kernel, (0, 1)), (0, 1, 3, 2))
    input_gradient = return_field(pre_grad, table, rotated)
    return (activation, input_gradient, kernel_grad, bias_grad)


def solution(mesh):
    return jax.shard_map(
        local,
        mesh=mesh,
        in_specs=(P(None, "frow", "fcol", None), P(), P(), P(None, "frow", "fcol", None), P()),
        out_specs=(P(None, "frow", "fcol", None), P(None, "frow", "fcol", None), P(), P()),
        check_vma=False,
    )
```

```python
import functools
import math

import jax
import jax.numpy as jnp
import numpy as np
from jax import lax
from jax.experimental import pallas as pl
from jax.experimental.pallas import tpu as pltpu
from jax.sharding import PartitionSpec as P

DILATION_STEP = 2


half_root = 0.7071067811865476
density_scale = 0.3989422804014327
axes = ("frow", "fcol")
vmem_bytes = 12 * 1024 * 1024


def shifted_pairs(row_step, col_step):
    rows, cols = lax.axis_size("frow"), lax.axis_size("fcol")
    return [
        (r * cols + c, (r + row_step) % rows * cols + (c + col_step) % cols)
        for r in range(rows)
        for c in range(cols)
    ]


def mirror_pairs(edge_rows, flip_rows, flip_cols):
    rows, cols = lax.axis_size("frow"), lax.axis_size("fcol")
    pairs = []
    for r in range(rows):
        for c in range(cols):
            on_edge = r in (0, rows - 1) if edge_rows else c in (0, cols - 1)
            if on_edge:
                target_row = rows - 1 - r if flip_rows else r
                target_col = cols - 1 - c if flip_cols else c
                pairs.append((r * cols + c, target_row * cols + target_col))
    return pairs


def round_up(value, step):
    return -(-value // step) * step


def flip_table(width):
    size = 2 * width + 8
    table = np.zeros((4, size, size), np.float32)
    for kind in range(4):
        for d in range(2):
            source_d = 1 - d if kind % 2 else d
            for p in range(width):
                source_p = width - 1 - p if kind >= 2 else p
                table[kind, d * width + p, source_d * width + source_p] = 1
            for e in range(4):
                source_e = 3 - e if kind >= 2 else e
                table[kind, 2 * width + 4 * d + e, 2 * width + 4 * source_d + source_e] = 1
    return table


def row_flips(width):
    return jnp.asarray(flip_table(width), jnp.bfloat16)


def stack_places(tile_rows, width):
    strip = round_up(2 * width + 8, 16)
    beside = tile_rows * width
    above = beside + 4 * tile_rows
    below = above + strip
    return (beside, above, below, round_up(below + strip, 128))


def stack_row(tile_rows, width, q, w):
    beside, above, below, _ = stack_places(tile_rows, width)
    side_cell = w if w < 2 else w - width
    inner = 2 <= w < width + 2
    if 2 <= q < tile_rows + 2:
        y = q - 2
        if inner:
            return y * width + w - 2
        return beside + 2 * tile_rows * (side_cell // 2) + 2 * y + side_cell % 2
    base, d = (above, q) if q < 2 else (below, q - tile_rows - 2)
    return base + (d * width + w - 2 if inner else 2 * width + 4 * d + side_cell)


def pad_picks(tile_rows, width):
    breadth = round_up(width + 4, 8)
    size = stack_places(tile_rows, width)[3]
    table = np.zeros(((tile_rows + 4) * breadth, size), np.float32)
    for q in range(tile_rows + 4):
        for w in range(width + 4):
            table[q * breadth + w, stack_row(tile_rows, width, q, w)] = 1
    return jnp.asarray(table, jnp.bfloat16)


def pick(table, value):
    return jnp.dot(table, value, preferred_element_type=jnp.float32).astype(jnp.bfloat16)


def seam_of(adjacency, face, side):
    base = (face * 4 + side) * 3
    near = (adjacency[base + 1] == side).astype(jnp.int32)
    return adjacency[base], 2 * adjacency[base + 2] + near


def one_hot(source, size):
    columns = lax.broadcasted_iota(jnp.int32, (source.shape[0], size), 1)
    return jnp.where(source == columns, 1.0, 0.0).astype(jnp.bfloat16)


def col_flip(kind, tile_rows):
    size = 2 * tile_rows
    row = lax.broadcasted_iota(jnp.int32, (size, size), 0)
    if kind >= 2:
        row = 2 * (tile_rows - 1 - (row >> 1)) + (row & 1)
    return one_hot(row ^ 1 if kind % 2 else row, size)


def tail_pick(first, tile_rows):
    row = lax.broadcasted_iota(jnp.int32, (8, 4 * tile_rows), 0)
    place = 2 * tile_rows * ((row >> 1) & 1) + 2 * (first + (row >> 2)) + (row & 1)
    return one_hot(place, 4 * tile_rows)


def side_kernel(
    adjacency, edges, beside, far_same, far_cross, side_out, upper_out, lower_out, seam
):
    face_count, both_sides, channels = edges.shape
    tile_rows = both_sides // 4
    half = 2 * tile_rows
    row_place, col_place = lax.axis_index("frow"), lax.axis_index("fcol")
    at_top = row_place == 0
    at_bottom = row_place == lax.axis_size("frow") - 1
    at_left = col_place == 0
    at_right = col_place == lax.axis_size("fcol") - 1

    @pl.when(jnp.logical_or(at_left, at_right))
    def _():
        @pl.loop(0, face_count)
        def _(face):
            source, kind = seam_of(adjacency, face, jnp.where(at_left, 2, 3))

            @pl.when(kind == 0)
            def _():
                both = beside[source]
                seam[face] = jnp.where(at_left, both[half:], both[:half])

            @pl.when(kind == 1)
            def _():
                both = edges[source]
                own = jnp.where(at_left, both[:half], both[half:])
                seam[face] = pick(col_flip(1, tile_rows), own)

            @pl.when(kind == 2)
            def _():
                seam[face] = pick(col_flip(2, tile_rows), far_cross[source])

            @pl.when(kind == 3)
            def _():
                seam[face] = pick(col_flip(3, tile_rows), far_same[source])

    upper_pick = tail_pick(0, tile_rows)
    lower_pick = tail_pick(tile_rows - 2, tile_rows)
    for face in range(face_count):
        both = beside[face]
        left = jnp.where(at_left, seam[face], both[half:])
        right = jnp.where(at_right, seam[face], both[:half])
        sides = jnp.concatenate([left, right], 0)
        side_out[face] = sides
        blank = jnp.zeros_like(left)
        inner = jnp.concatenate(
            [jnp.where(at_left, blank, left), jnp.where(at_right, blank, right)], 0
        )
        upper_out[face] = pick(upper_pick, jnp.where(at_top, inner, sides))
        lower_out[face] = pick(lower_pick, jnp.where(at_bottom, inner, sides))


def col_kernel(
    adjacency, field, edges, beside, far_same, far_cross, side_out, top_out, bottom_out, edge_out,
    upper, lower, seam,
):
    face_count, tile_rows, width, channels = field.shape
    at_top = lax.axis_index("frow") == 0
    side_kernel(adjacency, edges, beside, far_same, far_cross, side_out, upper, lower, seam)
    for face in range(face_count):
        for d in range(2):
            rows = pl.ds(d * width, width)
            first, last = field[face, d], field[face, tile_rows - 2 + d]
            top_out[face, rows] = first
            bottom_out[face, rows] = last
            edge_out[face, rows] = jnp.where(at_top, first, last)
        rows = pl.ds(2 * width, 8)
        top_out[face, rows] = upper[face]
        bottom_out[face, rows] = lower[face]
        edge_out[face, rows] = jnp.where(at_top, upper[face], lower[face])


def joint_readers(up, down, edge, far_same, far_cross):
    def reader(ref):
        return lambda source: ref[source]

    return [[reader(ref) for ref in (near, edge, far_cross, far_same)] for near in (up, down)]


def load_stack(adjacency, face, field, sides, readers, flips, stack):
    tile_rows, width, channels = field.shape[1:]
    strip = 2 * width + 8
    beside, above, below, _ = stack_places(tile_rows, width)
    row_place = lax.axis_index("frow")
    stack[face, pl.ds(0, beside)] = field[face].reshape(beside, channels)
    stack[face, pl.ds(beside, 4 * tile_rows)] = sides[face]
    for side, place in ((0, above), (1, below)):
        at_edge = row_place == side * (lax.axis_size("frow") - 1)
        rows = pl.ds(place, strip)

        @pl.when(jnp.logical_not(at_edge))
        def _():
            stack[face, rows] = readers[side][0](face)

        source, kind = seam_of(adjacency, face, side)
        for choice, read in enumerate(readers[side]):

            @pl.when(jnp.logical_and(at_edge, kind == choice))
            def _():
                stack[face, rows] = pick(flips[choice], read(source))


def write_padded(picks, stack, padded):
    face_count, rows, breadth, channels = padded.shape
    step = picks.shape[0] // rows
    for face in range(face_count):
        out = pick(picks[...], stack[face])
        for q in range(rows):
            padded[face, q] = out[q * step : q * step + breadth]


def pad_kernel(adjacency, flips, picks, field, sides, *refs):
    padded, stack = refs[-2:]
    readers = joint_readers(*refs[:-2])
    stack[...] = jnp.zeros_like(stack)

    @pl.loop(0, field.shape[0])
    def _(face):
        load_stack(adjacency, face, field, sides, readers, flips, stack)

    write_padded(picks, stack, padded)


def whole(count):
    return [pl.BlockSpec(memory_space=pltpu.SMEM)] + [
        pl.BlockSpec(memory_space=pltpu.VMEM) for _ in range(count)
    ]


def exchange_cols(field):
    face_count, tile_rows, width, channels = field.shape
    left = field[:, :, :2].reshape(face_count, 2 * tile_rows, channels)
    right = field[:, :, width - 2 :].reshape(face_count, 2 * tile_rows, channels)
    edges = jnp.concatenate([left, right], 1)
    if lax.axis_size("fcol") == 2:
        beside = lax.ppermute(edges, axes, shifted_pairs(0, 1))
    else:
        beside = jnp.concatenate(
            [
                lax.ppermute(left, axes, shifted_pairs(0, -1)),
                lax.ppermute(right, axes, shifted_pairs(0, 1)),
            ],
            1,
        )
    edge = jnp.where(lax.axis_index("fcol") == 0, left, right)
    far_same = lax.ppermute(edge, axes, mirror_pairs(False, True, False))
    far_cross = lax.ppermute(edge, axes, mirror_pairs(False, True, True))
    return (edges, beside, far_same, far_cross)


def exchange_rows(top, bottom, edge):
    up = lax.ppermute(bottom, axes, shifted_pairs(1, 0))
    down = lax.ppermute(top, axes, shifted_pairs(-1, 0))
    row_same = lax.ppermute(edge, axes, mirror_pairs(True, False, True))
    row_cross = lax.ppermute(edge, axes, mirror_pairs(True, True, True))
    return (up, down, row_same, row_cross)


def side_call(body, field, inputs, outputs, scratch):
    face_count, tile_rows, _, channels = field.shape
    scratch = [*scratch, (face_count, 2 * tile_rows, channels)]
    return pl.pallas_call(
        body,
        out_shape=[jax.ShapeDtypeStruct(shape, field.dtype) for shape in outputs],
        in_specs=whole(len(inputs) - 1),
        out_specs=[pl.BlockSpec(memory_space=pltpu.VMEM) for _ in outputs],
        scratch_shapes=[pltpu.VMEM(shape, field.dtype) for shape in scratch],
        compiler_params=pltpu.CompilerParams(vmem_limit_bytes=vmem_bytes),
        cost_estimate=pl.CostEstimate(flops=1000, bytes_accessed=3000000, transcendentals=0),
    )(*inputs)


def side_strips(field, adjacency, cols):
    face_count, tile_rows, width, channels = field.shape
    strip = (face_count, 2 * width + 8, channels)
    tail = (face_count, 8, channels)
    return side_call(
        col_kernel,
        field,
        (adjacency, field, *cols),
        (cols[0].shape, strip, strip, strip),
        (tail, tail),
    )


def pad_field(field, adjacency):
    face_count, tile_rows, width, channels = field.shape
    sides, top, bottom, edge = side_strips(field, adjacency, exchange_cols(field))
    up, down, row_same, row_cross = exchange_rows(top, bottom, edge)
    strips = (field, sides, up, down, edge, row_same, row_cross)
    padded = (face_count, tile_rows + 4, width + 4, channels)
    size = stack_places(tile_rows, width)[3]
    return pl.pallas_call(
        pad_kernel,
        out_shape=jax.ShapeDtypeStruct(padded, field.dtype),
        in_specs=whole(len(strips) + 2),
        out_specs=pl.BlockSpec(memory_space=pltpu.VMEM),
        scratch_shapes=[pltpu.VMEM((face_count, size, channels), field.dtype)],
        compiler_params=pltpu.CompilerParams(vmem_limit_bytes=vmem_bytes),
        cost_estimate=pl.CostEstimate(flops=1000, bytes_accessed=5000000, transcendentals=0),
    )(adjacency, row_flips(width), pad_picks(tile_rows, width), *strips)


def seam_row_picks(width):
    flips = flip_table(width)
    table = np.zeros((3 * 2 * width, 2 * width + 8), np.float32)
    for shift in range(3):
        for d in range(2):
            for x in range(width):
                w = x + 2 * shift
                if 2 <= w < width + 2:
                    source = d * width + w - 2
                else:
                    source = 2 * width + 4 * d + (w if w < 2 else w - width)
                table[(shift * 2 + d) * width + x, source] = 1
    turned = table.reshape(3, 2 * width, -1)[::-1].reshape(table.shape)
    parts = [(turned if kind >= 2 else table) @ flips[kind] for kind in range(4)]
    return jnp.asarray(np.stack(parts), jnp.bfloat16)


def seam_col_picks(tile_rows, width):
    size = stack_places(tile_rows, width)[3]
    table = np.zeros((2, 3 * 2 * tile_rows, size), np.float32)
    for right in range(2):
        for shift in range(3):
            for y in range(tile_rows):
                for k in range(2):
                    w = width + 2 + k if right else k
                    table[
                        right,
                        (shift * tile_rows + y) * 2 + k,
                        stack_row(tile_rows, width, y + 2 * shift, w),
                    ] = 1
    return jnp.asarray(table, jnp.bfloat16)


def return_kernel(
    adjacency, picks, col_picks, rotated, field, sides, up, down, padded, extra, stack,
    kept_picks, col_terms, col_sum,
):
    face_count, tile_rows, width, channels = field.shape
    breadth = picks.shape[0] // (tile_rows + 4)
    half = 2 * tile_rows
    slot = round_up(half, 16)
    beside, above, below, _ = stack_places(tile_rows, width)
    row_place, col_place = lax.axis_index("frow"), lax.axis_index("fcol")
    at_top = row_place == 0
    at_bottom = row_place == lax.axis_size("frow") - 1
    at_left = col_place == 0
    at_right = col_place == lax.axis_size("fcol") - 1
    stack[...] = jnp.zeros_like(stack)
    extra[...] = jnp.zeros_like(extra)
    cell = lax.broadcasted_iota(jnp.int32, (breadth, picks.shape[1]), 0)
    dropped = jnp.logical_or(
        jnp.logical_and(at_left, cell < 2), jnp.logical_and(at_right, cell >= width + 2)
    )
    for q in range(tile_rows + 4):
        rows = pl.ds(q * breadth, breadth)
        kept = jnp.where(dropped, 0.0, picks[rows].astype(jnp.float32))
        kept_picks[rows] = kept.astype(jnp.bfloat16)
    for face in range(face_count):
        stack[face, pl.ds(0, beside)] = field[face].reshape(beside, channels)
        stack[face, pl.ds(beside, 4 * tile_rows)] = sides[face]
    for near, place, at_edge in ((up, above, at_top), (down, below, at_bottom)):

        @pl.when(jnp.logical_not(at_edge))
        def _():
            for face in range(face_count):
                stack[face, pl.ds(place, near.shape[1])] = near[face]

    write_padded(kept_picks, stack, padded)

    @pl.when(jnp.logical_or(at_left, at_right))
    def _():
        col_terms[...] = jnp.zeros_like(col_terms)
        table = col_picks[jnp.where(at_left, 0, 1)]
        for face in range(face_count):
            base = (face * 4 + jnp.where(at_left, 2, 3)) * 3
            turned = adjacency[base + 2]
            value = jnp.dot(table, stack[face], preferred_element_type=jnp.float32)
            rows = pl.ds(face * slot, half)
            for shift in range(3):
                part = value[shift * half : (shift + 1) * half].astype(jnp.bfloat16)
                tap = jnp.where(turned == 1, 2 - shift, shift)
                col_terms[adjacency[base + 1] - 2, tap, rows] = part

        total = jnp.zeros(col_sum.shape, jnp.float32)
        for side in range(2):
            for tap in range(3):
                total += jnp.dot(
                    col_terms[side, tap],
                    rotated[tap, 2 - 2 * side],
                    preferred_element_type=jnp.float32,
                )
        col_sum[...] = total

    for edge_col, at_edge in ((0, at_left), (width - 2, at_right)):

        @pl.when(at_edge)
        def _():
            cells = pl.ds(edge_col, 2)
            for face in range(face_count):
                value = col_sum[pl.ds(face * slot, half)]
                for y in range(tile_rows):
                    extra[face, y, cells] = value[2 * y : 2 * y + 2]


def seam_kernel(
    adjacency, row_picks, rotated, partial, up, down, edge, far_same, far_cross, out, values
):
    face_count, tile_rows, width, channels = partial.shape
    row_place = lax.axis_index("frow")
    out[...] = partial[...].astype(jnp.bfloat16)
    readers = joint_readers(up, down, edge, far_same, far_cross)
    for side in range(2):

        @pl.when(row_place == side * (lax.axis_size("frow") - 1))
        def _():
            @pl.loop(0, face_count)
            def _(face):
                source, kind = seam_of(adjacency, face, side)
                for choice, read in enumerate(readers[side]):

                    @pl.when(kind == choice)
                    def _():
                        values[face] = pick(row_picks[choice], read(source))

            for face in range(face_count):
                row_tap = 2 - 2 * adjacency[(face * 4 + side) * 3 + 1]
                total = jnp.zeros((2 * width, channels), jnp.float32)
                for tap in range(3):
                    total += jnp.dot(
                        values[face, pl.ds(tap * 2 * width, 2 * width)],
                        rotated[row_tap, tap],
                        preferred_element_type=jnp.float32,
                    )
                for d in range(2):
                    y = side * (tile_rows - 2) + d
                    term = total[d * width : (d + 1) * width]
                    out[face, y] = (partial[face, y] + term).astype(jnp.bfloat16)


def return_field(field, adjacency, rotated, sides, up, down, edge, row_same, row_cross):
    face_count, tile_rows, width, channels = field.shape
    padded = (face_count, tile_rows + 4, width + 4, channels)
    size = stack_places(tile_rows, width)[3]
    picks = pad_picks(tile_rows, width)
    cells = face_count * round_up(2 * tile_rows, 16)
    padded_grad, extra = pl.pallas_call(
        return_kernel,
        out_shape=(
            jax.ShapeDtypeStruct(padded, field.dtype),
            jax.ShapeDtypeStruct(field.shape, jnp.float32),
        ),
        in_specs=whole(7),
        out_specs=[pl.BlockSpec(memory_space=pltpu.VMEM)] * 2,
        scratch_shapes=[
            pltpu.VMEM((face_count, size, channels), field.dtype),
            pltpu.VMEM(picks.shape, field.dtype),
            pltpu.VMEM((2, 3, cells, channels), field.dtype),
            pltpu.VMEM((cells, channels), jnp.float32),
        ],
        compiler_params=pltpu.CompilerParams(vmem_limit_bytes=vmem_bytes),
        cost_estimate=pl.CostEstimate(flops=1000, bytes_accessed=8000000, transcendentals=0),
    )(adjacency, picks, seam_col_picks(tile_rows, width), rotated, field, sides, up, down)
    partial = conv(padded_grad, rotated) + extra
    return pl.pallas_call(
        seam_kernel,
        out_shape=jax.ShapeDtypeStruct(field.shape, field.dtype),
        in_specs=whole(8),
        out_specs=pl.BlockSpec(memory_space=pltpu.VMEM),
        scratch_shapes=[pltpu.VMEM((face_count, 6 * width, channels), field.dtype)],
        compiler_params=pltpu.CompilerParams(vmem_limit_bytes=vmem_bytes),
        cost_estimate=pl.CostEstimate(flops=1000, bytes_accessed=5000000, transcendentals=0),
    )(
        adjacency, seam_row_picks(width), rotated, partial, up, down, edge, row_same,
        row_cross,
    )


def conv(value, taps):
    return lax.conv_general_dilated(
        value,
        taps,
        (1, 1),
        "VALID",
        rhs_dilation=(DILATION_STEP, DILATION_STEP),
        dimension_numbers=("NHWC", "HWIO", "NHWC"),
        preferred_element_type=jnp.float32,
    )


def gelu_value(value):
    return 0.5 * value * (1.0 + jax.scipy.special.erf(value * half_root))


def gelu_slope(value):
    return (
        0.5 * (1.0 + jax.scipy.special.erf(value * half_root))
        + value * jnp.exp(-0.5 * value * value) * density_scale
    )


def reduce_stages():
    col_bits = lax.axis_size("fcol").bit_length() - 1
    all_bits = (lax.axis_size("frow") * lax.axis_size("fcol")).bit_length() - 1
    rest = [1 << bit for bit in range(all_bits) if bit != col_bits]
    stages = [(1 << col_bits,)]
    while rest:
        stages.append(tuple(rest[:2]))
        rest = rest[2:]
    return stages


def stage_offsets(stage):
    return (0, stage[0]) if len(stage) == 1 else (0, stage[0], stage[1], stage[0] ^ stage[1])


def stage_place(index, stage):
    place = (index >> (stage[0].bit_length() - 1)) & 1
    if len(stage) == 2:
        place = place + 2 * ((index >> (stage[1].bit_length() - 1)) & 1)
    return place


def fold_sum(terms):
    while len(terms) > 1:
        terms = [terms[i] + terms[i + 1] for i in range(0, len(terms), 2)]
    return terms[0]


def reduce_everywhere(matrix, vector, field, adjacency, cols):
    count = lax.axis_size("frow") * lax.axis_size("fcol")
    index = lax.axis_index("frow") * lax.axis_size("fcol") + lax.axis_index("fcol")
    width = matrix.shape[-1]
    pad = jnp.zeros((7, width), jnp.float32)
    vector = jnp.concatenate([vector[None], pad], 0)
    part = matrix.reshape(-1, width)
    stages = reduce_stages()
    for order, stage in enumerate(stages):
        part, vector = part.astype(jnp.bfloat16), vector.astype(jnp.bfloat16)
        if order == 0:
            part, vector, *cols = lax.optimization_barrier((part, vector, *cols))
            strips = side_strips(field, adjacency, cols)
        if order == 1:
            part, vector, *strips = lax.optimization_barrier((part, vector, *strips))
            sides, top, bottom, edge = strips
            up, down, row_same, row_cross = exchange_rows(top, bottom, edge)
        if order == 2:
            part, vector, up, down = lax.optimization_barrier((part, vector, up, down))
        offsets = stage_offsets(stage)
        place = stage_place(index, stage)
        part = part.reshape(len(offsets), -1, width).astype(jnp.bfloat16)
        vector = lax.optimization_barrier(vector.astype(jnp.bfloat16))
        rows = part.shape[1]
        sums, vectors = [], []
        for turn, offset in enumerate(offsets):
            piece = lax.dynamic_slice_in_dim(part, place ^ turn, 1, 0)[0]
            if offset:
                packed = jnp.concatenate([piece, vector], 0)
                packed = lax.ppermute(packed, axes, [(i, i ^ offset) for i in range(count)])
                sums.append(packed[:rows].astype(jnp.float32))
                vectors.append(packed[rows:].astype(jnp.float32))
            else:
                sums.append(piece.astype(jnp.float32))
                vectors.append(vector.astype(jnp.float32))
        part = fold_sum(sums)
        vector = fold_sum(vectors)
    part = lax.optimization_barrier(part.astype(jnp.bfloat16))[None]
    for order, stage in enumerate(stages[::-1]):
        if order == len(stages) - 2:
            part, row_same, row_cross = lax.optimization_barrier((part, row_same, row_cross))
        offsets = stage_offsets(stage)
        place = stage_place(index, stage)
        pieces = [part] + [
            lax.ppermute(part, axes, [(i, i ^ offset) for i in range(count)])
            for offset in offsets[1:]
        ]
        stacked = jnp.stack(pieces, 0)
        part = jnp.concatenate(
            [
                lax.dynamic_index_in_dim(stacked, place ^ order, 0, False)
                for order in range(len(offsets))
            ],
            0,
        )
    rows = (sides, up, down, edge, row_same, row_cross)
    return (part.reshape(matrix.shape).astype(jnp.float32), vector[0], rows)


def local(face_input, kernel, convolution_bias, upstream, adjacency):
    face_count, tile_rows, tile_cols, channels = face_input.shape
    table = adjacency.reshape(-1)
    padded_input = pad_field(face_input, table)
    preactivation = conv(padded_input, kernel) + convolution_bias
    activation = gelu_value(preactivation).astype(jnp.bfloat16)
    pre_grad = (upstream.astype(jnp.float32) * gelu_slope(preactivation)).astype(jnp.bfloat16)
    tap_list = []
    for a in range(3):
        for b in range(3):
            row, col = a * DILATION_STEP, b * DILATION_STEP
            window = padded_input[:, row : row + tile_rows, col : col + tile_cols]
            tap_list.append(
                lax.dot_general(
                    window,
                    pre_grad,
                    (((0, 1, 2), (0, 1, 2)), ((), ())),
                    preferred_element_type=jnp.float32,
                )
            )
    kernel_local = jnp.stack(tap_list, 0).reshape(kernel.shape)
    bias_local = jnp.sum(pre_grad.astype(jnp.float32), axis=(0, 1, 2))
    kernel_total, bias_total, rows = reduce_everywhere(
        kernel_local, bias_local, pre_grad, table, exchange_cols(pre_grad)
    )
    scale = 1.0 / math.sqrt(
        face_count * tile_rows * lax.axis_size("frow") * tile_cols * lax.axis_size("fcol")
    )
    kernel_grad = kernel_total * scale
    bias_grad = bias_total * scale
    rotated = jnp.transpose(jnp.flip(kernel, (0, 1)), (0, 1, 3, 2))
    input_gradient = return_field(pre_grad, table, rotated, *rows)
    return (activation, input_gradient, kernel_grad, bias_grad)


def solution(mesh):
    return jax.shard_map(
        local,
        mesh=mesh,
        in_specs=(P(None, "frow", "fcol", None), P(), P(), P(None, "frow", "fcol", None), P()),
        out_specs=(P(None, "frow", "fcol", None), P(None, "frow", "fcol", None), P(), P()),
        check_vma=False,
    )
```

```python
import functools
import math

import jax
import jax.numpy as jnp
import numpy as np
from jax import lax
from jax.experimental import pallas as pl
from jax.experimental.pallas import tpu as pltpu
from jax.sharding import PartitionSpec as P

DILATION_STEP = 2


half_root = 0.7071067811865476
density_scale = 0.3989422804014327
axes = ("frow", "fcol")
vmem_bytes = 12 * 1024 * 1024


def shifted_pairs(row_step, col_step):
    rows, cols = lax.axis_size("frow"), lax.axis_size("fcol")
    return [
        (r * cols + c, (r + row_step) % rows * cols + (c + col_step) % cols)
        for r in range(rows)
        for c in range(cols)
    ]


def mirror_pairs(edge_rows, flip_rows, flip_cols):
    rows, cols = lax.axis_size("frow"), lax.axis_size("fcol")
    pairs = []
    for r in range(rows):
        for c in range(cols):
            on_edge = r in (0, rows - 1) if edge_rows else c in (0, cols - 1)
            if on_edge:
                target_row = rows - 1 - r if flip_rows else r
                target_col = cols - 1 - c if flip_cols else c
                pairs.append((r * cols + c, target_row * cols + target_col))
    return pairs


def round_up(value, step):
    return -(-value // step) * step


def flip_table(width):
    size = 2 * width + 8
    table = np.zeros((4, size, size), np.float32)
    for kind in range(4):
        for d in range(2):
            source_d = 1 - d if kind % 2 else d
            for p in range(width):
                source_p = width - 1 - p if kind >= 2 else p
                table[kind, d * width + p, source_d * width + source_p] = 1
            for e in range(4):
                source_e = 3 - e if kind >= 2 else e
                table[kind, 2 * width + 4 * d + e, 2 * width + 4 * source_d + source_e] = 1
    return table


def row_flips(width):
    return jnp.asarray(flip_table(width), jnp.bfloat16)


def stack_places(tile_rows, width):
    strip = round_up(2 * width + 8, 16)
    beside = tile_rows * width
    above = beside + 4 * tile_rows
    below = above + strip
    return (beside, above, below, round_up(below + strip, 128))


def stack_row(tile_rows, width, q, w):
    beside, above, below, _ = stack_places(tile_rows, width)
    side_cell = w if w < 2 else w - width
    inner = 2 <= w < width + 2
    if 2 <= q < tile_rows + 2:
        y = q - 2
        if inner:
            return y * width + w - 2
        return beside + 2 * tile_rows * (side_cell // 2) + 2 * y + side_cell % 2
    base, d = (above, q) if q < 2 else (below, q - tile_rows - 2)
    return base + (d * width + w - 2 if inner else 2 * width + 4 * d + side_cell)


def pad_picks(tile_rows, width):
    breadth = round_up(width + 4, 8)
    size = stack_places(tile_rows, width)[3]
    table = np.zeros(((tile_rows + 4) * breadth, size), np.float32)
    for q in range(tile_rows + 4):
        for w in range(width + 4):
            table[q * breadth + w, stack_row(tile_rows, width, q, w)] = 1
    return jnp.asarray(table, jnp.bfloat16)


def pick(table, value):
    return jnp.dot(table, value, preferred_element_type=jnp.float32).astype(jnp.bfloat16)


def seam_of(adjacency, face, side):
    base = (face * 4 + side) * 3
    near = (adjacency[base + 1] == side).astype(jnp.int32)
    return adjacency[base], 2 * adjacency[base + 2] + near


def one_hot(source, size):
    columns = lax.broadcasted_iota(jnp.int32, (source.shape[0], size), 1)
    return jnp.where(source == columns, 1.0, 0.0).astype(jnp.bfloat16)


def col_flip(kind, tile_rows):
    size = 2 * tile_rows
    row = lax.broadcasted_iota(jnp.int32, (size, size), 0)
    if kind >= 2:
        row = 2 * (tile_rows - 1 - (row >> 1)) + (row & 1)
    return one_hot(row ^ 1 if kind % 2 else row, size)


def tail_pick(first, tile_rows):
    row = lax.broadcasted_iota(jnp.int32, (8, 4 * tile_rows), 0)
    place = 2 * tile_rows * ((row >> 1) & 1) + 2 * (first + (row >> 2)) + (row & 1)
    return one_hot(place, 4 * tile_rows)


def side_kernel(
    adjacency, edges, beside, far_same, far_cross, side_out, upper_out, lower_out, seam
):
    face_count, both_sides, channels = edges.shape
    tile_rows = both_sides // 4
    half = 2 * tile_rows
    row_place, col_place = lax.axis_index("frow"), lax.axis_index("fcol")
    at_top = row_place == 0
    at_bottom = row_place == lax.axis_size("frow") - 1
    at_left = col_place == 0
    at_right = col_place == lax.axis_size("fcol") - 1

    @pl.when(jnp.logical_or(at_left, at_right))
    def _():
        @pl.loop(0, face_count)
        def _(face):
            source, kind = seam_of(adjacency, face, jnp.where(at_left, 2, 3))

            @pl.when(kind == 0)
            def _():
                both = beside[source]
                seam[face] = jnp.where(at_left, both[half:], both[:half])

            @pl.when(kind == 1)
            def _():
                both = edges[source]
                own = jnp.where(at_left, both[:half], both[half:])
                seam[face] = pick(col_flip(1, tile_rows), own)

            @pl.when(kind == 2)
            def _():
                seam[face] = pick(col_flip(2, tile_rows), far_cross[source])

            @pl.when(kind == 3)
            def _():
                seam[face] = pick(col_flip(3, tile_rows), far_same[source])

    upper_pick = tail_pick(0, tile_rows)
    lower_pick = tail_pick(tile_rows - 2, tile_rows)
    for face in range(face_count):
        both = beside[face]
        left = jnp.where(at_left, seam[face], both[half:])
        right = jnp.where(at_right, seam[face], both[:half])
        sides = jnp.concatenate([left, right], 0)
        side_out[face] = sides
        blank = jnp.zeros_like(left)
        inner = jnp.concatenate(
            [jnp.where(at_left, blank, left), jnp.where(at_right, blank, right)], 0
        )
        upper_out[face] = pick(upper_pick, jnp.where(at_top, inner, sides))
        lower_out[face] = pick(lower_pick, jnp.where(at_bottom, inner, sides))


def col_kernel(
    adjacency, field, edges, beside, far_same, far_cross, side_out, top_out, bottom_out, edge_out,
    upper, lower, seam,
):
    face_count, tile_rows, width, channels = field.shape
    at_top = lax.axis_index("frow") == 0
    side_kernel(adjacency, edges, beside, far_same, far_cross, side_out, upper, lower, seam)
    for face in range(face_count):
        for d in range(2):
            rows = pl.ds(d * width, width)
            first, last = field[face, d], field[face, tile_rows - 2 + d]
            top_out[face, rows] = first
            bottom_out[face, rows] = last
            edge_out[face, rows] = jnp.where(at_top, first, last)
        rows = pl.ds(2 * width, 8)
        top_out[face, rows] = upper[face]
        bottom_out[face, rows] = lower[face]
        edge_out[face, rows] = jnp.where(at_top, upper[face], lower[face])


def joint_readers(up, down, edge, far_same, far_cross):
    def reader(ref):
        return lambda source: ref[source]

    return [[reader(ref) for ref in (near, edge, far_cross, far_same)] for near in (up, down)]


def load_stack(adjacency, face, field, sides, readers, flips, stack):
    tile_rows, width, channels = field.shape[1:]
    strip = 2 * width + 8
    beside, above, below, _ = stack_places(tile_rows, width)
    row_place = lax.axis_index("frow")
    stack[face, pl.ds(0, beside)] = field[face].reshape(beside, channels)
    stack[face, pl.ds(beside, 4 * tile_rows)] = sides[face]
    for side, place in ((0, above), (1, below)):
        at_edge = row_place == side * (lax.axis_size("frow") - 1)
        rows = pl.ds(place, strip)

        @pl.when(jnp.logical_not(at_edge))
        def _():
            stack[face, rows] = readers[side][0](face)

        source, kind = seam_of(adjacency, face, side)
        for choice, read in enumerate(readers[side]):

            @pl.when(jnp.logical_and(at_edge, kind == choice))
            def _():
                stack[face, rows] = pick(flips[choice], read(source))


def write_padded(picks, stack, padded):
    face_count, rows, breadth, channels = padded.shape
    step = picks.shape[0] // rows
    for face in range(face_count):
        out = pick(picks[...], stack[face])
        for q in range(rows):
            padded[face, q] = out[q * step : q * step + breadth]


def copies(sources, targets, arrivals, first=0):
    return [
        pltpu.make_async_copy(source, target, arrivals.at[first + i])
        for i, (source, target) in enumerate(zip(sources, targets))
    ]


def run_all(moves, begin):
    for move in moves:
        if begin:
            move.start()
        else:
            move.wait()


def on_row_edge():
    row_place = lax.axis_index("frow")
    return jnp.logical_or(row_place == 0, row_place == lax.axis_size("frow") - 1)


def pad_kernel(adjacency, flips, picks, field, sides, *refs):
    sources, padded, stack = refs[:5], refs[5], refs[6]
    targets, arrivals = refs[7:12], refs[12]
    near = copies(sources[:2], targets[:2], arrivals)
    far = copies(sources[2:], targets[2:], arrivals, 2)
    run_all(near, True)

    @pl.when(on_row_edge())
    def _():
        run_all(far, True)

    stack[...] = jnp.zeros_like(stack)
    run_all(near, False)

    @pl.when(on_row_edge())
    def _():
        run_all(far, False)

    readers = joint_readers(*targets)

    @pl.loop(0, field.shape[0])
    def _(face):
        load_stack(adjacency, face, field, sides, readers, flips, stack)

    write_padded(picks, stack, padded)


def whole(count, left=0):
    specs = [pl.BlockSpec(memory_space=pltpu.SMEM)]
    specs += [pl.BlockSpec(memory_space=pltpu.VMEM) for _ in range(count)]
    return specs + [pl.BlockSpec(memory_space=pltpu.HBM) for _ in range(left)]


def exchange_cols(field):
    face_count, tile_rows, width, channels = field.shape
    left = field[:, :, :2].reshape(face_count, 2 * tile_rows, channels)
    right = field[:, :, width - 2 :].reshape(face_count, 2 * tile_rows, channels)
    edges = jnp.concatenate([left, right], 1)
    if lax.axis_size("fcol") == 2:
        beside = lax.ppermute(edges, axes, shifted_pairs(0, 1))
    else:
        beside = jnp.concatenate(
            [
                lax.ppermute(left, axes, shifted_pairs(0, -1)),
                lax.ppermute(right, axes, shifted_pairs(0, 1)),
            ],
            1,
        )
    edge = jnp.where(lax.axis_index("fcol") == 0, left, right)
    far_same = lax.ppermute(edge, axes, mirror_pairs(False, True, False))
    far_cross = lax.ppermute(edge, axes, mirror_pairs(False, True, True))
    return (edges, beside, far_same, far_cross)


def exchange_rows(top, bottom, edge):
    up = lax.ppermute(bottom, axes, shifted_pairs(1, 0))
    down = lax.ppermute(top, axes, shifted_pairs(-1, 0))
    row_same = lax.ppermute(edge, axes, mirror_pairs(True, False, True))
    row_cross = lax.ppermute(edge, axes, mirror_pairs(True, True, True))
    return (up, down, row_same, row_cross)


def side_call(body, field, inputs, outputs, scratch):
    face_count, tile_rows, _, channels = field.shape
    scratch = [*scratch, (face_count, 2 * tile_rows, channels)]
    return pl.pallas_call(
        body,
        out_shape=[jax.ShapeDtypeStruct(shape, field.dtype) for shape in outputs],
        in_specs=whole(len(inputs) - 1),
        out_specs=[pl.BlockSpec(memory_space=pltpu.VMEM) for _ in outputs],
        scratch_shapes=[pltpu.VMEM(shape, field.dtype) for shape in scratch],
        compiler_params=pltpu.CompilerParams(vmem_limit_bytes=vmem_bytes),
        cost_estimate=pl.CostEstimate(flops=1000, bytes_accessed=3000000, transcendentals=0),
    )(*inputs)


def side_strips(field, adjacency, cols):
    face_count, tile_rows, width, channels = field.shape
    strip = (face_count, 2 * width + 8, channels)
    tail = (face_count, 8, channels)
    return side_call(
        col_kernel,
        field,
        (adjacency, field, *cols),
        (cols[0].shape, strip, strip, strip),
        (tail, tail),
    )


def pad_field(field, adjacency):
    face_count, tile_rows, width, channels = field.shape
    sides, top, bottom, edge = side_strips(field, adjacency, exchange_cols(field))
    up, down, row_same, row_cross = exchange_rows(top, bottom, edge)
    strips = (field, sides, up, down, edge, row_same, row_cross)
    padded = (face_count, tile_rows + 4, width + 4, channels)
    size = stack_places(tile_rows, width)[3]
    return pl.pallas_call(
        pad_kernel,
        out_shape=jax.ShapeDtypeStruct(padded, field.dtype),
        in_specs=whole(4, 5),
        out_specs=pl.BlockSpec(memory_space=pltpu.VMEM),
        scratch_shapes=[
            pltpu.VMEM((face_count, size, channels), field.dtype),
            *[pltpu.VMEM(up.shape, field.dtype) for _ in range(5)],
            pltpu.SemaphoreType.DMA((5,)),
        ],
        compiler_params=pltpu.CompilerParams(vmem_limit_bytes=vmem_bytes),
        cost_estimate=pl.CostEstimate(flops=1000, bytes_accessed=5000000, transcendentals=0),
    )(adjacency, row_flips(width), pad_picks(tile_rows, width), *strips)


def seam_row_picks(width):
    flips = flip_table(width)
    table = np.zeros((3 * 2 * width, 2 * width + 8), np.float32)
    for shift in range(3):
        for d in range(2):
            for x in range(width):
                w = x + 2 * shift
                if 2 <= w < width + 2:
                    source = d * width + w - 2
                else:
                    source = 2 * width + 4 * d + (w if w < 2 else w - width)
                table[(shift * 2 + d) * width + x, source] = 1
    turned = table.reshape(3, 2 * width, -1)[::-1].reshape(table.shape)
    parts = [(turned if kind >= 2 else table) @ flips[kind] for kind in range(4)]
    return jnp.asarray(np.stack(parts), jnp.bfloat16)


def seam_col_picks(tile_rows, width):
    size = stack_places(tile_rows, width)[3]
    table = np.zeros((2, 3 * 2 * tile_rows, size), np.float32)
    for right in range(2):
        for shift in range(3):
            for y in range(tile_rows):
                for k in range(2):
                    w = width + 2 + k if right else k
                    table[
                        right,
                        (shift * tile_rows + y) * 2 + k,
                        stack_row(tile_rows, width, y + 2 * shift, w),
                    ] = 1
    return jnp.asarray(table, jnp.bfloat16)


def return_kernel(
    adjacency, picks, col_picks, rotated, field, sides, above_strip, below_strip, padded, extra,
    stack, kept_picks, col_terms, col_sum, up, down, arrivals,
):
    moves = copies((above_strip, below_strip), (up, down), arrivals)
    run_all(moves, True)
    face_count, tile_rows, width, channels = field.shape
    breadth = picks.shape[0] // (tile_rows + 4)
    half = 2 * tile_rows
    slot = round_up(half, 16)
    beside, above, below, _ = stack_places(tile_rows, width)
    row_place, col_place = lax.axis_index("frow"), lax.axis_index("fcol")
    at_top = row_place == 0
    at_bottom = row_place == lax.axis_size("frow") - 1
    at_left = col_place == 0
    at_right = col_place == lax.axis_size("fcol") - 1
    stack[...] = jnp.zeros_like(stack)
    extra[...] = jnp.zeros_like(extra)
    cell = lax.broadcasted_iota(jnp.int32, (breadth, picks.shape[1]), 0)
    dropped = jnp.logical_or(
        jnp.logical_and(at_left, cell < 2), jnp.logical_and(at_right, cell >= width + 2)
    )
    for q in range(tile_rows + 4):
        rows = pl.ds(q * breadth, breadth)
        kept = jnp.where(dropped, 0.0, picks[rows].astype(jnp.float32))
        kept_picks[rows] = kept.astype(jnp.bfloat16)
    for face in range(face_count):
        stack[face, pl.ds(0, beside)] = field[face].reshape(beside, channels)
        stack[face, pl.ds(beside, 4 * tile_rows)] = sides[face]
    run_all(moves, False)
    for near, place, at_edge in ((up, above, at_top), (down, below, at_bottom)):

        @pl.when(jnp.logical_not(at_edge))
        def _():
            for face in range(face_count):
                stack[face, pl.ds(place, near.shape[1])] = near[face]

    write_padded(kept_picks, stack, padded)

    @pl.when(jnp.logical_or(at_left, at_right))
    def _():
        col_terms[...] = jnp.zeros_like(col_terms)
        table = col_picks[jnp.where(at_left, 0, 1)]
        for face in range(face_count):
            base = (face * 4 + jnp.where(at_left, 2, 3)) * 3
            turned = adjacency[base + 2]
            value = jnp.dot(table, stack[face], preferred_element_type=jnp.float32)
            rows = pl.ds(face * slot, half)
            for shift in range(3):
                part = value[shift * half : (shift + 1) * half].astype(jnp.bfloat16)
                tap = jnp.where(turned == 1, 2 - shift, shift)
                col_terms[adjacency[base + 1] - 2, tap, rows] = part

        total = jnp.zeros(col_sum.shape, jnp.float32)
        for side in range(2):
            for tap in range(3):
                total += jnp.dot(
                    col_terms[side, tap],
                    rotated[tap, 2 - 2 * side],
                    preferred_element_type=jnp.float32,
                )
        col_sum[...] = total

    for edge_col, at_edge in ((0, at_left), (width - 2, at_right)):

        @pl.when(at_edge)
        def _():
            cells = pl.ds(edge_col, 2)
            for face in range(face_count):
                value = col_sum[pl.ds(face * slot, half)]
                for y in range(tile_rows):
                    extra[face, y, cells] = value[2 * y : 2 * y + 2]


def seam_kernel(
    adjacency, row_picks, rotated, partial, up, down, edge, far_same, far_cross, out, values,
    *refs,
):
    targets, arrivals = refs[:5], refs[5]
    moves = copies((up, down, edge, far_same, far_cross), targets, arrivals)

    @pl.when(on_row_edge())
    def _():
        run_all(moves, True)

    face_count, tile_rows, width, channels = partial.shape
    row_place = lax.axis_index("frow")
    out[...] = partial[...].astype(jnp.bfloat16)

    @pl.when(on_row_edge())
    def _():
        run_all(moves, False)

    readers = joint_readers(*targets)
    for side in range(2):

        @pl.when(row_place == side * (lax.axis_size("frow") - 1))
        def _():
            @pl.loop(0, face_count)
            def _(face):
                source, kind = seam_of(adjacency, face, side)
                for choice, read in enumerate(readers[side]):

                    @pl.when(kind == choice)
                    def _():
                        values[face] = pick(row_picks[choice], read(source))

            for face in range(face_count):
                row_tap = 2 - 2 * adjacency[(face * 4 + side) * 3 + 1]
                total = jnp.zeros((2 * width, channels), jnp.float32)
                for tap in range(3):
                    total += jnp.dot(
                        values[face, pl.ds(tap * 2 * width, 2 * width)],
                        rotated[row_tap, tap],
                        preferred_element_type=jnp.float32,
                    )
                for d in range(2):
                    y = side * (tile_rows - 2) + d
                    term = total[d * width : (d + 1) * width]
                    out[face, y] = (partial[face, y] + term).astype(jnp.bfloat16)


def return_field(field, adjacency, rotated, sides, up, down, edge, row_same, row_cross):
    face_count, tile_rows, width, channels = field.shape
    padded = (face_count, tile_rows + 4, width + 4, channels)
    size = stack_places(tile_rows, width)[3]
    picks = pad_picks(tile_rows, width)
    cells = face_count * round_up(2 * tile_rows, 16)
    padded_grad, extra = pl.pallas_call(
        return_kernel,
        out_shape=(
            jax.ShapeDtypeStruct(padded, field.dtype),
            jax.ShapeDtypeStruct(field.shape, jnp.float32),
        ),
        in_specs=whole(5, 2),
        out_specs=[pl.BlockSpec(memory_space=pltpu.VMEM)] * 2,
        scratch_shapes=[
            pltpu.VMEM((face_count, size, channels), field.dtype),
            pltpu.VMEM(picks.shape, field.dtype),
            pltpu.VMEM((2, 3, cells, channels), field.dtype),
            pltpu.VMEM((cells, channels), jnp.float32),
            pltpu.VMEM(up.shape, field.dtype),
            pltpu.VMEM(up.shape, field.dtype),
            pltpu.SemaphoreType.DMA((2,)),
        ],
        compiler_params=pltpu.CompilerParams(vmem_limit_bytes=vmem_bytes),
        cost_estimate=pl.CostEstimate(flops=1000, bytes_accessed=8000000, transcendentals=0),
    )(adjacency, picks, seam_col_picks(tile_rows, width), rotated, field, sides, up, down)
    partial = conv(padded_grad, rotated) + extra
    return pl.pallas_call(
        seam_kernel,
        out_shape=jax.ShapeDtypeStruct(field.shape, field.dtype),
        in_specs=whole(3, 5),
        out_specs=pl.BlockSpec(memory_space=pltpu.VMEM),
        scratch_shapes=[
            pltpu.VMEM((face_count, 6 * width, channels), field.dtype),
            *[pltpu.VMEM(up.shape, field.dtype) for _ in range(5)],
            pltpu.SemaphoreType.DMA((5,)),
        ],
        compiler_params=pltpu.CompilerParams(vmem_limit_bytes=vmem_bytes),
        cost_estimate=pl.CostEstimate(flops=1000, bytes_accessed=5000000, transcendentals=0),
    )(
        adjacency, seam_row_picks(width), rotated, partial, up, down, edge, row_same,
        row_cross,
    )


def conv(value, taps):
    return lax.conv_general_dilated(
        value,
        taps,
        (1, 1),
        "VALID",
        rhs_dilation=(DILATION_STEP, DILATION_STEP),
        dimension_numbers=("NHWC", "HWIO", "NHWC"),
        preferred_element_type=jnp.float32,
    )


def gelu_value(value):
    return 0.5 * value * (1.0 + jax.scipy.special.erf(value * half_root))


def gelu_slope(value):
    return (
        0.5 * (1.0 + jax.scipy.special.erf(value * half_root))
        + value * jnp.exp(-0.5 * value * value) * density_scale
    )


def reduce_stages():
    col_bits = lax.axis_size("fcol").bit_length() - 1
    all_bits = (lax.axis_size("frow") * lax.axis_size("fcol")).bit_length() - 1
    rest = [1 << bit for bit in range(all_bits) if bit != col_bits]
    stages = [(1 << col_bits,)]
    while rest:
        stages.append(tuple(rest[:2]))
        rest = rest[2:]
    return stages


def stage_offsets(stage):
    return (0, stage[0]) if len(stage) == 1 else (0, stage[0], stage[1], stage[0] ^ stage[1])


def stage_place(index, stage):
    place = (index >> (stage[0].bit_length() - 1)) & 1
    if len(stage) == 2:
        place = place + 2 * ((index >> (stage[1].bit_length() - 1)) & 1)
    return place


def fold_sum(terms):
    while len(terms) > 1:
        terms = [terms[i] + terms[i + 1] for i in range(0, len(terms), 2)]
    return terms[0]


def reduce_everywhere(matrix, vector, field, adjacency, cols):
    count = lax.axis_size("frow") * lax.axis_size("fcol")
    index = lax.axis_index("frow") * lax.axis_size("fcol") + lax.axis_index("fcol")
    width = matrix.shape[-1]
    pad = jnp.zeros((7, width), jnp.float32)
    vector = jnp.concatenate([vector[None], pad], 0)
    part = matrix.reshape(-1, width)
    stages = reduce_stages()
    for order, stage in enumerate(stages):
        part, vector = part.astype(jnp.bfloat16), vector.astype(jnp.bfloat16)
        if order == 2:
            strips = side_strips(field, adjacency, cols)
            part, vector, *strips = lax.optimization_barrier((part, vector, *strips))
            sides, top, bottom, edge = strips
            up, down, row_same, row_cross = exchange_rows(top, bottom, edge)
        offsets = stage_offsets(stage)
        place = stage_place(index, stage)
        part = part.reshape(len(offsets), -1, width).astype(jnp.bfloat16)
        vector = lax.optimization_barrier(vector.astype(jnp.bfloat16))
        rows = part.shape[1]
        sums, vectors = [], []
        for turn, offset in enumerate(offsets):
            piece = lax.dynamic_slice_in_dim(part, place ^ turn, 1, 0)[0]
            if offset:
                packed = jnp.concatenate([piece, vector], 0)
                packed = lax.ppermute(packed, axes, [(i, i ^ offset) for i in range(count)])
                sums.append(packed[:rows].astype(jnp.float32))
                vectors.append(packed[rows:].astype(jnp.float32))
            else:
                sums.append(piece.astype(jnp.float32))
                vectors.append(vector.astype(jnp.float32))
        part = fold_sum(sums)
        vector = fold_sum(vectors)
    part = lax.optimization_barrier(part.astype(jnp.bfloat16))[None]
    for order, stage in enumerate(stages[::-1]):
        if order == len(stages) - 2:
            part, up, down = lax.optimization_barrier((part, up, down))
        offsets = stage_offsets(stage)
        place = stage_place(index, stage)
        pieces = [part] + [
            lax.ppermute(part, axes, [(i, i ^ offset) for i in range(count)])
            for offset in offsets[1:]
        ]
        stacked = jnp.stack(pieces, 0)
        part = jnp.concatenate(
            [
                lax.dynamic_index_in_dim(stacked, place ^ order, 0, False)
                for order in range(len(offsets))
            ],
            0,
        )
    rows = (sides, up, down, edge, row_same, row_cross)
    return (part.reshape(matrix.shape).astype(jnp.float32), vector[0], rows)


def local(face_input, kernel, convolution_bias, upstream, adjacency):
    face_count, tile_rows, tile_cols, channels = face_input.shape
    table = adjacency.reshape(-1)
    padded_input = pad_field(face_input, table)
    preactivation = conv(padded_input, kernel) + convolution_bias
    activation = gelu_value(preactivation).astype(jnp.bfloat16)
    pre_grad = (upstream.astype(jnp.float32) * gelu_slope(preactivation)).astype(jnp.bfloat16)
    tap_list = []
    for a in range(3):
        for b in range(3):
            row, col = a * DILATION_STEP, b * DILATION_STEP
            window = padded_input[:, row : row + tile_rows, col : col + tile_cols]
            tap_list.append(
                lax.dot_general(
                    window,
                    pre_grad,
                    (((0, 1, 2), (0, 1, 2)), ((), ())),
                    preferred_element_type=jnp.float32,
                )
            )
    kernel_local = jnp.stack(tap_list, 0).reshape(kernel.shape)
    bias_local = jnp.sum(pre_grad.astype(jnp.float32), axis=(0, 1, 2))
    kernel_total, bias_total, rows = reduce_everywhere(
        kernel_local, bias_local, pre_grad, table, exchange_cols(pre_grad)
    )
    scale = 1.0 / math.sqrt(
        face_count * tile_rows * lax.axis_size("frow") * tile_cols * lax.axis_size("fcol")
    )
    kernel_grad = kernel_total * scale
    bias_grad = bias_total * scale
    rotated = jnp.transpose(jnp.flip(kernel, (0, 1)), (0, 1, 3, 2))
    input_gradient = return_field(pre_grad, table, rotated, *rows)
    return (activation, input_gradient, kernel_grad, bias_grad)


def solution(mesh):
    return jax.shard_map(
        local,
        mesh=mesh,
        in_specs=(P(None, "frow", "fcol", None), P(), P(), P(None, "frow", "fcol", None), P()),
        out_specs=(P(None, "frow", "fcol", None), P(None, "frow", "fcol", None), P(), P()),
        check_vma=False,
    )
```

```python
import functools
import math

import jax
import jax.numpy as jnp
import numpy as np
from jax import lax
from jax.experimental import pallas as pl
from jax.experimental.pallas import tpu as pltpu
from jax.sharding import PartitionSpec as P

DILATION_STEP = 2


half_root = 0.7071067811865476
density_scale = 0.3989422804014327
axes = ("frow", "fcol")
vmem_bytes = 12 * 1024 * 1024


def shifted_pairs(row_step, col_step):
    rows, cols = lax.axis_size("frow"), lax.axis_size("fcol")
    return [
        (r * cols + c, (r + row_step) % rows * cols + (c + col_step) % cols)
        for r in range(rows)
        for c in range(cols)
    ]


def mirror_pairs(edge_rows, flip_rows, flip_cols):
    rows, cols = lax.axis_size("frow"), lax.axis_size("fcol")
    pairs = []
    for r in range(rows):
        for c in range(cols):
            on_edge = r in (0, rows - 1) if edge_rows else c in (0, cols - 1)
            if on_edge:
                target_row = rows - 1 - r if flip_rows else r
                target_col = cols - 1 - c if flip_cols else c
                pairs.append((r * cols + c, target_row * cols + target_col))
    return pairs


def round_up(value, step):
    return -(-value // step) * step


def flip_table(width):
    size = 2 * width + 8
    table = np.zeros((4, size, size), np.float32)
    for kind in range(4):
        for d in range(2):
            source_d = 1 - d if kind % 2 else d
            for p in range(width):
                source_p = width - 1 - p if kind >= 2 else p
                table[kind, d * width + p, source_d * width + source_p] = 1
            for e in range(4):
                source_e = 3 - e if kind >= 2 else e
                table[kind, 2 * width + 4 * d + e, 2 * width + 4 * source_d + source_e] = 1
    return table


def row_flips(width):
    return jnp.asarray(flip_table(width), jnp.bfloat16)


def stack_places(tile_rows, width):
    strip = round_up(2 * width + 8, 16)
    beside = tile_rows * width
    above = beside + 4 * tile_rows
    below = above + strip
    return (beside, above, below, round_up(below + strip, 128))


def stack_row(tile_rows, width, q, w):
    beside, above, below, _ = stack_places(tile_rows, width)
    side_cell = w if w < 2 else w - width
    inner = 2 <= w < width + 2
    if 2 <= q < tile_rows + 2:
        y = q - 2
        if inner:
            return y * width + w - 2
        return beside + 2 * tile_rows * (side_cell // 2) + 2 * y + side_cell % 2
    base, d = (above, q) if q < 2 else (below, q - tile_rows - 2)
    return base + (d * width + w - 2 if inner else 2 * width + 4 * d + side_cell)


def pad_picks(tile_rows, width):
    breadth = round_up(width + 4, 8)
    size = stack_places(tile_rows, width)[3]
    table = np.zeros(((tile_rows + 4) * breadth, size), np.float32)
    for q in range(tile_rows + 4):
        for w in range(width + 4):
            table[q * breadth + w, stack_row(tile_rows, width, q, w)] = 1
    return jnp.asarray(table, jnp.bfloat16)


def pick(table, value):
    return jnp.dot(table, value, preferred_element_type=jnp.float32).astype(jnp.bfloat16)


def seam_of(adjacency, face, side):
    base = (face * 4 + side) * 3
    near = (adjacency[base + 1] == side).astype(jnp.int32)
    return adjacency[base], 2 * adjacency[base + 2] + near


def one_hot(source, size):
    columns = lax.broadcasted_iota(jnp.int32, (source.shape[0], size), 1)
    return jnp.where(source == columns, 1.0, 0.0).astype(jnp.bfloat16)


def col_flip(kind, tile_rows):
    size = 2 * tile_rows
    row = lax.broadcasted_iota(jnp.int32, (size, size), 0)
    if kind >= 2:
        row = 2 * (tile_rows - 1 - (row >> 1)) + (row & 1)
    return one_hot(row ^ 1 if kind % 2 else row, size)


def tail_pick(first, tile_rows):
    row = lax.broadcasted_iota(jnp.int32, (8, 4 * tile_rows), 0)
    place = 2 * tile_rows * ((row >> 1) & 1) + 2 * (first + (row >> 2)) + (row & 1)
    return one_hot(place, 4 * tile_rows)


def side_kernel(
    adjacency, edges, beside, far, side_out, upper_out, lower_out, seam
):
    face_count, both_sides, channels = edges.shape
    tile_rows = both_sides // 4
    half = 2 * tile_rows
    row_place, col_place = lax.axis_index("frow"), lax.axis_index("fcol")
    at_top = row_place == 0
    at_bottom = row_place == lax.axis_size("frow") - 1
    at_left = col_place == 0
    at_right = col_place == lax.axis_size("fcol") - 1

    @pl.when(jnp.logical_or(at_left, at_right))
    def _():
        @pl.loop(0, face_count)
        def _(face):
            source, kind = seam_of(adjacency, face, jnp.where(at_left, 2, 3))

            @pl.when(kind == 0)
            def _():
                both = beside[source]
                seam[face] = jnp.where(at_left, both[half:], both[:half])

            @pl.when(kind == 1)
            def _():
                both = edges[source]
                own = jnp.where(at_left, both[:half], both[half:])
                seam[face] = pick(col_flip(1, tile_rows), own)

            @pl.when(kind == 2)
            def _():
                seam[face] = pick(col_flip(2, tile_rows), far[source][half:])

            @pl.when(kind == 3)
            def _():
                seam[face] = pick(col_flip(3, tile_rows), far[source][:half])

    upper_pick = tail_pick(0, tile_rows)
    lower_pick = tail_pick(tile_rows - 2, tile_rows)
    for face in range(face_count):
        both = beside[face]
        left = jnp.where(at_left, seam[face], both[half:])
        right = jnp.where(at_right, seam[face], both[:half])
        sides = jnp.concatenate([left, right], 0)
        side_out[face] = sides
        blank = jnp.zeros_like(left)
        inner = jnp.concatenate(
            [jnp.where(at_left, blank, left), jnp.where(at_right, blank, right)], 0
        )
        upper_out[face] = pick(upper_pick, jnp.where(at_top, inner, sides))
        lower_out[face] = pick(lower_pick, jnp.where(at_bottom, inner, sides))


def col_kernel(
    adjacency, edges, beside, far, source, side_out, top_out, bottom_out, edge_out, upper, lower,
    seam, field, arrivals,
):
    moves = copies([source], [field], arrivals)
    run_all(moves, True)
    face_count, tile_rows, width, channels = field.shape
    at_top = lax.axis_index("frow") == 0
    side_kernel(adjacency, edges, beside, far, side_out, upper, lower, seam)
    run_all(moves, False)
    for face in range(face_count):
        for d in range(2):
            rows = pl.ds(d * width, width)
            first, last = field[face, d], field[face, tile_rows - 2 + d]
            top_out[face, rows] = first
            bottom_out[face, rows] = last
            edge_out[face, rows] = jnp.where(at_top, first, last)
        rows = pl.ds(2 * width, 8)
        top_out[face, rows] = upper[face]
        bottom_out[face, rows] = lower[face]
        edge_out[face, rows] = jnp.where(at_top, upper[face], lower[face])


def joint_readers(up, down, edge, far_same, far_cross):
    def reader(ref):
        return lambda source: ref[source]

    return [[reader(ref) for ref in (near, edge, far_cross, far_same)] for near in (up, down)]


def load_stack(adjacency, face, field, sides, readers, flips, stack):
    tile_rows, width, channels = field.shape[1:]
    strip = 2 * width + 8
    beside, above, below, _ = stack_places(tile_rows, width)
    row_place = lax.axis_index("frow")
    stack[face, pl.ds(0, beside)] = field[face].reshape(beside, channels)
    stack[face, pl.ds(beside, 4 * tile_rows)] = sides[face]
    for side, place in ((0, above), (1, below)):
        at_edge = row_place == side * (lax.axis_size("frow") - 1)
        rows = pl.ds(place, strip)

        @pl.when(jnp.logical_not(at_edge))
        def _():
            stack[face, rows] = readers[side][0](face)

        source, kind = seam_of(adjacency, face, side)
        for choice, read in enumerate(readers[side]):

            @pl.when(jnp.logical_and(at_edge, kind == choice))
            def _():
                stack[face, rows] = pick(flips[choice], read(source))


def write_padded(picks, stack, padded):
    face_count, rows, breadth, channels = padded.shape
    step = picks.shape[0] // rows
    for face in range(face_count):
        out = pick(picks[...], stack[face])
        for q in range(rows):
            padded[face, q] = out[q * step : q * step + breadth]


def copies(sources, targets, arrivals, first=0):
    return [
        pltpu.make_async_copy(source, target, arrivals.at[first + i])
        for i, (source, target) in enumerate(zip(sources, targets))
    ]


def run_all(moves, begin):
    for move in moves:
        if begin:
            move.start()
        else:
            move.wait()


def on_row_edge():
    row_place = lax.axis_index("frow")
    return jnp.logical_or(row_place == 0, row_place == lax.axis_size("frow") - 1)


def pad_kernel(adjacency, flips, picks, field, sides, *refs):
    sources, padded, stack = refs[:5], refs[5], refs[6]
    targets, arrivals = refs[7:12], refs[12]
    near = copies(sources[:2], targets[:2], arrivals)
    far = copies(sources[2:], targets[2:], arrivals, 2)
    run_all(near, True)

    @pl.when(on_row_edge())
    def _():
        run_all(far, True)

    stack[...] = jnp.zeros_like(stack)
    run_all(near, False)

    @pl.when(on_row_edge())
    def _():
        run_all(far, False)

    readers = joint_readers(*targets)

    @pl.loop(0, field.shape[0])
    def _(face):
        load_stack(adjacency, face, field, sides, readers, flips, stack)

    write_padded(picks, stack, padded)


def whole(count, left=0):
    specs = [pl.BlockSpec(memory_space=pltpu.SMEM)]
    specs += [pl.BlockSpec(memory_space=pltpu.VMEM) for _ in range(count)]
    return specs + [pl.BlockSpec(memory_space=pltpu.HBM) for _ in range(left)]


def exchange_cols(field):
    face_count, tile_rows, width, channels = field.shape
    left = field[:, :, :2].reshape(face_count, 2 * tile_rows, channels)
    right = field[:, :, width - 2 :].reshape(face_count, 2 * tile_rows, channels)
    edges = jnp.concatenate([left, right], 1)
    if lax.axis_size("fcol") == 2:
        beside = lax.ppermute(edges, axes, shifted_pairs(0, 1))
    else:
        beside = jnp.concatenate(
            [
                lax.ppermute(left, axes, shifted_pairs(0, -1)),
                lax.ppermute(right, axes, shifted_pairs(0, 1)),
            ],
            1,
        )
    half = 2 * tile_rows
    packed = jnp.where(
        lax.axis_index("fcol") == 0,
        jnp.concatenate([left, beside[:, half:]], 1),
        jnp.concatenate([right, beside[:, :half]], 1),
    )
    far = lax.ppermute(packed, axes, mirror_pairs(False, True, False))
    return (edges, beside, far)


def exchange_rows(top, bottom, edge):
    up = lax.ppermute(bottom, axes, shifted_pairs(1, 0))
    down = lax.ppermute(top, axes, shifted_pairs(-1, 0))
    row_same = lax.ppermute(edge, axes, mirror_pairs(True, False, True))
    row_cross = lax.ppermute(edge, axes, mirror_pairs(True, True, True))
    return (up, down, row_same, row_cross)


def side_strips(field, adjacency, cols):
    face_count, tile_rows, width, channels = field.shape
    strip = (face_count, 2 * width + 8, channels)
    tail = pltpu.VMEM((face_count, 8, channels), field.dtype)
    return pl.pallas_call(
        col_kernel,
        out_shape=[
            jax.ShapeDtypeStruct(shape, field.dtype)
            for shape in (cols[0].shape, strip, strip, strip)
        ],
        in_specs=whole(3) + [pl.BlockSpec(memory_space=pl.ANY)],
        out_specs=[pl.BlockSpec(memory_space=pltpu.VMEM)] * 4,
        scratch_shapes=[
            tail,
            tail,
            pltpu.VMEM((face_count, 2 * tile_rows, channels), field.dtype),
            pltpu.VMEM(field.shape, field.dtype),
            pltpu.SemaphoreType.DMA((1,)),
        ],
        compiler_params=pltpu.CompilerParams(vmem_limit_bytes=vmem_bytes),
        cost_estimate=pl.CostEstimate(flops=1000, bytes_accessed=3000000, transcendentals=0),
    )(adjacency, *cols, field)


def pad_field(field, adjacency):
    face_count, tile_rows, width, channels = field.shape
    sides, top, bottom, edge = side_strips(field, adjacency, exchange_cols(field))
    up, down, row_same, row_cross = exchange_rows(top, bottom, edge)
    strips = (field, sides, up, down, edge, row_same, row_cross)
    padded = (face_count, tile_rows + 4, width + 4, channels)
    size = stack_places(tile_rows, width)[3]
    return pl.pallas_call(
        pad_kernel,
        out_shape=jax.ShapeDtypeStruct(padded, field.dtype),
        in_specs=whole(4, 5),
        out_specs=pl.BlockSpec(memory_space=pltpu.VMEM),
        scratch_shapes=[
            pltpu.VMEM((face_count, size, channels), field.dtype),
            *[pltpu.VMEM(up.shape, field.dtype) for _ in range(5)],
            pltpu.SemaphoreType.DMA((5,)),
        ],
        compiler_params=pltpu.CompilerParams(vmem_limit_bytes=vmem_bytes),
        cost_estimate=pl.CostEstimate(flops=1000, bytes_accessed=5000000, transcendentals=0),
    )(adjacency, row_flips(width), pad_picks(tile_rows, width), *strips)


def seam_row_picks(width):
    flips = flip_table(width)
    table = np.zeros((3 * 2 * width, 2 * width + 8), np.float32)
    for shift in range(3):
        for d in range(2):
            for x in range(width):
                w = x + 2 * shift
                if 2 <= w < width + 2:
                    source = d * width + w - 2
                else:
                    source = 2 * width + 4 * d + (w if w < 2 else w - width)
                table[(shift * 2 + d) * width + x, source] = 1
    turned = table.reshape(3, 2 * width, -1)[::-1].reshape(table.shape)
    parts = [(turned if kind >= 2 else table) @ flips[kind] for kind in range(4)]
    return jnp.asarray(np.stack(parts), jnp.bfloat16)


def seam_col_picks(tile_rows, width):
    size = stack_places(tile_rows, width)[3]
    table = np.zeros((2, 3 * 2 * tile_rows, size), np.float32)
    for right in range(2):
        for shift in range(3):
            for y in range(tile_rows):
                for k in range(2):
                    w = width + 2 + k if right else k
                    table[
                        right,
                        (shift * tile_rows + y) * 2 + k,
                        stack_row(tile_rows, width, y + 2 * shift, w),
                    ] = 1
    return jnp.asarray(table, jnp.bfloat16)


def return_kernel(
    adjacency, picks, col_picks, rotated, field, sides, above_strip, below_strip, padded, extra,
    stack, kept_picks, col_terms, col_sum, up, down, arrivals,
):
    moves = copies((above_strip, below_strip), (up, down), arrivals)
    run_all(moves, True)
    face_count, tile_rows, width, channels = field.shape
    breadth = picks.shape[0] // (tile_rows + 4)
    half = 2 * tile_rows
    slot = round_up(half, 16)
    beside, above, below, _ = stack_places(tile_rows, width)
    row_place, col_place = lax.axis_index("frow"), lax.axis_index("fcol")
    at_top = row_place == 0
    at_bottom = row_place == lax.axis_size("frow") - 1
    at_left = col_place == 0
    at_right = col_place == lax.axis_size("fcol") - 1
    stack[...] = jnp.zeros_like(stack)
    extra[...] = jnp.zeros_like(extra)
    cell = lax.broadcasted_iota(jnp.int32, (breadth, picks.shape[1]), 0)
    dropped = jnp.logical_or(
        jnp.logical_and(at_left, cell < 2), jnp.logical_and(at_right, cell >= width + 2)
    )
    for q in range(tile_rows + 4):
        rows = pl.ds(q * breadth, breadth)
        kept = jnp.where(dropped, 0.0, picks[rows].astype(jnp.float32))
        kept_picks[rows] = kept.astype(jnp.bfloat16)
    for face in range(face_count):
        stack[face, pl.ds(0, beside)] = field[face].reshape(beside, channels)
        stack[face, pl.ds(beside, 4 * tile_rows)] = sides[face]
    run_all(moves, False)
    for near, place, at_edge in ((up, above, at_top), (down, below, at_bottom)):

        @pl.when(jnp.logical_not(at_edge))
        def _():
            for face in range(face_count):
                stack[face, pl.ds(place, near.shape[1])] = near[face]

    write_padded(kept_picks, stack, padded)

    @pl.when(jnp.logical_or(at_left, at_right))
    def _():
        col_terms[...] = jnp.zeros_like(col_terms)
        table = col_picks[jnp.where(at_left, 0, 1)]
        for face in range(face_count):
            base = (face * 4 + jnp.where(at_left, 2, 3)) * 3
            turned = adjacency[base + 2]
            value = jnp.dot(table, stack[face], preferred_element_type=jnp.float32)
            rows = pl.ds(face * slot, half)
            for shift in range(3):
                part = value[shift * half : (shift + 1) * half].astype(jnp.bfloat16)
                tap = jnp.where(turned == 1, 2 - shift, shift)
                col_terms[adjacency[base + 1] - 2, tap, rows] = part

        total = jnp.zeros(col_sum.shape, jnp.float32)
        for side in range(2):
            for tap in range(3):
                total += jnp.dot(
                    col_terms[side, tap],
                    rotated[tap, 2 - 2 * side],
                    preferred_element_type=jnp.float32,
                )
        col_sum[...] = total

    for edge_col, at_edge in ((0, at_left), (width - 2, at_right)):

        @pl.when(at_edge)
        def _():
            cells = pl.ds(edge_col, 2)
            for face in range(face_count):
                value = col_sum[pl.ds(face * slot, half)]
                for y in range(tile_rows):
                    extra[face, y, cells] = value[2 * y : 2 * y + 2]


def seam_kernel(
    adjacency, row_picks, rotated, partial, up, down, edge, far_same, far_cross, out, values,
    *refs,
):
    targets, arrivals = refs[:5], refs[5]
    moves = copies((up, down, edge, far_same, far_cross), targets, arrivals)

    @pl.when(on_row_edge())
    def _():
        run_all(moves, True)

    face_count, tile_rows, width, channels = partial.shape
    row_place = lax.axis_index("frow")
    out[...] = partial[...].astype(jnp.bfloat16)

    @pl.when(on_row_edge())
    def _():
        run_all(moves, False)

    readers = joint_readers(*targets)
    for side in range(2):

        @pl.when(row_place == side * (lax.axis_size("frow") - 1))
        def _():
            @pl.loop(0, face_count)
            def _(face):
                source, kind = seam_of(adjacency, face, side)
                for choice, read in enumerate(readers[side]):

                    @pl.when(kind == choice)
                    def _():
                        values[face] = pick(row_picks[choice], read(source))

            for face in range(face_count):
                row_tap = 2 - 2 * adjacency[(face * 4 + side) * 3 + 1]
                total = jnp.zeros((2 * width, channels), jnp.float32)
                for tap in range(3):
                    total += jnp.dot(
                        values[face, pl.ds(tap * 2 * width, 2 * width)],
                        rotated[row_tap, tap],
                        preferred_element_type=jnp.float32,
                    )
                for d in range(2):
                    y = side * (tile_rows - 2) + d
                    term = total[d * width : (d + 1) * width]
                    out[face, y] = (partial[face, y] + term).astype(jnp.bfloat16)


def return_field(field, adjacency, rotated, sides, up, down, edge, row_same, row_cross):
    face_count, tile_rows, width, channels = field.shape
    padded = (face_count, tile_rows + 4, width + 4, channels)
    size = stack_places(tile_rows, width)[3]
    picks = pad_picks(tile_rows, width)
    cells = face_count * round_up(2 * tile_rows, 16)
    padded_grad, extra = pl.pallas_call(
        return_kernel,
        out_shape=(
            jax.ShapeDtypeStruct(padded, field.dtype),
            jax.ShapeDtypeStruct(field.shape, jnp.float32),
        ),
        in_specs=whole(5, 2),
        out_specs=[pl.BlockSpec(memory_space=pltpu.VMEM)] * 2,
        scratch_shapes=[
            pltpu.VMEM((face_count, size, channels), field.dtype),
            pltpu.VMEM(picks.shape, field.dtype),
            pltpu.VMEM((2, 3, cells, channels), field.dtype),
            pltpu.VMEM((cells, channels), jnp.float32),
            pltpu.VMEM(up.shape, field.dtype),
            pltpu.VMEM(up.shape, field.dtype),
            pltpu.SemaphoreType.DMA((2,)),
        ],
        compiler_params=pltpu.CompilerParams(vmem_limit_bytes=vmem_bytes),
        cost_estimate=pl.CostEstimate(flops=1000, bytes_accessed=8000000, transcendentals=0),
    )(adjacency, picks, seam_col_picks(tile_rows, width), rotated, field, sides, up, down)
    partial = conv(padded_grad, rotated) + extra
    return pl.pallas_call(
        seam_kernel,
        out_shape=jax.ShapeDtypeStruct(field.shape, field.dtype),
        in_specs=whole(3, 5),
        out_specs=pl.BlockSpec(memory_space=pltpu.VMEM),
        scratch_shapes=[
            pltpu.VMEM((face_count, 6 * width, channels), field.dtype),
            *[pltpu.VMEM(up.shape, field.dtype) for _ in range(5)],
            pltpu.SemaphoreType.DMA((5,)),
        ],
        compiler_params=pltpu.CompilerParams(vmem_limit_bytes=vmem_bytes),
        cost_estimate=pl.CostEstimate(flops=1000, bytes_accessed=5000000, transcendentals=0),
    )(
        adjacency, seam_row_picks(width), rotated, partial, up, down, edge, row_same,
        row_cross,
    )


def conv(value, taps):
    return lax.conv_general_dilated(
        value,
        taps,
        (1, 1),
        "VALID",
        rhs_dilation=(DILATION_STEP, DILATION_STEP),
        dimension_numbers=("NHWC", "HWIO", "NHWC"),
        preferred_element_type=jnp.float32,
    )


def gelu_value(value):
    return 0.5 * value * (1.0 + jax.scipy.special.erf(value * half_root))


def gelu_slope(value):
    return (
        0.5 * (1.0 + jax.scipy.special.erf(value * half_root))
        + value * jnp.exp(-0.5 * value * value) * density_scale
    )


def reduce_stages():
    col_bits = lax.axis_size("fcol").bit_length() - 1
    all_bits = (lax.axis_size("frow") * lax.axis_size("fcol")).bit_length() - 1
    rest = [1 << bit for bit in range(all_bits) if bit != col_bits]
    stages = [(1 << col_bits,)]
    while rest:
        stages.append(tuple(rest[:2]))
        rest = rest[2:]
    return stages


def stage_offsets(stage):
    return (0, stage[0]) if len(stage) == 1 else (0, stage[0], stage[1], stage[0] ^ stage[1])


def stage_place(index, stage):
    place = (index >> (stage[0].bit_length() - 1)) & 1
    if len(stage) == 2:
        place = place + 2 * ((index >> (stage[1].bit_length() - 1)) & 1)
    return place


def fold_sum(terms):
    while len(terms) > 1:
        terms = [terms[i] + terms[i + 1] for i in range(0, len(terms), 2)]
    return terms[0]


def reduce_everywhere(matrix, vector, field, adjacency, cols):
    count = lax.axis_size("frow") * lax.axis_size("fcol")
    index = lax.axis_index("frow") * lax.axis_size("fcol") + lax.axis_index("fcol")
    width = matrix.shape[-1]
    pad = jnp.zeros((7, width), jnp.float32)
    vector = jnp.concatenate([vector[None], pad], 0)
    part = matrix.reshape(-1, width)
    stages = reduce_stages()
    for order, stage in enumerate(stages):
        part, vector = part.astype(jnp.bfloat16), vector.astype(jnp.bfloat16)
        if order == 0:
            strips = side_strips(field, adjacency, cols)
        if order == 1:
            sides, top, bottom, edge = strips
            up, down, row_same, row_cross = exchange_rows(top, bottom, edge)
        offsets = stage_offsets(stage)
        place = stage_place(index, stage)
        part = part.reshape(len(offsets), -1, width).astype(jnp.bfloat16)
        vector = lax.optimization_barrier(vector.astype(jnp.bfloat16))
        rows = part.shape[1]
        sums, vectors = [], []
        for turn, offset in enumerate(offsets):
            piece = lax.dynamic_slice_in_dim(part, place ^ turn, 1, 0)[0]
            if offset:
                packed = jnp.concatenate([piece, vector], 0)
                packed = lax.ppermute(packed, axes, [(i, i ^ offset) for i in range(count)])
                sums.append(packed[:rows].astype(jnp.float32))
                vectors.append(packed[rows:].astype(jnp.float32))
            else:
                sums.append(piece.astype(jnp.float32))
                vectors.append(vector.astype(jnp.float32))
        part = fold_sum(sums)
        vector = fold_sum(vectors)
    part = lax.optimization_barrier(part.astype(jnp.bfloat16))[None]
    for order, stage in enumerate(stages[::-1]):
        if order == len(stages) - 2:
            pass
        offsets = stage_offsets(stage)
        place = stage_place(index, stage)
        pieces = [part] + [
            lax.ppermute(part, axes, [(i, i ^ offset) for i in range(count)])
            for offset in offsets[1:]
        ]
        stacked = jnp.stack(pieces, 0)
        part = jnp.concatenate(
            [
                lax.dynamic_index_in_dim(stacked, place ^ order, 0, False)
                for order in range(len(offsets))
            ],
            0,
        )
    rows = (sides, up, down, edge, row_same, row_cross)
    return (part.reshape(matrix.shape).astype(jnp.float32), vector[0], rows)


def local(face_input, kernel, convolution_bias, upstream, adjacency):
    face_count, tile_rows, tile_cols, channels = face_input.shape
    table = adjacency.reshape(-1)
    padded_input = pad_field(face_input, table)
    preactivation = conv(padded_input, kernel) + convolution_bias
    activation = gelu_value(preactivation).astype(jnp.bfloat16)
    pre_grad = (upstream.astype(jnp.float32) * gelu_slope(preactivation)).astype(jnp.bfloat16)
    activation, pre_grad = lax.optimization_barrier((activation, pre_grad))
    tap_list = []
    for a in range(3):
        for b in range(3):
            row, col = a * DILATION_STEP, b * DILATION_STEP
            window = padded_input[:, row : row + tile_rows, col : col + tile_cols]
            tap_list.append(
                lax.dot_general(
                    window,
                    pre_grad,
                    (((0, 1, 2), (0, 1, 2)), ((), ())),
                    preferred_element_type=jnp.float32,
                )
            )
    kernel_local = jnp.stack(tap_list, 0).reshape(kernel.shape)
    bias_local = jnp.sum(pre_grad.astype(jnp.float32), axis=(0, 1, 2))
    kernel_total, bias_total, rows = reduce_everywhere(
        kernel_local, bias_local, pre_grad, table, exchange_cols(pre_grad)
    )
    scale = 1.0 / math.sqrt(
        face_count * tile_rows * lax.axis_size("frow") * tile_cols * lax.axis_size("fcol")
    )
    kernel_grad = kernel_total * scale
    bias_grad = bias_total * scale
    rotated = jnp.transpose(jnp.flip(kernel, (0, 1)), (0, 1, 3, 2))
    input_gradient = return_field(pre_grad, table, rotated, *rows)
    return (activation, input_gradient, kernel_grad, bias_grad)


def solution(mesh):
    return jax.shard_map(
        local,
        mesh=mesh,
        in_specs=(P(None, "frow", "fcol", None), P(), P(), P(None, "frow", "fcol", None), P()),
        out_specs=(P(None, "frow", "fcol", None), P(None, "frow", "fcol", None), P(), P()),
        check_vma=False,
    )
```
